32 devices in a mesh: dp: 8 (over z, y), tensor: 4 (over x, core).
Axes of the slice: x: 2, y: 2, z: 4, core: 2. Of those that a mesh axis runs over, the one named last changes fastest.
Arguments:
- tokens: bfloat16 [12288, 768], P('dp'), may hold values from -6 to 6
- segment_ids: int32 [24, 512], P('dp'), may hold values from 0 to 16, as said below
- prev_scores: bfloat16 [24, 12, 512, 512], P('dp', 'tensor'), may hold values from -6 to 6
- out_grad: bfloat16 [12288, 768], P('dp'), may hold values from -6 to 6
- attn_in_master: float32 [3, 768, 768], P(None, 'dp', 'tensor'), may hold values from -0.21875 to 0.21875
- attn_out_master: float32 [768, 768], P('tensor', 'dp'), may hold values from -0.875 to 0.875
- ffn_in_master: float32 [768, 3072], P('dp', 'tensor'), may hold values from -0.21875 to 0.21875
- ffn_out_master: float32 [3072, 768], P('tensor', 'dp'), may hold values from -0.109375 to 0.109375
- attn_in_first: float32 [3, 768, 768], P(None, 'dp', 'tensor'), may hold values from -0.0024414062 to 0.0024414062
- attn_out_first: float32 [768, 768], P('tensor', 'dp'), may hold values from -0.0024414062 to 0.0024414062
- ffn_in_first: float32 [768, 3072], P('dp', 'tensor'), may hold values from -0.0024414062 to 0.0024414062
- ffn_out_first: float32 [3072, 768], P('tensor', 'dp'), may hold values from -0.0024414062 to 0.0024414062
- attn_in_second: float32 [3, 768, 768], P(None, 'dp', 'tensor'), may hold values from 1.4110135e-07 to 5.644054e-07
- attn_out_second: float32 [768, 768], P('tensor', 'dp'), may hold values from 1.4110135e-07 to 5.644054e-07
- ffn_in_second: float32 [768, 3072], P('dp', 'tensor'), may hold values from 1.4110135e-07 to 5.644054e-07
- ffn_out_second: float32 [3072, 768], P('tensor', 'dp'), may hold values from 1.4110135e-07 to 5.644054e-07
- qv_bias: float32 [2, 768], P(None, 'tensor'), may hold values from -1.75 to 1.75
- ffn_bias: float32 [3072], P('tensor'), may hold values from -1.75 to 1.75
- row_params: float32 [6, 768], replicated, may hold values from -0.75 to 1.65, as said below
- qv_bias_first: float32 [2, 768], P(None, 'tensor'), may hold values from -0.009765625 to 0.009765625
- ffn_bias_first: float32 [3072], P('tensor'), may hold values from -0.0024414062 to 0.0024414062
- row_params_first: float32 [6, 768], replicated, may hold values from -0.009765625 to 0.009765625
- qv_bias_second: float32 [2, 768], P(None, 'tensor'), may hold values from 2.2576216e-06 to 9.030487e-06
- ffn_bias_second: float32 [3072], P('tensor'), may hold values from 7.0550676e-08 to 2.822027e-07
- row_params_second: float32 [6, 768], replicated, may hold values from 2.2576216e-06 to 9.030487e-06
Outputs:
- out_tokens: bfloat16 [12288, 768], P('dp')
- tokens_grad: float32 [12288, 768], P('dp')
- scores_grad: float32 [24, 12, 512, 512], P('dp', 'tensor')
- grad_norm: float32 [], replicated
- attn_in_new: float32 [3, 768, 768], P(None, 'dp', 'tensor')
- attn_out_new: float32 [768, 768], P('tensor', 'dp')
- ffn_in_new: float32 [768, 3072], P('dp', 'tensor')
- ffn_out_new: float32 [3072, 768], P('tensor', 'dp')
- attn_in_first_new: float32 [3, 768, 768], P(None, 'dp', 'tensor')
- attn_out_first_new: float32 [768, 768], P('tensor', 'dp')
- ffn_in_first_new: float32 [768, 3072], P('dp', 'tensor')
- ffn_out_first_new: float32 [3072, 768], P('tensor', 'dp')
- attn_in_second_new: float32 [3, 768, 768], P(None, 'dp', 'tensor')
- attn_out_second_new: float32 [768, 768], P('tensor', 'dp')
- ffn_in_second_new: float32 [768, 3072], P('dp', 'tensor')
- ffn_out_second_new: float32 [3072, 768], P('tensor', 'dp')
- attn_in_copy: bfloat16 [3, 768, 768], P(None, 'dp', 'tensor')
- attn_out_copy: bfloat16 [768, 768], P('tensor', 'dp')
- ffn_in_copy: bfloat16 [768, 3072], P('dp', 'tensor')
- ffn_out_copy: bfloat16 [3072, 768], P('tensor', 'dp')
- qv_bias_new: float32 [2, 768], P(None, 'tensor')
- ffn_bias_new: float32 [3072], P('tensor')
- row_params_new: float32 [6, 768], replicated
- qv_bias_first_new: float32 [2, 768], P(None, 'tensor')
- ffn_bias_first_new: float32 [3072], P('tensor')
- row_params_first_new: float32 [6, 768], replicated
- qv_bias_second_new: float32 [2, 768], P(None, 'tensor')
- ffn_bias_second_new: float32 [3072], P('tensor')
- row_params_second_new: float32 [6, 768], replicated
The draws below stay inside these ranges and needn't reach their ends.
Inputs may be any that keep to these rules, and one draw needn't show every extreme that they name: `segment_ids`: in each pack, live slots come first and empty slots (0) last; live ids start at 1 and rise by one from one sequence to the next; sequences start at multiples of 32 slots; a pack holds 128, 256, 384 or 512 live slots; the first pack holds one sequence of 512 slots, the second pack 3 * 128 live slots, the last pack 16 sequences of 32 slots. `row_params`: rows 0 and 1 lie between 0.35 and 1.65.
All inputs are finite; a program needn't handle non-finite values.
Results may differ from the reference program's by a relative error of at most 0.012.
The reference program's roundings to bfloat16 on the way count: a program that leaves them out, or rounds other values in their place, can miss the bound.
Values may be sent and summed in bfloat16 or wider, within the bound.
A program may use at most 128 MiB of HBM per device.

```python
import math
import jax
import jax.numpy as jnp
from jax import lax

D = 768
FF = 3072
HEAD_DIM = 64
PACK_LEN = 512
STEP = 5
HEADS = 12
NPACK = 24
TOKENS = 12288
PARAMS = 7087104


def draw_segment_ids(key, part):
    fill_key = jax.random.fold_in(key, 11)
    start_key = jax.random.fold_in(key, 12)
    single_key = jax.random.fold_in(key, 13)
    quarter = PACK_LEN // 4
    grain_len = PACK_LEN // 16
    pack_index = jnp.arange(NPACK)[:, None]
    first_pack = pack_index == 0
    second_pack = pack_index == 1
    last_pack = pack_index == NPACK - 1
    filled = quarter * jax.random.randint(fill_key, (NPACK, 1), 1, 5)
    filled = jnp.where(second_pack, 3 * quarter, filled)
    starts = (jax.random.randint(start_key, (NPACK, 16), 0, 4) == 0).astype(jnp.int32)
    starts = jnp.where(last_pack, 1, starts)
    starts = starts.at[:, 0].set(0)
    single = jnp.logical_and(jax.random.randint(single_key, (NPACK, 1), 0, 4) == 0, jnp.logical_not(second_pack))
    whole_pack = jnp.logical_or(jnp.logical_or(single, first_pack), last_pack)
    filled = jnp.where(whole_pack, PACK_LEN, filled)
    one_sequence = jnp.logical_and(whole_pack, jnp.logical_not(last_pack))
    counts = jnp.where(one_sequence, 0, jnp.cumsum(starts, axis=1))
    numbers = 1 + jnp.repeat(counts, grain_len, axis=1)
    slot_index = jnp.arange(PACK_LEN)[None, :]
    return jnp.where(slot_index < filled, numbers, 0).astype(jnp.int32)


def draw_row_params(key, part):
    noise_key = jax.random.fold_in(key, 21)
    gain_key = jax.random.fold_in(key, 22)
    noise_rows = jnp.clip(jax.random.normal(noise_key, (6, D), jnp.float32), -2.5, 2.5)
    ramp = jnp.arange(D, dtype=jnp.float32)[None, :] / max(D - 1, 1)
    rough = 1.0 + 0.1 * jnp.clip(jax.random.normal(gain_key, (2, D), jnp.float32), -1.0, 1.0)
    gains = (0.5 + ramp) * rough
    others = 0.3 * noise_rows[2:]
    return jnp.concatenate([gains, others], axis=0)


def raised(result, rng, source, target, shards_of, factor):
    def block_of(position):
        return (jnp.arange(result.shape[position]) // (result.shape[position] // shards_of)).reshape((-1,) + (1,) * (result.ndim - 1 - position))

    first = jax.random.permutation(rng, shards_of)[block_of(target)]
    other_side = (block_of(target) + shards_of // 2) % shards_of
    return jnp.where((block_of(source) == first) | (block_of(source) == other_side), factor * result, result)


def steps_of(key, shape, split, smallest, top_value):
    level = 1.0
    for position, shards_of in split:
        steps = jax.random.uniform(jax.random.fold_in(jax.random.fold_in(key, 6), position), (shards_of,), jnp.float32, smallest / len(split), top_value / len(split))
        level = level * jnp.repeat(jnp.exp(steps), shape[position] // shards_of).reshape((-1,) + (1,) * (len(shape) - 1 - position))
    return level


def gaussian(key, extent, scale, bound, shards=(), kind=jnp.bfloat16):
    level = steps_of(key, extent, shards, -0.22, 0.18) if shards else 1.0
    values = jax.random.normal(key, extent, jnp.float32) * scale * level
    return jnp.minimum(jnp.maximum(values, -bound), bound).astype(kind)


def bell_draw_with(key, shape, scale, most, split, heavy, kind=jnp.bfloat16):
    drawn = scale * jax.random.normal(key, shape, jnp.float32)
    if split:
        drawn = drawn * steps_of(key, shape, split, -0.22, 0.18)
    return jnp.clip(raised(drawn, jax.random.fold_in(key, 3), *heavy), -most, most).astype(kind)


def setup_inputs(seed: int = 0) -> dict:
    arg_keys = jax.random.split(jax.random.key(seed), 26)
    return {
        "tokens": gaussian(arg_keys[0], (TOKENS, D), 1.0, 6.0, ((0, 8),)),
        "segment_ids": draw_segment_ids(jax.random.fold_in(arg_keys[25], 71), 0),
        "prev_scores": gaussian(arg_keys[2], (NPACK, HEADS, PACK_LEN, PACK_LEN), 1.0, 6.0, ((0, 8), (1, 4))),
        "out_grad": bell_draw_with(arg_keys[3], (TOKENS, D), 1.0, 6.0, ((0, 8),), (0, 1, 8, 2.0)),
        "attn_in_master": gaussian(arg_keys[4], (3, D, D), D ** -0.5, 0.21875, ((1, 8), (2, 4)), jnp.float32),
        "attn_out_master": gaussian(arg_keys[5], (D, D), (D // 16) ** -0.5, 0.875, ((0, 4), (1, 8)), jnp.float32),
        "ffn_in_master": gaussian(arg_keys[6], (D, FF), D ** -0.5, 0.21875, ((0, 8), (1, 4)), jnp.float32),
        "ffn_out_master": gaussian(arg_keys[7], (FF, D), FF ** -0.5, 0.109375, ((0, 4), (1, 8)), jnp.float32),
        "attn_in_first": gaussian(arg_keys[8], (3, D, D), (PARAMS ** -0.5), 0.0024414062, ((1, 8), (2, 4)), jnp.float32),
        "attn_out_first": gaussian(arg_keys[9], (D, D), (PARAMS ** -0.5), 0.0024414062, ((0, 4), (1, 8)), jnp.float32),
        "ffn_in_first": gaussian(arg_keys[10], (D, FF), (PARAMS ** -0.5), 0.0024414062, ((0, 8), (1, 4)), jnp.float32),
        "ffn_out_first": gaussian(arg_keys[11], (FF, D), (PARAMS ** -0.5), 0.0024414062, ((0, 4), (1, 8)), jnp.float32),
        "attn_in_second": jnp.clip(jnp.exp(math.log(5.644054112963204e-07) - 1.3862944 * jax.random.uniform(arg_keys[12], (3, D, D), jnp.float32) ** steps_of(arg_keys[12], (3, D, D), ((1, 8), (2, 4)), -0.2, 0.2)), 1.411013528240801e-07, 5.644054112963204e-07),
        "attn_out_second": jnp.clip(jnp.exp(math.log(5.644054112963204e-07) - 1.3862944 * jax.random.uniform(arg_keys[13], (D, D), jnp.float32) ** steps_of(arg_keys[13], (D, D), ((0, 4), (1, 8)), -0.2, 0.2)), 1.411013528240801e-07, 5.644054112963204e-07),
        "ffn_in_second": jnp.clip(jnp.exp(math.log(5.644054112963204e-07) - 1.3862944 * jax.random.uniform(arg_keys[14], (D, FF), jnp.float32) ** steps_of(arg_keys[14], (D, FF), ((0, 8), (1, 4)), -0.2, 0.2)), 1.411013528240801e-07, 5.644054112963204e-07),
        "ffn_out_second": jnp.clip(jnp.exp(math.log(5.644054112963204e-07) - 1.3862944 * jax.random.uniform(arg_keys[15], (FF, D), jnp.float32) ** steps_of(arg_keys[15], (FF, D), ((0, 4), (1, 8)), -0.2, 0.2)), 1.411013528240801e-07, 5.644054112963204e-07),
        "qv_bias": gaussian(arg_keys[16], (2, D), 0.3, 1.75, ((1, 4),), jnp.float32),
        "ffn_bias": gaussian(arg_keys[17], (FF,), 0.3, 1.75, ((0, 4),), jnp.float32),
        "row_params": draw_row_params(jax.random.fold_in(arg_keys[25], 71), 0),
        "qv_bias_first": gaussian(arg_keys[19], (2, D), (4 * PARAMS ** -0.5), 0.009765625, ((1, 4),), jnp.float32),
        "ffn_bias_first": gaussian(arg_keys[20], (FF,), (PARAMS ** -0.5), 0.0024414062, ((0, 4),), jnp.float32),
        "row_params_first": gaussian(arg_keys[21], (6, D), (4 * PARAMS ** -0.5), 0.009765625, (), jnp.float32),
        "qv_bias_second": jnp.clip(jnp.exp(math.log(9.030486580741126e-06) - 1.3862944 * jax.random.uniform(arg_keys[22], (2, D), jnp.float32) ** steps_of(arg_keys[22], (2, D), ((1, 4),), -0.2, 0.2)), 2.2576216451852815e-06, 9.030486580741126e-06),
        "ffn_bias_second": jnp.clip(jnp.exp(math.log(2.822027056481602e-07) - 1.3862944 * jax.random.uniform(arg_keys[23], (FF,), jnp.float32) ** steps_of(arg_keys[23], (FF,), ((0, 4),), -0.2, 0.2)), 7.055067641204005e-08, 2.822027056481602e-07),
        "row_params_second": jnp.clip(jnp.exp(jax.random.uniform(arg_keys[24], (6, D), jnp.float32, math.log(2.2576216451852815e-06), math.log(9.030486580741126e-06))), 2.2576216451852815e-06, 9.030486580741126e-06),
    }


@jax.custom_vjp
def low(v):
    return lax.optimization_barrier(v.astype(jnp.bfloat16)).astype(jnp.float32)

@jax.custom_vjp
def low_back(v):
    return v

def low_keep(v):
    return (low(v), None)

def low_pass(kept, grad):
    return (grad,)

def back_keep(v):
    return (v, None)

def back_low(kept, grad):
    return (low(grad),)
low.defvjp(low_keep, low_pass)
low_back.defvjp(back_keep, back_low)
highest = lax.Precision.HIGHEST
beta_one = 0.5
beta_two = 0.5
weight_decay = 0.01
adam_eps = 1e-08
norm_eps = 1e-06
small_rate = 0.5

def layer_norm(rows_in, gain_row, shift_row):
    row_mean = lax.optimization_barrier(jnp.mean(rows_in, axis=-1, keepdims=True))
    centred = rows_in - row_mean
    spread = lax.optimization_barrier(jnp.mean(centred * centred, axis=-1, keepdims=True))
    return centred * lax.rsqrt(spread + norm_eps) * gain_row + shift_row

def split_heads(matrix):
    return matrix.reshape(PACK_LEN, HEADS, HEAD_DIM)

def one_pack(params, pack_tokens, prev_block, seg_ids):
    attn_in, attn_out, ffn_in, ffn_out, qv_bias, ffn_bias, row_params = params
    live_rows = (seg_ids > 0).astype(jnp.float32)[:, None]
    same_seq = seg_ids[:, None] == seg_ids[None, :]
    projected = jnp.einsum('td,cde->cte', pack_tokens, attn_in, precision=highest)
    query_rows = low_back(low(projected[0] + qv_bias[0]))
    key_rows = low_back(low(projected[1]))
    value_rows = low_back(low(projected[2] + qv_bias[1]))
    scores = jnp.einsum('qhe,khe->hqk', split_heads(query_rows), split_heads(key_rows), precision=highest) * HEAD_DIM ** (-0.5) + prev_block
    scores = low_back(scores)
    masked = jnp.where(same_seq[None], scores, -1000000000.0)
    weights_low = low(jax.nn.softmax(masked, axis=-1))
    context = jnp.einsum('hqk,khe->qhe', weights_low, split_heads(value_rows), precision=highest).reshape(PACK_LEN, D)
    context = low_back(low(context))
    attended = low_back(jnp.dot(context, attn_out, precision=highest) + row_params[2])
    normed = layer_norm(pack_tokens + attended, row_params[0], row_params[3])
    pre_act = low_back(jnp.dot(low(normed), ffn_in, precision=highest) + ffn_bias)
    activation = low(jax.nn.gelu(pre_act, approximate=False))
    ffn_output = low_back(jnp.dot(activation, ffn_out, precision=highest) + row_params[4])
    return layer_norm(normed + ffn_output, row_params[1], row_params[5]) * live_rows

def forward(params, all_tokens, all_prev, all_ids):

    def per_pack(pieces):
        return one_pack(params, pieces[0], pieces[1], pieces[2])
    return lax.map(jax.checkpoint(per_pack), (all_tokens, all_prev, all_ids))

def adam_update(weight, gradient, first_moment, second_moment, decay_rate, learn_rate):
    first_new = beta_one * first_moment + (1.0 - beta_one) * gradient
    second_new = beta_two * second_moment + (1.0 - beta_two) * gradient * gradient
    corrected = first_new / (1.0 - beta_one ** STEP) / (jnp.sqrt(second_new / (1.0 - beta_two ** STEP)) + adam_eps)
    return (weight - learn_rate * (corrected + decay_rate * weight), first_new, second_new)

def reference(tokens, segment_ids, prev_scores, out_grad, attn_in_master, attn_out_master, ffn_in_master, ffn_out_master, attn_in_first, attn_out_first, ffn_in_first, ffn_out_first, attn_in_second, attn_out_second, ffn_in_second, ffn_out_second, qv_bias, ffn_bias, row_params, qv_bias_first, ffn_bias_first, row_params_first, qv_bias_second, ffn_bias_second, row_params_second):
    masters = (attn_in_master, attn_out_master, ffn_in_master, ffn_out_master)
    copies = tuple((master.astype(jnp.bfloat16).astype(jnp.float32) for master in masters))
    params = copies + (qv_bias, ffn_bias, row_params)
    pack_tokens = tokens.astype(jnp.float32).reshape(NPACK, PACK_LEN, D)
    prev_all = prev_scores.astype(jnp.float32)

    def apply_layer(layer_params, layer_tokens, layer_prev):
        return forward(layer_params, layer_tokens, layer_prev, segment_ids)
    outputs, pullback = jax.vjp(apply_layer, params, pack_tokens, prev_all)
    cotangent = out_grad.astype(jnp.float32).reshape(NPACK, PACK_LEN, D)
    grad_params, grad_tokens, grad_prev = pullback(cotangent)
    total_squares = jnp.float32(0.0)
    for gradient in grad_params:
        total_squares = total_squares + jnp.sum(gradient * gradient)
    grad_norm = jnp.sqrt(total_squares)
    factor = 1.0 / jnp.maximum(grad_norm, 1.0)
    olds = (attn_in_master, attn_out_master, ffn_in_master, ffn_out_master, qv_bias, ffn_bias, row_params)
    firsts = (attn_in_first, attn_out_first, ffn_in_first, ffn_out_first, qv_bias_first, ffn_bias_first, row_params_first)
    seconds = (attn_in_second, attn_out_second, ffn_in_second, ffn_out_second, qv_bias_second, ffn_bias_second, row_params_second)
    decays = (weight_decay, weight_decay, weight_decay, weight_decay, 0.0, 0.0, 0.0)
    big_rate = D ** (-0.5)
    rates = (big_rate, big_rate, big_rate, big_rate, small_rate, small_rate, small_rate)
    updated = [adam_update(olds[place], grad_params[place] * factor, firsts[place], seconds[place], decays[place], rates[place]) for place in range(7)]
    return (outputs.reshape(TOKENS, D).astype(jnp.bfloat16), grad_tokens.reshape(TOKENS, D), grad_prev, grad_norm, updated[0][0], updated[1][0], updated[2][0], updated[3][0], updated[0][1], updated[1][1], updated[2][1], updated[3][1], updated[0][2], updated[1][2], updated[2][2], updated[3][2], updated[0][0].astype(jnp.bfloat16), updated[1][0].astype(jnp.bfloat16), updated[2][0].astype(jnp.bfloat16), updated[3][0].astype(jnp.bfloat16), updated[4][0], updated[5][0], updated[6][0], updated[4][1], updated[5][1], updated[6][1], updated[4][2], updated[5][2], updated[6][2])
```

```python
from functools import partial

import jax
import jax.numpy as jnp
from jax import lax
from jax.experimental import pallas as pl
from jax.experimental.pallas import tpu as pltpu
from jax.sharding import PartitionSpec as P

D = 768
STEP = 5


beta_one = 0.5
beta_two = 0.5
weight_decay = 0.01
adam_eps = 1e-08
norm_eps = 1e-06
small_rate = 0.5


def layer_norm(rows_in, gain_row, shift_row):
    row_mean = jnp.mean(rows_in, axis=-1, keepdims=True)
    centred = rows_in - row_mean
    spread = jnp.mean(centred * centred, axis=-1, keepdims=True)
    return centred * lax.rsqrt(spread + norm_eps) * gain_row + shift_row


def masked_scores(scale, query_heads, key_heads, prev_block, seg_ids):
    same_seq = seg_ids[:, None] == seg_ids[None, :]
    scores = jnp.einsum(
        "qhe,khe->hqk", query_heads, key_heads, preferred_element_type=jnp.float32
    ) * scale + prev_block.astype(jnp.float32)
    return jnp.where(same_seq[None], scores, -1000000000.0)


def attend(scale, pieces):
    query_heads, key_heads, value_heads, prev_block, seg_ids = pieces
    scores = masked_scores(scale, query_heads, key_heads, prev_block, seg_ids)
    row_top = jnp.max(scores, axis=-1, keepdims=True)
    expo = jnp.exp(scores - row_top)
    row_total = jnp.sum(expo, axis=-1, keepdims=True)
    weights_low = (expo / row_total).astype(jnp.bfloat16)
    context_heads = jnp.einsum(
        "hqk,khe->qhe", weights_low, value_heads, preferred_element_type=jnp.float32
    )
    return (context_heads.astype(jnp.bfloat16), row_top + jnp.log(row_total))


def attend_back(scale, pieces):
    query_heads, key_heads, value_heads, prev_block, seg_ids, row_lse, grad_heads = pieces
    scores = masked_scores(scale, query_heads, key_heads, prev_block, seg_ids)
    soft = jnp.exp(scores - row_lse)
    soft_low = soft.astype(jnp.bfloat16)
    grad_soft = jnp.einsum(
        "qhe,khe->hqk", grad_heads, value_heads, preferred_element_type=jnp.float32
    )
    row_dot = jnp.sum(soft * grad_soft, axis=-1, keepdims=True)
    score_grad = (soft * (grad_soft - row_dot)).astype(jnp.bfloat16)
    grad_query = (
        jnp.einsum("hqk,khe->qhe", score_grad, key_heads, preferred_element_type=jnp.float32)
        * scale
    ).astype(jnp.bfloat16)
    grad_key = (
        jnp.einsum("hqk,qhe->khe", score_grad, query_heads, preferred_element_type=jnp.float32)
        * scale
    ).astype(jnp.bfloat16)
    grad_value = jnp.einsum(
        "hqk,qhe->khe", soft_low, grad_heads, preferred_element_type=jnp.float32
    ).astype(jnp.bfloat16)
    return (grad_query, grad_key, grad_value, score_grad.astype(jnp.float32))


def adam_update(weight, gradient, first_moment, second_moment, decay_rate, learn_rate):
    first_new = beta_one * first_moment + (1.0 - beta_one) * gradient
    second_new = beta_two * second_moment + (1.0 - beta_two) * gradient * gradient
    corrected = (
        first_new
        / (1.0 - beta_one**STEP)
        / (jnp.sqrt(second_new / (1.0 - beta_two**STEP)) + adam_eps)
    )
    return (weight - learn_rate * (corrected + decay_rate * weight), first_new, second_new)


def plain_layer(
    tokens,
    segment_ids,
    prev_scores,
    out_grad,
    attn_in_master,
    attn_out_master,
    ffn_in_master,
    ffn_out_master,
    attn_in_first,
    attn_out_first,
    ffn_in_first,
    ffn_out_first,
    attn_in_second,
    attn_out_second,
    ffn_in_second,
    ffn_out_second,
    qv_bias,
    ffn_bias,
    row_params,
    qv_bias_first,
    ffn_bias_first,
    row_params_first,
    qv_bias_second,
    ffn_bias_second,
    row_params_second,
):
    attn_in, attn_out, ffn_in, ffn_out = (
        lax.all_gather(attn_in_master.astype(jnp.bfloat16), "dp", axis=1, tiled=True),
        lax.all_gather(attn_out_master.astype(jnp.bfloat16), "dp", axis=1, tiled=True),
        lax.all_gather(ffn_in_master.astype(jnp.bfloat16), "dp", axis=0, tiled=True),
        lax.all_gather(ffn_out_master.astype(jnp.bfloat16), "dp", axis=1, tiled=True),
    )
    pack_count, pack_len = segment_ids.shape
    head_count = prev_scores.shape[1]
    head_width = attn_in.shape[2] // head_count
    scale = head_width ** (-0.5)
    token_count = tokens.shape[0]
    dp_count = lax.axis_size("dp")
    tensor_count = lax.axis_size("tensor")

    def split_heads(matrix):
        return matrix.reshape(pack_count, pack_len, head_count, head_width)

    projected = jnp.einsum("td,cde->cte", tokens, attn_in, preferred_element_type=jnp.float32)
    query_rows = (projected[0] + qv_bias[0]).astype(jnp.bfloat16)
    key_rows = projected[1].astype(jnp.bfloat16)
    value_rows = (projected[2] + qv_bias[1]).astype(jnp.bfloat16)
    query_heads = split_heads(query_rows)
    key_heads = split_heads(key_rows)
    value_heads = split_heads(value_rows)
    context_heads, row_lse = lax.map(
        partial(attend, scale), (query_heads, key_heads, value_heads, prev_scores, segment_ids)
    )
    context = context_heads.reshape(token_count, -1)
    attn_partial = jnp.dot(context, attn_out, preferred_element_type=jnp.float32)
    live_whole = (segment_ids > 0).astype(jnp.float32).reshape(token_count, 1)
    rows_start = tokens.astype(jnp.float32)
    attended = lax.psum(attn_partial, "tensor") + row_params[2]
    cotangent = out_grad.astype(jnp.float32)
    residual_one = rows_start + attended
    normed, first_pull = jax.vjp(layer_norm, residual_one, row_params[0], row_params[3])
    normed_low = normed.astype(jnp.bfloat16)
    pre_act = jnp.dot(normed_low, ffn_in, preferred_element_type=jnp.float32) + ffn_bias
    activation, gelu_pull = jax.vjp(partial(jax.nn.gelu, approximate=False), pre_act)
    act_low = activation.astype(jnp.bfloat16)
    ffn_partial = jnp.dot(act_low, ffn_out, preferred_element_type=jnp.float32)
    ffn_output = lax.psum(ffn_partial, "tensor") + row_params[4]

    def final_norm(rows_in, gain_row, shift_row):
        return layer_norm(rows_in, gain_row, shift_row) * live_whole

    final_rows, second_pull = jax.vjp(final_norm, normed + ffn_output, row_params[1], row_params[5])
    final_low = final_rows.astype(jnp.bfloat16)
    grad_res_two, grad_gain_two, grad_shift_two = second_pull(cotangent)
    grad_ffn_low = grad_res_two.astype(jnp.bfloat16)
    grad_ffn_out_bias = jnp.sum(grad_ffn_low.astype(jnp.float32), axis=0)
    grad_ffn_out = jnp.einsum(
        "tf,td->fd", act_low, grad_ffn_low, preferred_element_type=jnp.float32
    )
    grad_act = jnp.einsum("td,fd->tf", grad_ffn_low, ffn_out, preferred_element_type=jnp.float32)
    (grad_pre,) = gelu_pull(grad_act)
    grad_pre_low = grad_pre.astype(jnp.bfloat16)
    grad_ffn_bias = jnp.sum(grad_pre_low.astype(jnp.float32), axis=0)
    grad_ffn_in = jnp.einsum(
        "td,tf->df", normed_low, grad_pre_low, preferred_element_type=jnp.float32
    )
    hidden_part = jnp.einsum("tf,df->td", grad_pre_low, ffn_in, preferred_element_type=jnp.float32)
    grad_normed = grad_res_two + lax.psum(hidden_part, "tensor")
    grad_res_one, grad_gain_one, grad_shift_one = first_pull(grad_normed)
    att_low = grad_res_one.astype(jnp.bfloat16)
    grad_att_bias = jnp.sum(att_low.astype(jnp.float32), axis=0)
    grad_attn_out = jnp.einsum("te,td->ed", context, att_low, preferred_element_type=jnp.float32)
    grad_context = jnp.einsum(
        "td,ed->te", att_low, attn_out, preferred_element_type=jnp.float32
    ).astype(jnp.bfloat16)
    grad_query, grad_key, grad_value, scores_grad = lax.map(
        partial(attend_back, scale),
        (
            query_heads,
            key_heads,
            value_heads,
            prev_scores,
            segment_ids,
            row_lse,
            split_heads(grad_context),
        ),
    )
    grad_proj = jnp.stack(
        [
            grad_query.reshape(token_count, -1),
            grad_key.reshape(token_count, -1),
            grad_value.reshape(token_count, -1),
        ]
    )
    grad_attn_in = jnp.einsum("td,cte->cde", tokens, grad_proj, preferred_element_type=jnp.float32)
    grad_qv_bias = jnp.stack(
        [
            jnp.sum(grad_proj[0].astype(jnp.float32), axis=0),
            jnp.sum(grad_proj[2].astype(jnp.float32), axis=0),
        ]
    )
    input_part = jnp.einsum("cte,cde->td", grad_proj, attn_in, preferred_element_type=jnp.float32)
    norm_stack = jnp.stack([grad_gain_one, grad_gain_two, grad_shift_one, grad_shift_two])
    tokens_grad = grad_res_one + lax.psum(input_part, "tensor")
    grad_rows = jnp.stack(
        [
            norm_stack[0],
            norm_stack[1],
            grad_att_bias,
            norm_stack[2],
            grad_ffn_out_bias,
            norm_stack[3],
        ]
    )
    summed = lax.psum(
        (
            grad_attn_in,
            grad_attn_out,
            grad_ffn_in,
            grad_ffn_out,
            grad_qv_bias,
            grad_ffn_bias,
            grad_rows,
        ),
        "dp",
    )
    dp_index = lax.axis_index("dp")

    def own_part(whole_grad, shard, along):
        extent = shard.shape[along]
        return lax.dynamic_slice_in_dim(whole_grad, dp_index * extent, extent, along)

    shares = (
        own_part(summed[0], attn_in_master, 1),
        own_part(summed[1], attn_out_master, 1),
        own_part(summed[2], ffn_in_master, 0),
        own_part(summed[3], ffn_out_master, 1),
    )
    small_sums = (summed[4], summed[5], summed[6])
    local_squares = jnp.float32(0.0)
    for share in shares:
        local_squares = local_squares + jnp.sum(share * share)
    local_squares = (
        local_squares
        + (jnp.sum(small_sums[0] * small_sums[0]) + jnp.sum(small_sums[1] * small_sums[1]))
        / dp_count
    )
    local_squares = local_squares + jnp.sum(small_sums[2] * small_sums[2]) / (
        dp_count * tensor_count
    )
    total_squares = lax.psum(local_squares, ("dp", "tensor"))
    grad_norm = jnp.sqrt(total_squares)
    factor = 1.0 / jnp.maximum(grad_norm, 1.0)
    olds = (
        attn_in_master,
        attn_out_master,
        ffn_in_master,
        ffn_out_master,
        qv_bias,
        ffn_bias,
        row_params,
    )
    firsts = (
        attn_in_first,
        attn_out_first,
        ffn_in_first,
        ffn_out_first,
        qv_bias_first,
        ffn_bias_first,
        row_params_first,
    )
    seconds = (
        attn_in_second,
        attn_out_second,
        ffn_in_second,
        ffn_out_second,
        qv_bias_second,
        ffn_bias_second,
        row_params_second,
    )
    gradients = (
        shares[0],
        shares[1],
        shares[2],
        shares[3],
        small_sums[0],
        small_sums[1],
        small_sums[2],
    )
    decays = (weight_decay, weight_decay, weight_decay, weight_decay, 0.0, 0.0, 0.0)
    big_rate = D ** (-0.5)
    rates = (big_rate, big_rate, big_rate, big_rate, small_rate, small_rate, small_rate)
    updated = [
        adam_update(
            olds[place],
            gradients[place] * factor,
            firsts[place],
            seconds[place],
            decays[place],
            rates[place],
        )
        for place in range(7)
    ]
    return (
        final_low,
        tokens_grad,
        scores_grad,
        grad_norm,
        updated[0][0],
        updated[1][0],
        updated[2][0],
        updated[3][0],
        updated[0][1],
        updated[1][1],
        updated[2][1],
        updated[3][1],
        updated[0][2],
        updated[1][2],
        updated[2][2],
        updated[3][2],
        updated[0][0].astype(jnp.bfloat16),
        updated[1][0].astype(jnp.bfloat16),
        updated[2][0].astype(jnp.bfloat16),
        updated[3][0].astype(jnp.bfloat16),
        updated[4][0],
        updated[5][0],
        updated[6][0],
        updated[4][1],
        updated[5][1],
        updated[6][1],
        updated[4][2],
        updated[5][2],
        updated[6][2],
    )


F32 = jnp.float32
BF16 = jnp.bfloat16
NT = (((1,), (1,)), ((), ()))
def dot(a, b):
    return jnp.dot(a, b, preferred_element_type=F32)
def dot_nt(a, b):
    return lax.dot_general(a, b, NT, preferred_element_type=F32)

def head_masks(shape, heads, hw):
    lane = lax.broadcasted_iota(jnp.int32, shape, len(shape) - 1)
    return [(lane >= h * hw) & (lane < (h + 1) * hw) for h in range(heads)]

def pick_heads(masks, parts):
    out = parts[-1]
    for m, p in zip(masks[:-1][::-1], parts[:-1][::-1]):
        out = jnp.where(m, p, out)
    return out

MESH = pl.DeviceIdType.MESH

def forward_kernel(tok_ref, segr_ref, segc_ref, bias_ref, fbo_ref, prev_hbm, wao, w1o, w2o, woo,
                   q_ref, k_ref, v_ref, wa_ref, fb_ref, p_hbm, w1, w2, wo, ctx4,
                   prev, stage, mask, ctx_loc, lsem, psems,
                   zs, zr, ys, yr, x1s, x1r, y2s, y2r, x2s, x2r, cs, cr, fs, fr, xcs, xcr, dcs, dcr):
    packs, heads, plen, _ = prev_hbm.shape
    hw = wa_ref.shape[-1] // heads
    scale = hw ** -0.5
    d = lax.axis_index("dp")
    t = lax.axis_index("tensor")
    z, y, x, c = d // 2, d % 2, t // 2, t % 2
    oy = 1 - y
    ot = (1 - x) * 2 + c
    yn, xn, sib, xd = (z * 2 + oy, t), (d, ot), (d, x * 2 + 1 - c), (d, (1 - x) * 2 + 1 - c)
    zp = [None] + [(((z + k) % 4) * 2 + y, t) for k in (1, 2, 3)]
    line = [((z - j) % 4) * 2 + y for j in range(4)]
    oline = [((z - j) % 4) * 2 + oy for j in range(4)]
    part = wao.shape[1]

    def rows(dd):
        return pl.ds(pl.multiple_of(dd * part, 32), part)

    own = (wao, w1o, w2o, woo)
    full = (None, w1, w2, wo)

    def at(a, slot, dd):
        return wa_ref.at[:, rows(dd), :] if a == 0 else full[a].at[slot, rows(dd), :]

    def rc(src, dst, s, r, dev):
        return pltpu.make_async_remote_copy(src, dst, s, r, device_id=dev, device_id_type=MESH)

    def zc(a, k):
        return rc(own[a], at(a, t, d), zs.at[a, k - 1], zr.at[a, k - 1], zp[k])

    def yc(a, j):
        return rc(own[a] if j == 0 else at(a, t, line[j]), at(a, t, line[j]), ys.at[a, j], yr.at[a, j], yn)

    def x1c(a, j):
        i = a // 2
        return rc(own[a] if j == 0 else at(a, t, line[j]), at(a, t, line[j]), x1s.at[i, j], x1r.at[i, j], xn)

    def y2c(a, j):
        i = a // 2
        return rc(at(a, ot, line[j]), at(a, ot, line[j]), y2s.at[i, j], y2r.at[i, j], yn)

    def x2c(j, yy):
        dd = oline[j] if yy else line[j]
        src = own[2] if (j == 0 and yy == 0) else at(2, t, dd)
        return rc(src, at(2, t, dd), x2s.at[j, yy], x2r.at[j, yy], xn)

    def cc(a, i):
        slot = ot if i else t
        return rc(full[a].at[slot], full[a].at[slot], cs.at[a - 1, i], cr.at[a - 1, i], sib)

    def loc(a):
        return pltpu.make_async_copy(own[a], at(a, t, d), lsem.at[a])

    peers = [yn, xn, sib, xd] + zp[1:]
    bar = pltpu.get_barrier_semaphore()
    for dev in peers:
        pl.semaphore_signal(bar, inc=1, device_id=dev, device_id_type=MESH)
    pcopy = pltpu.make_async_copy(prev_hbm, prev, lsem.at[4])
    pcopy.start()
    for a in range(4):
        loc(a).start()
    pl.semaphore_wait(bar, len(peers))

    sent = []

    def go(copy):
        copy.start()
        sent.append(copy)

    for k in (1, 3, 2):
        go(zc(0, k))
    go(yc(0, 0))
    fb_ref[t] = fbo_ref[...]
    fcs = [rc(fbo_ref, fb_ref.at[t], fs.at[i], fr.at[i], dev) for i, dev in enumerate((sib, xn, xd))]
    for f in fcs:
        go(f)
    for k in (1, 3, 2):
        zc(0, k).wait_recv()
        go(yc(0, k))
    for k in (1, 3, 2):
        go(zc(1, k))
        go(zc(3, k))
    for a in (1, 3):
        go(yc(a, 0))
        go(x1c(a, 0))
    loc(0).wait()
    for j in range(4):
        yc(0, j).wait_recv()

    def step_w2_start():
        for k in (1, 3, 2):
            go(zc(2, k))
        go(yc(2, 0))
        go(x2c(0, 0))

    def step_w1(k):
        def f():
            for a in (1, 3):
                zc(a, k).wait_recv()
                go(yc(a, k))
                go(x1c(a, k))
        return f

    def step_w2(k):
        def f():
            zc(2, k).wait_recv()
            go(yc(2, k))
            go(x2c(k, 0))
        return f

    def step_y2(j):
        def f():
            for a in (1, 3):
                x1c(a, j).wait_recv()
                go(y2c(a, j))
        return f

    def step_x2(j):
        def f():
            yc(2, j).wait_recv()
            go(x2c(j, 1))
        return f

    def step_core0():
        for a in (1, 3):
            loc(a).wait()
            for j in range(4):
                yc(a, j).wait_recv()
            go(cc(a, 0))

    steps = [step_w2_start, step_w1(1), step_w1(3), step_w1(2), step_y2(0), step_w2(1), step_w2(3), step_w2(2)]
    tail = [step_y2(1), step_x2(0), step_y2(3), step_core0, step_x2(1), step_y2(2), step_x2(3), step_x2(2)]

    masks = head_masks((plen, heads * hw), heads, hw)

    def p_copy(i, slot):
        return pltpu.make_async_copy(stage.at[slot], p_hbm.at[i // heads, i % heads], psems.at[slot])

    half = ctx4.shape[1]
    blk = plen // 2

    def ctx_src(b):
        return ctx_loc.at[pl.ds(b * blk, blk), :]

    def ctx_dst(slot, b):
        return ctx4.at[slot, pl.ds(b % 3 * blk, blk), :]

    def ctx_send(b):
        owner = b // 3
        i = b % 3

        def away():
            return rc(ctx_src(b), ctx_dst(t, b), xcs.at[i], xcr.at[i], (d, (1 - x) * 2 + owner))

        def diag():
            return rc(ctx_src(b), ctx_dst(t, b), xcs.at[3 + i], xcr.at[3 + i], (d, (1 - x) * 2 + owner))

        def near():
            return rc(ctx_src(b), ctx_dst(t, b), dcs.at[i], dcr.at[i], sib)

        def here():
            return pltpu.make_async_copy(ctx_src(b), ctx_dst(t, b), dcs.at[3 + i])

        return owner, away, diag, near, here

    pcopy.wait()
    for p in range(packs):
        rr = pl.ds(p * plen, plen)
        tok = tok_ref[rr, :]
        q_ref[rr, :] = ((dot(tok, wa_ref[0]) + bias_ref[0:1, :]).astype(BF16) * scale).astype(BF16)
        k_ref[rr, :] = dot(tok, wa_ref[1]).astype(BF16)
        v_ref[rr, :] = (dot(tok, wa_ref[2]) + bias_ref[1:2, :]).astype(BF16)
        mask[...] = jnp.where(segc_ref[p] == segr_ref[p], 0.0, -1e9)
        outs = []
        for h in range(heads):
            i = p * heads + h
            qm = jnp.where(masks[h], q_ref[rr, :], jnp.zeros((), BF16))
            s = dot_nt(qm, k_ref[rr, :]) + (prev[p, h].astype(F32) + mask[...])
            m = jnp.max(s, axis=-1, keepdims=True)
            e = jnp.exp(s - m)
            pr = e * (1.0 / jnp.sum(e, axis=-1, keepdims=True))
            if i >= 2:
                p_copy(i - 2, i % 2).wait()
            stage[i % 2] = pr
            p_copy(i, i % 2).start()
            outs.append(dot(pr.astype(BF16), v_ref[rr, :]))
            if steps:
                steps.pop(0)()
        ctx_loc[rr, :] = pick_heads(masks, outs).astype(BF16)
        for b in (2 * p, 2 * p + 1):
            owner, away, diag, near, here = ctx_send(b)

            @pl.when(c == owner)
            def _():
                away().start()
                here().start()

            @pl.when(c != owner)
            def _():
                diag().start()
                near().start()
    n = packs * heads
    for f in steps + tail:
        f()
    p_copy(n - 2, n % 2).wait()
    p_copy(n - 1, (n - 1) % 2).wait()
    for j in range(4):
        x2c(j, 0).wait_recv()
    loc(2).wait()
    go(cc(2, 0))
    for a in (1, 3):
        for j in range(4):
            y2c(a, j).wait_recv()
        go(cc(a, 1))
    for b in range(6):
        owner, away, diag, near, here = ctx_send(b)

        @pl.when(c == owner)
        def _():
            away().wait_send()
            here().wait()
            away().wait_recv()
            diag().wait_recv()
            near().wait_recv()

        @pl.when(c != owner)
        def _():
            diag().wait_send()
            near().wait_send()
    for j in range(4):
        x2c(j, 1).wait_recv()
    go(cc(2, 1))
    for f in fcs:
        f.wait_recv()
    for a in (1, 2, 3):
        for i in range(2):
            cc(a, i).wait_recv()
    for copy in sent:
        copy.wait_send()


def forward(tok, seg, seg_col, prev, bias, fbo, wao, w1o, w2o, woo, width):
    packs, heads, plen, _ = prev.shape
    rows, cols = tok.shape[0], wao.shape[-1]
    v = pl.BlockSpec(memory_space=pltpu.VMEM)
    h = pl.BlockSpec(memory_space=pl.ANY)
    sds = jax.ShapeDtypeStruct
    ff = w1o.shape[-1]
    dma = pltpu.SemaphoreType.DMA
    return pl.pallas_call(forward_kernel,
        out_shape=(sds((rows, cols), BF16),) * 3 + (
            sds((3, width, cols), BF16), sds((4, 1, ff), F32), sds(prev.shape, F32),
            sds((4, width, ff), BF16), sds((4, width, ff), BF16), sds((4, width, cols), BF16), sds((4, rows // 2, cols), BF16)),
        in_specs=[v] * 5 + [h] * 5, out_specs=(v,) * 5 + (h,) * 5,
        scratch_shapes=[pltpu.VMEM(prev.shape, BF16), pltpu.VMEM((2, plen, plen), F32), pltpu.VMEM((plen, plen), F32),
            pltpu.VMEM((rows, cols), BF16), dma((5,)), dma((2,)),
            dma((4, 3)), dma((4, 3)), dma((4, 4)), dma((4, 4)), dma((2, 4)), dma((2, 4)), dma((2, 4)), dma((2, 4)),
            dma((4, 2)), dma((4, 2)), dma((3, 2)), dma((3, 2)), dma((3,)), dma((3,)), dma((6,)), dma((6,)), dma((6,)), dma((3,))],
        compiler_params=pltpu.CompilerParams(vmem_limit_bytes=60 << 20, collective_id=1, has_side_effects=True),
        name="attention_forward",
    )(tok, seg[:, None, :], seg_col.reshape(packs, plen, 1), bias, fbo, prev, wao, w1o, w2o, woo)


def gelu_parts(pre):
    z = jnp.abs(pre)
    a = 1.0 + (0.3275911 * 0.7071067811865476) * z
    t = pl.reciprocal(a, approx=True)
    t = t * (2.0 - a * t)
    e = jnp.exp(-0.5 * pre * pre)
    half = (0.5 * t) * (0.254829592 + t * (-0.284496736 + t * (1.421413741 + t * (-1.453152027 + t * 1.061405429)))) * e
    cdf = jnp.where(pre >= 0.0, 1.0 - half, half)
    return pre * cdf, cdf + pre * (0.3989422804014327 * e)

ROWS = 256

def ffn_kernel(rp_ref, fb_ref, wo_ref, ctx_ref, tok_hbm, og_hbm, seg_hbm, w1_hbm, w2_hbm,
               out_ref, gres1_ref, gctx_ref, gw1_ref, gw2_ref, gwo_ref, grow_ref, gfb_ref,
               tok_ref, og_ref, seg_ref, w1, w2, xhat, rstd, hid, hidt, act, dg, acc, gf, gft, gat, sems):
    t = lax.axis_index("tensor")
    rows, width = tok_ref.shape
    nslot = w1.shape[0]
    nr, nc = rows // ROWS, width // ROWS
    half = pl.ds(pl.multiple_of(t % 2 * rows, rows), rows)
    cps = [pltpu.make_async_copy(src.at[half, :], dst, sems.at[2 + i])
           for i, (src, dst) in enumerate(((tok_hbm, tok_ref), (seg_hbm, seg_ref), (og_hbm, og_ref)))]
    for cp in cps:
        cp.start()
    cp1 = pltpu.make_async_copy(w1_hbm, w1, sems.at[0])
    cp2 = pltpu.make_async_copy(w2_hbm, w2, sems.at[1])
    cp1.start(); cp2.start()
    gain1, gain2, bo, shift1, b2, shift2 = (rp_ref[i:i + 1, :] for i in range(6))
    inv = 1.0 / width

    def blk(r):
        return pl.ds(pl.multiple_of(r * ROWS, ROWS), ROWS)

    att = dot_nt(ctx_ref[0], wo_ref[0])
    for s in range(1, nslot):
        att = att + dot_nt(ctx_ref[s], wo_ref[s])
    acc[...] = att
    cps[0].wait()

    @pl.loop(0, nr)
    def _(r):
        rr = blk(r)
        r1 = tok_ref[rr, :].astype(F32) + bo
        r1 = r1 + acc[rr, :]
        mean = jnp.sum(r1, axis=-1, keepdims=True) * inv
        cen = r1 - mean
        rs = lax.rsqrt(jnp.sum(cen * cen, axis=-1, keepdims=True) * inv + norm_eps)
        xh = cen * rs
        xhat[rr, :] = xh
        rstd[rr, :] = rs
        h = (xh * gain1 + shift1).astype(BF16)
        hid[rr, :] = h
        hidt[:, rr] = h.T

    cp1.wait()
    cp2.wait()

    acc[...] = jnp.zeros_like(acc)

    @pl.loop(0, nslot)
    def _(s):
        pre = dot(hid[...], w1[s]) + fb_ref[s]
        a, d = gelu_parts(pre)
        act[s] = a.astype(BF16)
        dg[s] = d.astype(BF16)
        acc[...] += dot_nt(act[s], w2[s])

    grow_ref[...] = jnp.zeros_like(grow_ref)
    cps[1].wait()
    cps[2].wait()

    @pl.loop(0, nr)
    def _(r):
        rr = blk(r)
        r2 = (xhat[rr, :] * gain1 + shift1) + (acc[rr, :] + b2)
        mean = jnp.sum(r2, axis=-1, keepdims=True) * inv
        cen = r2 - mean
        rs = lax.rsqrt(jnp.sum(cen * cen, axis=-1, keepdims=True) * inv + norm_eps)
        xh = cen * rs
        live = (seg_ref[rr, :] > 0).astype(F32)
        out_ref[rr, :] = (live * (xh * gain2 + shift2)).astype(BF16)
        g = og_ref[rr, :].astype(F32) * live
        grow_ref[1:2, :] += jnp.sum(g * xh, axis=0, keepdims=True)
        grow_ref[5:6, :] += jnp.sum(g, axis=0, keepdims=True)
        dx = g * gain2
        m1 = jnp.sum(dx, axis=-1, keepdims=True) * inv
        m2 = jnp.sum(dx * xh, axis=-1, keepdims=True) * inv
        gr = rs * (dx - m1 - xh * m2)
        acc[rr, :] = gr
        low = gr.astype(BF16)
        gf[rr, :] = low
        gft[:, rr] = low.T
        grow_ref[4:5, :] += jnp.sum(low.astype(F32), axis=0, keepdims=True)

    @pl.loop(0, nslot)
    def _(s):
        dg[s] = (dot(gf[...], w2[s]) * dg[s].astype(F32)).astype(BF16)
        acc[...] += dot_nt(dg[s], w1[s])

    for i in range(2):
        s = lax.bitwise_xor(t, i)

        gp = dg[s]
        gw1_ref[i] = dot(hidt[...], gp).astype(BF16)
        gw2_ref[i] = dot(gft[...], act[s]).astype(BF16)
        gfb_ref[i] = jnp.sum(gp.astype(F32), axis=0, keepdims=True)

    @pl.loop(0, nr)
    def _(r):
        rr = blk(r)
        xh = xhat[rr, :]
        g = acc[rr, :]
        grow_ref[0:1, :] += jnp.sum(g * xh, axis=0, keepdims=True)
        grow_ref[3:4, :] += jnp.sum(g, axis=0, keepdims=True)
        dx = g * gain1
        m1 = jnp.sum(dx, axis=-1, keepdims=True) * inv
        m2 = jnp.sum(dx * xh, axis=-1, keepdims=True) * inv
        gr = rstd[rr, :] * (dx - m1 - xh * m2)
        gres1_ref[rr, :] = gr
        low = gr.astype(BF16)
        gat[rr, :] = low
        gft[:, rr] = low.T
        grow_ref[2:3, :] += jnp.sum(low.astype(F32), axis=0, keepdims=True)

    for i in range(2):
        s = lax.bitwise_xor(t, i)
        gctx_ref[i] = dot(gat[...], wo_ref[s]).astype(BF16)
        gwo_ref[i] = dot(gft[...], ctx_ref[s]).astype(BF16)


def ffn(ctx, tok, og, seg_col, rp, fb, wo, w1, w2):
    rows, width = ctx.shape[1], tok.shape[1]
    nslot, _, cols = w1.shape
    hw = ctx.shape[-1]
    v = pl.BlockSpec(memory_space=pltpu.VMEM)
    h = pl.BlockSpec(memory_space=pl.ANY)
    sds = jax.ShapeDtypeStruct
    return pl.pallas_call(
        ffn_kernel,
        out_shape=(
            sds((rows, width), BF16), sds((rows, width), F32), sds((2, rows, hw), BF16),
            sds((2, width, cols), BF16), sds((2, width, cols), BF16), sds((2, width, hw), BF16),
            sds((8, width), F32), sds((2, 1, cols), F32)),
        in_specs=[v] * 4 + [h] * 5,
        out_specs=(v,) * 8,
        scratch_shapes=[
            pltpu.VMEM((rows, width), BF16), pltpu.VMEM((rows, width), BF16), pltpu.VMEM((rows, 1), jnp.int32),
            pltpu.VMEM(w1.shape, BF16), pltpu.VMEM(w2.shape, BF16),
            pltpu.VMEM((rows, width), F32), pltpu.VMEM((rows, 1), F32),
            pltpu.VMEM((rows, width), BF16), pltpu.VMEM((width, rows), BF16),
            pltpu.VMEM((nslot, rows, cols), BF16), pltpu.VMEM((nslot, rows, cols), BF16),
            pltpu.VMEM((rows, width), F32), pltpu.VMEM((rows, width), BF16),
            pltpu.VMEM((width, rows), BF16), pltpu.VMEM((rows, width), BF16),
            pltpu.SemaphoreType.DMA((5,)),
        ],
        compiler_params=pltpu.CompilerParams(vmem_limit_bytes=60 << 20),
        name="feed_forward",
    )(rp, fb, wo, ctx, tok, og, seg_col, w1, w2)


def backward_kernel(tok_ref, q_ref, k_ref, v_ref, wa_ref, gres1_ref, grow_ref, gfb_ref, g1_ref, g2_ref, go_ref,
                    gctx_hbm, out_hbm, p_hbm,
                    s1_ref, s2_ref, so_ref, sa_ref, small_ref, norm_ref, tok_grad, out_full, sg_hbm,
                    pbuf, stage, tokt, gts, gc, ga, gb, r1, r2, ro, rrow, rfb,
                    b1, b2, bo, ba, y1, y2, yo, ya, z1, z2, zo, za,
                    mine, ssend, srecv, cx, rx, tg, sm_send, sm_recv, sq, sqt, sqd,
                    insem, outsem, lsem, cs, cr, ys, yr, zs, zr, ts, tr, xs, xr, us, ur, ul, ms, mr, ns, nr):
    packs, heads, plen, _ = p_hbm.shape
    cols = wa_ref.shape[-1]
    hw = cols // heads
    scale = hw ** -0.5
    n = packs * heads
    blk = plen // 2
    half = out_hbm.shape[0]
    d = lax.axis_index("dp")
    t = lax.axis_index("tensor")
    z, y, x, c = d // 2, d % 2, t // 2, t % 2
    oy = 1 - y
    yn, xn, sib = (z * 2 + oy, t), (d, (1 - x) * 2 + c), (d, x * 2 + 1 - c)
    xd = (d, (1 - x) * 2 + 1 - c)
    zk = [(z + k) % 4 for k in range(4)]
    zp = [(zk[k] * 2 + y, t) for k in range(4)]
    dpp = [((d + m) % 8, t) for m in range(8)]
    part = y1.shape[1]
    masks = head_masks((plen, cols), heads, hw)

    def rc(src, dst, s, r, dev):
        return pltpu.make_async_remote_copy(src, dst, s, r, device_id=dev, device_id_type=MESH)

    peers = [xn, sib, xd] + dpp[1:]
    bar = pltpu.get_barrier_semaphore()
    for dev in peers:
        pl.semaphore_signal(bar, inc=1, device_id=dev, device_id_type=MESH)

    def p_in(i):
        return pltpu.make_async_copy(p_hbm.at[i // heads, i % heads], pbuf.at[i % 3], insem.at[i % 3])

    def s_out(i):
        return pltpu.make_async_copy(stage.at[i % 2], sg_hbm.at[i // heads, i % heads], outsem.at[i % 2])

    p_in(0).start()
    p_in(1).start()
    hrow = pl.ds(pl.multiple_of(c * half, half), half)
    gloc = pltpu.make_async_copy(gctx_hbm.at[0], gc.at[hrow, :], lsem.at[0])
    gloc.start()
    oloc = pltpu.make_async_copy(out_hbm, out_full.at[hrow, :], lsem.at[1])
    oloc.start()
    pl.semaphore_wait(bar, len(peers))
    sent = []

    def go(copy):
        copy.start()
        sent.append(copy)
        return copy

    gsib = go(rc(gctx_hbm.at[1], gc.at[hrow, :], cs.at[0], cr.at[0], sib))
    csib = [go(rc(src.at[1], dst, cs.at[i], cr.at[i], sib))
            for i, (src, dst) in enumerate(((g1_ref, r1), (g2_ref, r2), (go_ref, ro), (gfb_ref, rfb)), 1)]
    csib.append(go(rc(grow_ref, rrow, cs.at[5], cr.at[5], sib)))
    osib = go(rc(out_hbm, out_full.at[hrow, :], cs.at[6], cr.at[6], sib))

    own = (g1_ref, g2_ref, go_ref)
    sib_r = (r1, r2, ro)
    bufs = (b1, b2, bo, ba)
    yrec = (y1, y2, yo, ya)
    zrec = (z1, z2, zo, za)
    outs = (s1_ref, s2_ref, so_ref, sa_ref)

    def brow(dd):
        return pl.ds(pl.multiple_of(dd * part, 32), part)

    def bat(a, dd):
        return ba.at[:, brow(dd), :] if a == 3 else bufs[a].at[dd]

    def yc(a, k):
        return rc(bat(a, zk[k] * 2 + oy), yrec[a].at[k], ys.at[a, k], yr.at[a, k], yn)

    def zc(a, k):
        return rc(bat(a, zk[k] * 2 + y), zrec[a].at[k - 1], zs.at[a, k - 1], zr.at[a, k - 1], zp[k])

    def fold_core(a):
        def f():
            csib[a].wait_recv()

            @pl.loop(0, own[a].shape[1])
            def _(i):
                bufs[a][i] = (own[a][0, i].astype(F32) + sib_r[a][i].astype(F32)).astype(BF16)
            for k in (1, 2, 3, 0):
                go(yc(a, k))
        return f

    def load(a, dd):
        return ba[:, brow(dd), :] if a == 3 else bufs[a][dd]

    def fold_y(a, k):
        def f():
            yc(a, k).wait_recv()
            dd = zk[k] * 2 + y
            total = load(a, dd).astype(F32) + yrec[a][k].astype(F32)
            if k == 0:
                outs[a][...] = total
            else:
                low = total.astype(BF16)
                if a == 3:
                    ba[:, brow(dd), :] = low
                else:
                    bufs[a][dd] = low
                go(zc(a, k))
        return f

    def fold_z(a):
        def f():
            total = outs[a][...]
            for k in (1, 2, 3):
                zc(a, k).wait_recv()
                total = total + zrec[a][k - 1].astype(F32)
            outs[a][...] = total
        return f

    def tc(i):
        return rc(ssend.at[i], srecv.at[i], ts.at[i], tr.at[i], sib)

    def xc(i):
        return rc(cx.at[i], rx.at[i], xs.at[i], xr.at[i], xn)

    def trow(b):
        return pl.ds(b * blk, blk)

    def ucl(b):
        return pltpu.make_async_copy(tg.at[b % 3], tok_grad.at[trow(b), :], ul.at[b % 3])

    def ucr(b):
        return rc(tg.at[b % 3], tok_grad.at[trow(b), :], us.at[b % 3], ur.at[b % 3], sib)

    def part_ready(b, total):
        i = b % 3

        @pl.when(c == b // 3)
        def _():
            mine[i] = total

        @pl.when(c != b // 3)
        def _():
            ssend[i] = total.astype(BF16)
            tc(i).start()

    def part_chip(b):
        i = b % 3

        def f():
            @pl.when(c == b // 3)
            def _():
                tc(i).wait_recv()
                cx[i] = (mine[i] + srecv[i].astype(F32)).astype(BF16)
                xc(i).start()
        return f

    def part_done(b):
        i = b % 3

        def f():
            @pl.when(c == b // 3)
            def _():
                xc(i).wait_recv()
                tg[i] = gres1_ref[pl.ds(i * blk, blk), :] + (cx[i].astype(F32) + rx[i].astype(F32))
                ucl(b).start()
                ucr(b).start()
        return f

    steps = {0: [fold_core(0)], 1: [fold_core(1)], 2: [fold_core(2)],
             3: [part_chip(0), part_chip(1)], 4: [fold_y(0, 1)], 5: [fold_y(0, 2)],
             6: [part_chip(2), part_chip(3), fold_y(0, 3)], 7: [fold_y(0, 0)], 8: [part_done(0)]}

    for p in range(packs):
        tokt[:, p * plen:(p + 1) * plen] = tok_ref[pl.ds(p * plen, plen), :].T
    gloc.wait()
    gsib.wait_recv()
    for p in range(packs):
        rr = pl.ds(p * plen, plen)
        qt = q_ref[rr, :].T
        kt = k_ref[rr, :].T
        gct = gc[rr, :].T
        for h in range(heads):
            i = p * heads + h
            hh = slice(h * hw, (h + 1) * hw)
            p_in(i).wait()
            if i + 2 < n:
                p_in(i + 2).start()
            gm = jnp.where(masks[h], gc[rr, :], jnp.zeros((), BF16))
            pf = pbuf[i % 3]
            dp = dot_nt(gm, v_ref[rr, :])
            rd = jnp.sum(pf * dp, axis=-1, keepdims=True)
            ds = (pf * (dp - rd)).astype(BF16)
            if i >= 2:
                s_out(i - 2).wait()
            stage[i % 2] = ds.astype(F32)
            s_out(i).start()
            gts[0, hh, :] = dot_nt(kt[hh, :], ds) * scale
            gts[1, hh, :] = dot(qt[hh, :], ds)
            gts[2, hh, :] = dot(gct[hh, :], pf.astype(BF16))
            for f in steps.get(i, ()):
                f()
        total = None
        for j in range(3):
            gcol = gts[j].T.astype(BF16)
            xx = dot_nt(gcol, wa_ref[j])
            total = xx if total is None else total + xx
            yy = dot(tokt[:, p * plen:(p + 1) * plen], gcol)
            bb = jnp.sum(gcol.astype(F32), axis=0, keepdims=True)
            if p == 0:
                ga[j] = yy
                gb[j] = bb
            elif p < packs - 1:
                ga[j] += yy
                gb[j] += bb
            else:
                ba[j] = (ga[j] + yy).astype(BF16)
                gb[j] += bb
        part_ready(2 * p, total[:blk])
        part_ready(2 * p + 1, total[blk:])
    for k in (1, 2, 3, 0):
        go(yc(3, k))
    part_chip(4)()
    part_chip(5)()

    csib[3].wait_recv()
    csib[4].wait_recv()
    sm_send[0:8, :] = grow_ref[...] + rrow[...]
    sm_send[8:16, :] = jnp.zeros_like(sm_send[8:16, :])
    sm_send[8:9, :] = gfb_ref[0] + rfb[...]
    sm_send[9:10, 0:cols] = gb[0]
    sm_send[10:11, 0:cols] = gb[2]

    def mc(m):
        return rc(sm_send, sm_recv.at[d], ms.at[m - 1], mr.at[m - 1], dpp[m])

    for m in range(1, 8):
        go(mc(m))
    sm_recv[d] = sm_send[...]

    part_done(1)()
    part_done(2)()
    part_done(3)()
    fold_z(0)()
    for k in (1, 2, 3, 0):
        fold_y(1, k)()
    for k in (1, 2, 3, 0):
        fold_y(2, k)()
    for m in range(1, 8):
        mc(m).wait_recv()
    small = sm_recv[0]
    for i in range(1, 8):
        small = small + sm_recv[i]
    small_ref[...] = small
    part_done(4)()
    part_done(5)()
    fold_z(1)()
    fold_z(2)()
    for k in (1, 2, 3, 0):
        fold_y(3, k)()
    fold_z(3)()

    def square(v):
        return jnp.sum(v * v, keepdims=True)

    share = square(small[8:16, :])
    sh = square(s1_ref[...]) + square(s2_ref[...]) + square(so_ref[...])
    for j in range(3):
        sh = sh + square(sa_ref[j])
    sh = sh + share * (1.0 / 8.0)
    sq[...] = jnp.broadcast_to(sh, sq.shape)

    tp = [None, sib, xn, xd]

    def nc(m):
        return rc(sq, sqt.at[t], ns.at[m - 1], nr.at[m - 1], tp[m])

    for m in range(1, 4):
        go(nc(m))
    sqt[t] = sq[...]
    for m in range(1, 4):
        nc(m).wait_recv()
    tot = sqt[0] + sqt[1] + sqt[2] + sqt[3]
    sqd[8] = tot

    def nd(m):
        return rc(sqd.at[8], sqd.at[d], ns.at[2 + m], nr.at[2 + m], dpp[m])

    for m in range(1, 8):
        go(nd(m))
    sqd[d] = tot
    for m in range(1, 8):
        nd(m).wait_recv()
    tot = sqd[0]
    for i in range(1, 8):
        tot = tot + sqd[i]
    norm_ref[...] = jnp.sqrt(tot + square(small[0:8, :]))

    for b in range(6):
        i = b % 3

        @pl.when(c == b // 3)
        def _():
            xc(i).wait_send()
            ucl(b).wait()
            ucr(b).wait_send()

        @pl.when(c != b // 3)
        def _():
            tc(i).wait_send()
            ucr(b).wait_recv()
    s_out(n - 2).wait()
    s_out(n - 1).wait()
    oloc.wait()
    osib.wait_recv()
    for copy in sent:
        copy.wait_send()


def backward(tok, q, k, v, wa, gres1, grow, gfb, g1, g2, go, gctx, out_half, pf):
    packs, heads, plen, _ = pf.shape
    rows, cols = q.shape
    width = tok.shape[1]
    ff = g1.shape[-1]
    part = width // 8
    vm = pl.BlockSpec(memory_space=pltpu.VMEM)
    h = pl.BlockSpec(memory_space=pl.ANY)
    sds = jax.ShapeDtypeStruct
    V = pltpu.VMEM
    dma = pltpu.SemaphoreType.DMA
    g1, g2, go = (g.reshape(2, 8, part, g.shape[-1]) for g in (g1, g2, go))
    blk = plen // 2
    return pl.pallas_call(backward_kernel,
        out_shape=(sds((part, ff), F32), sds((part, ff), F32), sds((part, cols), F32), sds((3, part, cols), F32),
                   sds((16, width), F32), sds((8, 128), F32), sds((rows, width), F32), sds((rows, width), BF16), sds(pf.shape, F32)),
        in_specs=[vm] * 11 + [h] * 3, out_specs=(vm,) * 6 + (h,) * 3,
        scratch_shapes=[
            V((3, plen, plen), F32), V((2, plen, plen), F32), V((width, rows), BF16), V((3, cols, plen), F32),
            V((rows, cols), BF16), V((3, width, cols), F32), V((3, 1, cols), F32),
            V((8, part, ff), BF16), V((8, part, ff), BF16), V((8, part, cols), BF16), V((8, width), F32), V((1, ff), F32),
            V((8, part, ff), BF16), V((8, part, ff), BF16), V((8, part, cols), BF16), V((3, width, cols), BF16),
            V((4, part, ff), BF16), V((4, part, ff), BF16), V((4, part, cols), BF16), V((4, 3, part, cols), BF16),

            V((3, part, ff), BF16), V((3, part, ff), BF16), V((3, part, cols), BF16), V((3, 3, part, cols), BF16),
            V((3, blk, width), F32), V((3, blk, width), BF16), V((3, blk, width), BF16), V((3, blk, width), BF16), V((3, blk, width), BF16),
            V((3, blk, width), F32), V((16, width), F32), V((8, 16, width), F32), V((8, 128), F32), V((4, 8, 128), F32), V((9, 8, 128), F32),
            dma((3,)), dma((2,)), dma((2,)), dma((7,)), dma((7,)), dma((4, 4)), dma((4, 4)), dma((4, 3)), dma((4, 3)),
            dma((3,)), dma((3,)), dma((3,)), dma((3,)), dma((3,)), dma((3,)), dma((3,)), dma((7,)), dma((7,)), dma((10,)), dma((10,))],
        compiler_params=pltpu.CompilerParams(vmem_limit_bytes=60 << 20, collective_id=2, has_side_effects=True),
        name="attention_backward",
    )(tok, q, k, v, wa, gres1, grow, gfb, g1, g2, go, gctx, out_half, pf)


def adam_kernel(norm_ref, sa, s1, s2, so, small, wa, wo, w1, w2, wq, wf, wr, ma, mo, m1, m2, mq, mf, mr, va, vo, v1, v2, vq, vf, vr,
                *outs):
    factor = 1.0 / jnp.maximum(norm_ref[0:1, 0:1], 1.0)
    big_rate = wr.shape[-1] ** -0.5
    cols = wq.shape[-1]

    def update(g, w, m, v, rate, decay, o):
        g = g * factor
        mn = beta_one * m + (1.0 - beta_one) * g
        vn = beta_two * v + (1.0 - beta_two) * g * g
        corr = mn / (1.0 - beta_one ** STEP) / (jnp.sqrt(vn / (1.0 - beta_two ** STEP)) + adam_eps)
        new = w - rate * (corr + decay * w)
        o[0][...], o[1][...], o[2][...] = new, mn, vn
        if len(o) > 3:
            o[3][...] = new.astype(BF16)

    oa, oo, o1, o2 = (outs[i:i + 4] for i in range(0, 16, 4))
    oq, of, orr = (outs[i:i + 3] for i in (16, 19, 22))
    for j in range(3):
        update(sa[j], wa[j], ma[j], va[j], big_rate, weight_decay, [o.at[j] for o in oa])
    update(so[...].T, wo[...], mo[...], vo[...], big_rate, weight_decay, oo)
    update(s1[...], w1[...], m1[...], v1[...], big_rate, weight_decay, o1)
    update(s2[...].T, w2[...], m2[...], v2[...], big_rate, weight_decay, o2)
    update(small[9:11, 0:cols], wq[...], mq[...], vq[...], small_rate, 0.0, oq)
    update(small[8:9, :], wf[...], mf[...], vf[...], small_rate, 0.0, of)
    update(small[0:6, :], wr[...], mr[...], vr[...], small_rate, 0.0, orr)

def adam(norm, sa, s1, s2, so, small, ws, ms, vs):
    vm = pl.BlockSpec(memory_space=pltpu.VMEM)
    sds = jax.ShapeDtypeStruct
    shapes = []
    for i, w in enumerate(ws):
        shapes += [sds(w.shape, F32)] * 3 + ([sds(w.shape, BF16)] if i < 4 else [])
    return pl.pallas_call(adam_kernel, out_shape=tuple(shapes), in_specs=[vm] * 27, out_specs=(vm,) * 25,
        compiler_params=pltpu.CompilerParams(vmem_limit_bytes=60 << 20), name="adam",
    )(norm, sa, s1, s2, so, small, *ws, *ms, *vs)


def fast_layer(
    tokens, segment_ids, prev_scores, out_grad,
    attn_in_master, attn_out_master, ffn_in_master, ffn_out_master,
    attn_in_first, attn_out_first, ffn_in_first, ffn_out_first,
    attn_in_second, attn_out_second, ffn_in_second, ffn_out_second,
    qv_bias, ffn_bias, row_params,
    qv_bias_first, ffn_bias_first, row_params_first,
    qv_bias_second, ffn_bias_second, row_params_second,
):
    width = tokens.shape[1]
    seg_col = segment_ids.reshape(-1, 1)
    q, k, v, wa, fb, pf, w1, w2, wo, ctx = forward(
        tokens, segment_ids, seg_col, prev_scores, qv_bias, ffn_bias.reshape(1, -1),
        attn_in_master.astype(BF16), ffn_in_master.astype(BF16),
        ffn_out_master.astype(BF16).T, attn_out_master.astype(BF16).T, width)
    out_half, gres1, gctx, g1, g2, go, grow, gfb = ffn(
        ctx, tokens, out_grad, seg_col, row_params, fb, wo, w1, w2)
    s1, s2, so, sa, small, norm, tokens_grad, out_tokens, scores_grad = backward(
        tokens, q, k, v, wa, gres1, grow, gfb, g1, g2, go, gctx, out_half, pf)
    flat = lambda a: a.reshape(1, -1)
    new = adam(
        norm, sa, s1, s2, so, small,
        (attn_in_master, attn_out_master, ffn_in_master, ffn_out_master, qv_bias, flat(ffn_bias), row_params),
        (attn_in_first, attn_out_first, ffn_in_first, ffn_out_first, qv_bias_first, flat(ffn_bias_first), row_params_first),
        (attn_in_second, attn_out_second, ffn_in_second, ffn_out_second, qv_bias_second, flat(ffn_bias_second), row_params_second))
    big = [new[i:i + 4] for i in range(0, 16, 4)]
    small_new = [new[i:i + 3] for i in range(16, 25, 3)]
    small_new[1] = [a.reshape(-1) for a in small_new[1]]
    return (
        out_tokens, tokens_grad, scores_grad, norm[0, 0],
        *[b[0] for b in big], *[b[1] for b in big], *[b[2] for b in big], *[b[3] for b in big],
        *[s[0] for s in small_new], *[s[1] for s in small_new], *[s[2] for s in small_new],
    )


def solution(mesh):
    in_specs = (
        P("dp", None),
        P("dp", None),
        P("dp", "tensor", None, None),
        P("dp", None),
        P(None, "dp", "tensor"),
        P("tensor", "dp"),
        P("dp", "tensor"),
        P("tensor", "dp"),
        P(None, "dp", "tensor"),
        P("tensor", "dp"),
        P("dp", "tensor"),
        P("tensor", "dp"),
        P(None, "dp", "tensor"),
        P("tensor", "dp"),
        P("dp", "tensor"),
        P("tensor", "dp"),
        P(None, "tensor"),
        P("tensor"),
        P(),
        P(None, "tensor"),
        P("tensor"),
        P(),
        P(None, "tensor"),
        P("tensor"),
        P(),
    )
    out_specs = (
        P("dp", None),
        P("dp", None),
        P("dp", "tensor", None, None),
        P(),
        P(None, "dp", "tensor"),
        P("tensor", "dp"),
        P("dp", "tensor"),
        P("tensor", "dp"),
        P(None, "dp", "tensor"),
        P("tensor", "dp"),
        P("dp", "tensor"),
        P("tensor", "dp"),
        P(None, "dp", "tensor"),
        P("tensor", "dp"),
        P("dp", "tensor"),
        P("tensor", "dp"),
        P(None, "dp", "tensor"),
        P("tensor", "dp"),
        P("dp", "tensor"),
        P("tensor", "dp"),
        P(None, "tensor"),
        P("tensor"),
        P(),
        P(None, "tensor"),
        P("tensor"),
        P(),
        P(None, "tensor"),
        P("tensor"),
        P(),
    )
    layer = fast_layer if dict(mesh.shape) == {"dp": 8, "tensor": 4} else plain_layer
    return jax.shard_map(
        layer, mesh=mesh, in_specs=in_specs, out_specs=out_specs, check_vma=False
    )
```

```python
from functools import partial

import jax
import jax.numpy as jnp
from jax import lax
from jax.experimental import pallas as pl
from jax.experimental.pallas import tpu as pltpu
from jax.sharding import PartitionSpec as P

D = 768
STEP = 5


beta_one = 0.5
beta_two = 0.5
weight_decay = 0.01
adam_eps = 1e-08
norm_eps = 1e-06
small_rate = 0.5


def layer_norm(rows_in, gain_row, shift_row):
    row_mean = jnp.mean(rows_in, axis=-1, keepdims=True)
    centred = rows_in - row_mean
    spread = jnp.mean(centred * centred, axis=-1, keepdims=True)
    return centred * lax.rsqrt(spread + norm_eps) * gain_row + shift_row


def masked_scores(scale, query_heads, key_heads, prev_block, seg_ids):
    same_seq = seg_ids[:, None] == seg_ids[None, :]
    scores = jnp.einsum(
        "qhe,khe->hqk", query_heads, key_heads, preferred_element_type=jnp.float32
    ) * scale + prev_block.astype(jnp.float32)
    return jnp.where(same_seq[None], scores, -1000000000.0)


def attend(scale, pieces):
    query_heads, key_heads, value_heads, prev_block, seg_ids = pieces
    scores = masked_scores(scale, query_heads, key_heads, prev_block, seg_ids)
    row_top = jnp.max(scores, axis=-1, keepdims=True)
    expo = jnp.exp(scores - row_top)
    row_total = jnp.sum(expo, axis=-1, keepdims=True)
    weights_low = (expo / row_total).astype(jnp.bfloat16)
    context_heads = jnp.einsum(
        "hqk,khe->qhe", weights_low, value_heads, preferred_element_type=jnp.float32
    )
    return (context_heads.astype(jnp.bfloat16), row_top + jnp.log(row_total))


def attend_back(scale, pieces):
    query_heads, key_heads, value_heads, prev_block, seg_ids, row_lse, grad_heads = pieces
    scores = masked_scores(scale, query_heads, key_heads, prev_block, seg_ids)
    soft = jnp.exp(scores - row_lse)
    soft_low = soft.astype(jnp.bfloat16)
    grad_soft = jnp.einsum(
        "qhe,khe->hqk", grad_heads, value_heads, preferred_element_type=jnp.float32
    )
    row_dot = jnp.sum(soft * grad_soft, axis=-1, keepdims=True)
    score_grad = (soft * (grad_soft - row_dot)).astype(jnp.bfloat16)
    grad_query = (
        jnp.einsum("hqk,khe->qhe", score_grad, key_heads, preferred_element_type=jnp.float32)
        * scale
    ).astype(jnp.bfloat16)
    grad_key = (
        jnp.einsum("hqk,qhe->khe", score_grad, query_heads, preferred_element_type=jnp.float32)
        * scale
    ).astype(jnp.bfloat16)
    grad_value = jnp.einsum(
        "hqk,qhe->khe", soft_low, grad_heads, preferred_element_type=jnp.float32
    ).astype(jnp.bfloat16)
    return (grad_query, grad_key, grad_value, score_grad.astype(jnp.float32))


def adam_update(weight, gradient, first_moment, second_moment, decay_rate, learn_rate):
    first_new = beta_one * first_moment + (1.0 - beta_one) * gradient
    second_new = beta_two * second_moment + (1.0 - beta_two) * gradient * gradient
    corrected = (
        first_new
        / (1.0 - beta_one**STEP)
        / (jnp.sqrt(second_new / (1.0 - beta_two**STEP)) + adam_eps)
    )
    return (weight - learn_rate * (corrected + decay_rate * weight), first_new, second_new)


def plain_layer(
    tokens,
    segment_ids,
    prev_scores,
    out_grad,
    attn_in_master,
    attn_out_master,
    ffn_in_master,
    ffn_out_master,
    attn_in_first,
    attn_out_first,
    ffn_in_first,
    ffn_out_first,
    attn_in_second,
    attn_out_second,
    ffn_in_second,
    ffn_out_second,
    qv_bias,
    ffn_bias,
    row_params,
    qv_bias_first,
    ffn_bias_first,
    row_params_first,
    qv_bias_second,
    ffn_bias_second,
    row_params_second,
):
    attn_in, attn_out, ffn_in, ffn_out = (
        lax.all_gather(attn_in_master.astype(jnp.bfloat16), "dp", axis=1, tiled=True),
        lax.all_gather(attn_out_master.astype(jnp.bfloat16), "dp", axis=1, tiled=True),
        lax.all_gather(ffn_in_master.astype(jnp.bfloat16), "dp", axis=0, tiled=True),
        lax.all_gather(ffn_out_master.astype(jnp.bfloat16), "dp", axis=1, tiled=True),
    )
    pack_count, pack_len = segment_ids.shape
    head_count = prev_scores.shape[1]
    head_width = attn_in.shape[2] // head_count
    scale = head_width ** (-0.5)
    token_count = tokens.shape[0]
    dp_count = lax.axis_size("dp")
    tensor_count = lax.axis_size("tensor")

    def split_heads(matrix):
        return matrix.reshape(pack_count, pack_len, head_count, head_width)

    projected = jnp.einsum("td,cde->cte", tokens, attn_in, preferred_element_type=jnp.float32)
    query_rows = (projected[0] + qv_bias[0]).astype(jnp.bfloat16)
    key_rows = projected[1].astype(jnp.bfloat16)
    value_rows = (projected[2] + qv_bias[1]).astype(jnp.bfloat16)
    query_heads = split_heads(query_rows)
    key_heads = split_heads(key_rows)
    value_heads = split_heads(value_rows)
    context_heads, row_lse = lax.map(
        partial(attend, scale), (query_heads, key_heads, value_heads, prev_scores, segment_ids)
    )
    context = context_heads.reshape(token_count, -1)
    attn_partial = jnp.dot(context, attn_out, preferred_element_type=jnp.float32)
    live_whole = (segment_ids > 0).astype(jnp.float32).reshape(token_count, 1)
    rows_start = tokens.astype(jnp.float32)
    attended = lax.psum(attn_partial, "tensor") + row_params[2]
    cotangent = out_grad.astype(jnp.float32)
    residual_one = rows_start + attended
    normed, first_pull = jax.vjp(layer_norm, residual_one, row_params[0], row_params[3])
    normed_low = normed.astype(jnp.bfloat16)
    pre_act = jnp.dot(normed_low, ffn_in, preferred_element_type=jnp.float32) + ffn_bias
    activation, gelu_pull = jax.vjp(partial(jax.nn.gelu, approximate=False), pre_act)
    act_low = activation.astype(jnp.bfloat16)
    ffn_partial = jnp.dot(act_low, ffn_out, preferred_element_type=jnp.float32)
    ffn_output = lax.psum(ffn_partial, "tensor") + row_params[4]

    def final_norm(rows_in, gain_row, shift_row):
        return layer_norm(rows_in, gain_row, shift_row) * live_whole

    final_rows, second_pull = jax.vjp(final_norm, normed + ffn_output, row_params[1], row_params[5])
    final_low = final_rows.astype(jnp.bfloat16)
    grad_res_two, grad_gain_two, grad_shift_two = second_pull(cotangent)
    grad_ffn_low = grad_res_two.astype(jnp.bfloat16)
    grad_ffn_out_bias = jnp.sum(grad_ffn_low.astype(jnp.float32), axis=0)
    grad_ffn_out = jnp.einsum(
        "tf,td->fd", act_low, grad_ffn_low, preferred_element_type=jnp.float32
    )
    grad_act = jnp.einsum("td,fd->tf", grad_ffn_low, ffn_out, preferred_element_type=jnp.float32)
    (grad_pre,) = gelu_pull(grad_act)
    grad_pre_low = grad_pre.astype(jnp.bfloat16)
    grad_ffn_bias = jnp.sum(grad_pre_low.astype(jnp.float32), axis=0)
    grad_ffn_in = jnp.einsum(
        "td,tf->df", normed_low, grad_pre_low, preferred_element_type=jnp.float32
    )
    hidden_part = jnp.einsum("tf,df->td", grad_pre_low, ffn_in, preferred_element_type=jnp.float32)
    grad_normed = grad_res_two + lax.psum(hidden_part, "tensor")
    grad_res_one, grad_gain_one, grad_shift_one = first_pull(grad_normed)
    att_low = grad_res_one.astype(jnp.bfloat16)
    grad_att_bias = jnp.sum(att_low.astype(jnp.float32), axis=0)
    grad_attn_out = jnp.einsum("te,td->ed", context, att_low, preferred_element_type=jnp.float32)
    grad_context = jnp.einsum(
        "td,ed->te", att_low, attn_out, preferred_element_type=jnp.float32
    ).astype(jnp.bfloat16)
    grad_query, grad_key, grad_value, scores_grad = lax.map(
        partial(attend_back, scale),
        (
            query_heads,
            key_heads,
            value_heads,
            prev_scores,
            segment_ids,
            row_lse,
            split_heads(grad_context),
        ),
    )
    grad_proj = jnp.stack(
        [
            grad_query.reshape(token_count, -1),
            grad_key.reshape(token_count, -1),
            grad_value.reshape(token_count, -1),
        ]
    )
    grad_attn_in = jnp.einsum("td,cte->cde", tokens, grad_proj, preferred_element_type=jnp.float32)
    grad_qv_bias = jnp.stack(
        [
            jnp.sum(grad_proj[0].astype(jnp.float32), axis=0),
            jnp.sum(grad_proj[2].astype(jnp.float32), axis=0),
        ]
    )
    input_part = jnp.einsum("cte,cde->td", grad_proj, attn_in, preferred_element_type=jnp.float32)
    norm_stack = jnp.stack([grad_gain_one, grad_gain_two, grad_shift_one, grad_shift_two])
    tokens_grad = grad_res_one + lax.psum(input_part, "tensor")
    grad_rows = jnp.stack(
        [
            norm_stack[0],
            norm_stack[1],
            grad_att_bias,
            norm_stack[2],
            grad_ffn_out_bias,
            norm_stack[3],
        ]
    )
    summed = lax.psum(
        (
            grad_attn_in,
            grad_attn_out,
            grad_ffn_in,
            grad_ffn_out,
            grad_qv_bias,
            grad_ffn_bias,
            grad_rows,
        ),
        "dp",
    )
    dp_index = lax.axis_index("dp")

    def own_part(whole_grad, shard, along):
        extent = shard.shape[along]
        return lax.dynamic_slice_in_dim(whole_grad, dp_index * extent, extent, along)

    shares = (
        own_part(summed[0], attn_in_master, 1),
        own_part(summed[1], attn_out_master, 1),
        own_part(summed[2], ffn_in_master, 0),
        own_part(summed[3], ffn_out_master, 1),
    )
    small_sums = (summed[4], summed[5], summed[6])
    local_squares = jnp.float32(0.0)
    for share in shares:
        local_squares = local_squares + jnp.sum(share * share)
    local_squares = (
        local_squares
        + (jnp.sum(small_sums[0] * small_sums[0]) + jnp.sum(small_sums[1] * small_sums[1]))
        / dp_count
    )
    local_squares = local_squares + jnp.sum(small_sums[2] * small_sums[2]) / (
        dp_count * tensor_count
    )
    total_squares = lax.psum(local_squares, ("dp", "tensor"))
    grad_norm = jnp.sqrt(total_squares)
    factor = 1.0 / jnp.maximum(grad_norm, 1.0)
    olds = (
        attn_in_master,
        attn_out_master,
        ffn_in_master,
        ffn_out_master,
        qv_bias,
        ffn_bias,
        row_params,
    )
    firsts = (
        attn_in_first,
        attn_out_first,
        ffn_in_first,
        ffn_out_first,
        qv_bias_first,
        ffn_bias_first,
        row_params_first,
    )
    seconds = (
        attn_in_second,
        attn_out_second,
        ffn_in_second,
        ffn_out_second,
        qv_bias_second,
        ffn_bias_second,
        row_params_second,
    )
    gradients = (
        shares[0],
        shares[1],
        shares[2],
        shares[3],
        small_sums[0],
        small_sums[1],
        small_sums[2],
    )
    decays = (weight_decay, weight_decay, weight_decay, weight_decay, 0.0, 0.0, 0.0)
    big_rate = D ** (-0.5)
    rates = (big_rate, big_rate, big_rate, big_rate, small_rate, small_rate, small_rate)
    updated = [
        adam_update(
            olds[place],
            gradients[place] * factor,
            firsts[place],
            seconds[place],
            decays[place],
            rates[place],
        )
        for place in range(7)
    ]
    return (
        final_low,
        tokens_grad,
        scores_grad,
        grad_norm,
        updated[0][0],
        updated[1][0],
        updated[2][0],
        updated[3][0],
        updated[0][1],
        updated[1][1],
        updated[2][1],
        updated[3][1],
        updated[0][2],
        updated[1][2],
        updated[2][2],
        updated[3][2],
        updated[0][0].astype(jnp.bfloat16),
        updated[1][0].astype(jnp.bfloat16),
        updated[2][0].astype(jnp.bfloat16),
        updated[3][0].astype(jnp.bfloat16),
        updated[4][0],
        updated[5][0],
        updated[6][0],
        updated[4][1],
        updated[5][1],
        updated[6][1],
        updated[4][2],
        updated[5][2],
        updated[6][2],
    )


F32 = jnp.float32
BF16 = jnp.bfloat16
NT = (((1,), (1,)), ((), ()))
def dot(a, b):
    return jnp.dot(a, b, preferred_element_type=F32)
def dot_nt(a, b):
    return lax.dot_general(a, b, NT, preferred_element_type=F32)

def head_masks(shape, heads, hw):
    lane = lax.broadcasted_iota(jnp.int32, shape, len(shape) - 1)
    return [(lane >= h * hw) & (lane < (h + 1) * hw) for h in range(heads)]

def pick_heads(masks, parts):
    out = parts[-1]
    for m, p in zip(masks[:-1][::-1], parts[:-1][::-1]):
        out = jnp.where(m, p, out)
    return out

MESH = pl.DeviceIdType.MESH
ROWS = 256


def gelu_parts(pre):
    z = jnp.abs(pre)
    a = 1.0 + (0.3275911 * 0.7071067811865476) * z
    t = pl.reciprocal(a, approx=True)
    t = t * (2.0 - a * t)
    e = jnp.exp(-0.5 * pre * pre)
    half = (0.5 * t) * (0.254829592 + t * (-0.284496736 + t * (1.421413741 + t * (-1.453152027 + t * 1.061405429)))) * e
    cdf = jnp.where(pre >= 0.0, 1.0 - half, half)
    return pre * cdf, cdf + pre * (0.3989422804014327 * e)


def remote(src, dst, s, r, dev):
    return pltpu.make_async_remote_copy(src, dst, s, r, device_id=dev, device_id_type=MESH)


def forward_kernel(tok_ref, seg_ref, bias_ref, fbo_ref, rp_ref, wam_ref, w1m_ref, w2m_ref, wom_ref, prev_hbm, og_hbm,
                   q_ref, k_ref, v_ref, wa_ref, out_ref, gres1_ref, gctx_ref, gw1_ref, gw2_ref, gwo_ref, grow_ref, gfb_ref, p_hbm,
                   fb_ref, wo_ref, w1, w2, ctx4, ctx_loc, seg8, segt, lsem, psems,
                   zs, zr, ys, yr, xs, xr, x2s, x2r, cs, cr, os_, or_, fs, fr, xcs, xcr, dcs, dcr):
    packs, heads, plen, _ = prev_hbm.shape
    hw = wa_ref.shape[-1] // heads
    scale = hw ** -0.5
    d = lax.axis_index("dp")
    t = lax.axis_index("tensor")
    z, y, x, c = d // 2, d % 2, t // 2, t % 2
    oy = 1 - y
    ot = (1 - x) * 2 + c
    yn, xn, sib, xd = (z * 2 + oy, t), (d, ot), (d, x * 2 + 1 - c), (d, (1 - x) * 2 + 1 - c)
    zp = [None] + [(((z + k) % 4) * 2 + y, t) for k in (1, 2, 3)]
    line = [((z + 4 - j) % 4) * 2 + y for j in range(4)]
    oline = [((z + 4 - j) % 4) * 2 + oy for j in range(4)]
    part = wam_ref.shape[1]
    rows, width = tok_ref.shape
    half = rows // 2

    def drows(dd):
        return pl.ds(pl.multiple_of(dd * part, 32), part)

    def at(a, dd):
        if a == 0:
            return wa_ref.at[:, drows(dd), :]
        ref, slot = ((w1, t), (w2, t), (w1, ot), (wo_ref, t), (wo_ref, ot))[a - 1]
        return ref.at[slot, drows(dd), :]

    def zc(a, k):
        return remote(at(a, d), at(a, d), zs.at[a, k - 1], zr.at[a, k - 1], zp[k])

    def yc(a, j):
        return remote(at(a, line[j]), at(a, line[j]), ys.at[a, j], yr.at[a, j], yn)

    def x1c():
        return remote(at(1, d), at(1, d), xs.at[0], xr.at[0], xn)

    def x2c(j, yy):
        ref = at(2, oline[j] if yy else line[j])
        return remote(ref, ref, x2s.at[j, yy], x2r.at[j, yy], xn)

    def xoc():
        return remote(at(4, d), at(4, d), xs.at[1], xr.at[1], xn)

    def oc(i):
        src = wo_ref.at[ot if i else t]
        return remote(src, src, os_.at[i], or_.at[i], sib)

    def cc(a, i):
        ref = (w1, w2)[a - 1].at[ot if i else t]
        return remote(ref, ref, cs.at[a - 1, i], cr.at[a - 1, i], sib)

    peers = [yn, xn, sib, xd] + zp[1:]
    bar = pltpu.get_barrier_semaphore()
    for dev in peers:
        pl.semaphore_signal(bar, inc=1, device_id=dev, device_id_type=MESH)
    wa_ref[:, drows(d), :] = wam_ref[...].astype(BF16)
    wo_ref[t, drows(d), :] = wom_ref[...].T.astype(BF16)
    w1[t, drows(d), :] = w1m_ref[...].astype(BF16)
    w2[t, drows(d), :] = w2m_ref[...].astype(BF16)
    fb_ref[t] = fbo_ref[...].reshape(1, -1)
    pl.semaphore_wait(bar, len(peers))

    sent = []

    def go(make, *args):
        make(*args).start()
        sent.append((make, args))

    def line_out(a):
        for k in (1, 3, 2):
            go(zc, a, k)

    def out_y(a):
        go(yc, a, 0)

    def pass_y(a, k):
        zc(a, k).wait_recv()
        go(yc, a, k)

    def pass_w2(k):
        pass_y(2, k)
        go(x2c, k, 0)

    def pass_x(k):
        yc(2, k).wait_recv()
        go(x2c, k, 1)

    def pass_wo(k):
        pass_y(4, k)
        pass_y(5, k)

    def core_w1(i):
        for j in range(4):
            yc(3 if i else 1, j).wait_recv()
        go(cc, 1, i)

    def core_w2(i):
        if i:
            for j in range(4):
                x2c(j, 0).wait_recv()
                x2c(j, 1).wait_recv()
        go(cc, 2, i)

    def core_wo():
        for j in range(4):
            yc(4, j).wait_recv()
            yc(5, j).wait_recv()
        go(oc, 0)
        go(oc, 1)

    def run(*steps):
        for f, *args in steps:
            f(*args)

    run((line_out, 0), (go, xoc), (out_y, 4), (out_y, 0), (out_y, 2), (go, x1c))

    def fc(i):
        return remote(fb_ref.at[t], fb_ref.at[t], fs.at[i], fr.at[i], (sib, xn, xd)[i])

    for i in range(3):
        go(fc, i)

    blk = plen // 2

    def ctx_send(b):
        owner, i = b // 3, b % 3
        src = ctx_loc.at[pl.ds(b * blk, blk), :]
        dst = ctx4.at[t, pl.ds(i * blk, blk), :]
        far = (d, (1 - x) * 2 + owner)
        return (owner, remote(src, dst, xcs.at[i], xcr.at[i], far), remote(src, dst, xcs.at[3 + i], xcr.at[3 + i], far),
                remote(src, dst, dcs.at[i], dcr.at[i], sib))

    def attention(prev, stage, mask):
        def p_copy(i):
            return pltpu.make_async_copy(stage.at[i % 2], p_hbm.at[i // heads, i % heads], psems.at[i % 2])

        pcopy = pltpu.make_async_copy(prev_hbm, prev, lsem.at[0])
        pcopy.start()
        seg8[...] = jnp.zeros_like(seg8)
        seg8[0:packs, :] = seg_ref[...].astype(F32)
        segt[...] = seg8[...].T
        run((pass_y, 0, 3), (line_out, 2), (pass_y, 0, 1))
        xoc().wait_recv()
        run((line_out, 5), (pass_y, 0, 2), (pass_x, 0), (out_y, 1))
        x1c().wait_recv()
        line_out(4)
        for j in range(4):
            yc(0, j).wait_recv()
        run((out_y, 3), (pass_w2, 1), (out_y, 5), (go, x2c, 0, 0))
        steps = {0: [(line_out, 1), (pass_w2, 3)], 3: [(pass_w2, 2)], 4: [(pass_wo, 2)], 6: [(pass_wo, 1)]}
        masks = head_masks((plen, heads * hw), heads, hw)
        pcopy.wait()
        n = packs * heads
        for p in range(packs):
            rr = pl.ds(p * plen, plen)
            tok = tok_ref[rr, :]
            q_ref[rr, :] = ((dot(tok, wa_ref[0]) + bias_ref[0:1, :]).astype(BF16) * scale).astype(BF16)
            k_ref[rr, :] = dot(tok, wa_ref[1]).astype(BF16)
            v_ref[rr, :] = (dot(tok, wa_ref[2]) + bias_ref[1:2, :]).astype(BF16)
            mask[...] = jnp.where(segt[:, p:p + 1] == seg8[p:p + 1, :], 0.0, -1e9)
            outs = []
            for h in range(heads):
                i = p * heads + h
                qm = jnp.where(masks[h], q_ref[rr, :], jnp.zeros((), BF16))
                s = dot_nt(qm, k_ref[rr, :]) + (prev[p, h].astype(F32) + mask[...])
                m = jnp.max(s, axis=-1, keepdims=True)
                e = jnp.exp(s - m)
                pr = e * (1.0 / jnp.sum(e, axis=-1, keepdims=True))
                if i >= 2:
                    p_copy(i - 2).wait()
                stage[i % 2] = pr
                p_copy(i).start()
                outs.append(dot(pr.astype(BF16), v_ref[rr, :]))
                run(*steps.get(i, ()))
            ctx_loc[rr, :] = pick_heads(masks, outs).astype(BF16)
            for b in (2 * p, 2 * p + 1):
                owner, away, diag, near = ctx_send(b)

                @pl.when(c == owner)
                def _():
                    away.start()
                    ctx4[t, pl.ds(b % 3 * blk, blk), :] = ctx_loc[pl.ds(b * blk, blk), :]

                @pl.when(c != owner)
                def _():
                    diag.start()
                    near.start()
        p_copy(n - 2).wait()
        p_copy(n - 1).wait()

    pl.run_scoped(attention, pltpu.VMEM(prev_hbm.shape, BF16), pltpu.VMEM((2, plen, plen), F32), pltpu.VMEM((plen, plen), F32))

    def feed_forward(og_ref, live_ref, xhat, rstd, hid, hidt, act, dg, acc, gf, gft, gat):
        ogc = pltpu.make_async_copy(og_hbm.at[pl.ds(pl.multiple_of(c * half, half), half), :], og_ref, lsem.at[1])
        ogc.start()
        nr = half // ROWS
        gain1, gain2, bo, shift1, b2, shift2 = (rp_ref[i:i + 1, :] for i in range(6))
        inv = 1.0 / width

        def blkr(r):
            return pl.ds(pl.multiple_of(r * ROWS, ROWS), ROWS)

        run((pass_y, 1, 1), (pass_wo, 3), (pass_x, 3), (pass_y, 1, 3), (line_out, 3), (pass_x, 1), (pass_x, 2),
            (core_w2, 0), (pass_y, 1, 2), (core_wo,), (pass_y, 3, 1))
        for b in range(6):
            pack = b // 2
            col = (segt[b % 2 * blk:(b % 2 + 1) * blk, pack:pack + 1] > 0.0).astype(F32)

            @pl.when(c == b // 3)
            def _():
                live_ref[pl.ds(b % 3 * blk, blk), :] = col
        oc(0).wait_recv()
        oc(1).wait_recv()
        for b in range(6):
            owner, away, diag, near = ctx_send(b)

            @pl.when(c == owner)
            def _():
                away.wait_recv()
                diag.wait_recv()
                near.wait_recv()
        att = dot_nt(ctx4[0], wo_ref[0])
        for s in range(1, 4):
            att = att + dot_nt(ctx4[s], wo_ref[s])
        acc[...] = att
        run((core_w1, 0), (pass_y, 3, 3))

        @pl.loop(0, nr)
        def _(r):
            rr = blkr(r)
            trow = pl.ds(pl.multiple_of(c * half + r * ROWS, ROWS), ROWS)
            r1 = (tok_ref[trow, :].astype(F32) + bo) + acc[rr, :]
            mean = jnp.sum(r1, axis=-1, keepdims=True) * inv
            cen = r1 - mean
            rs = lax.rsqrt(jnp.sum(cen * cen, axis=-1, keepdims=True) * inv + norm_eps)
            xh = cen * rs
            xhat[rr, :] = xh
            rstd[rr, :] = rs
            h = (xh * gain1 + shift1).astype(BF16)
            hid[rr, :] = h
            hidt[:, rr] = h.T

        run((pass_y, 3, 2), (core_w2, 1))
        for i in range(3):
            fc(i).wait_recv()
        cc(1, 0).wait_recv()
        cc(2, 0).wait_recv()

        def unit_ff(s, out, first):
            pre = dot(hid[...], w1[s]) + fb_ref[s]
            a, g = gelu_parts(pre)
            act[s] = a.astype(BF16)
            dg[s] = g.astype(BF16)
            low = dot_nt(act[s], w2[s])
            if first:
                out[...] = low
            else:
                out[...] += low

        unit_ff(x * 2, acc, True)
        core_w1(1)
        unit_ff(x * 2 + 1, acc, False)
        cc(1, 1).wait_recv()
        cc(2, 1).wait_recv()
        unit_ff((1 - x) * 2, gres1_ref, True)
        unit_ff((1 - x) * 2 + 1, gres1_ref, False)

        grow_ref[...] = jnp.zeros_like(grow_ref)
        ogc.wait()

        @pl.loop(0, nr)
        def _(r):
            rr = blkr(r)
            r2 = (xhat[rr, :] * gain1 + shift1) + ((acc[rr, :] + gres1_ref[rr, :]) + b2)
            mean = jnp.sum(r2, axis=-1, keepdims=True) * inv
            cen = r2 - mean
            rs = lax.rsqrt(jnp.sum(cen * cen, axis=-1, keepdims=True) * inv + norm_eps)
            xh = cen * rs
            live = live_ref[rr, :]
            out_ref[rr, :] = (live * (xh * gain2 + shift2)).astype(BF16)
            g = og_ref[rr, :].astype(F32) * live
            grow_ref[1:2, :] += jnp.sum(g * xh, axis=0, keepdims=True)
            grow_ref[5:6, :] += jnp.sum(g, axis=0, keepdims=True)
            dx = g * gain2
            m1 = jnp.sum(dx, axis=-1, keepdims=True) * inv
            m2 = jnp.sum(dx * xh, axis=-1, keepdims=True) * inv
            gr = rs * (dx - m1 - xh * m2)
            acc[rr, :] = gr
            low = gr.astype(BF16)
            gf[rr, :] = low
            gft[:, rr] = low.T
            grow_ref[4:5, :] += jnp.sum(low.astype(F32), axis=0, keepdims=True)

        @pl.loop(0, 4)
        def _(s):
            dg[s] = (dot(gf[...], w2[s]) * dg[s].astype(F32)).astype(BF16)
            acc[...] += dot_nt(dg[s], w1[s])

        @pl.loop(0, 2)
        def _(i):
            s = t + i - 2 * i * c
            gp = dg[s]
            gw1_ref[i] = dot(hidt[...], gp).astype(BF16)
            gw2_ref[i] = dot(gft[...], act[s]).astype(BF16)
            gfb_ref[i] = jnp.sum(gp.astype(F32), axis=0, keepdims=True)

        @pl.loop(0, nr)
        def _(r):
            rr = blkr(r)
            xh = xhat[rr, :]
            g = acc[rr, :]
            grow_ref[0:1, :] += jnp.sum(g * xh, axis=0, keepdims=True)
            grow_ref[3:4, :] += jnp.sum(g, axis=0, keepdims=True)
            dx = g * gain1
            m1 = jnp.sum(dx, axis=-1, keepdims=True) * inv
            m2 = jnp.sum(dx * xh, axis=-1, keepdims=True) * inv
            gr = rstd[rr, :] * (dx - m1 - xh * m2)
            gres1_ref[rr, :] = gr
            low = gr.astype(BF16)
            gat[rr, :] = low
            gft[:, rr] = low.T
            grow_ref[2:3, :] += jnp.sum(low.astype(F32), axis=0, keepdims=True)

        for i in range(2):
            s = t + i - 2 * i * c
            gctx_ref[i] = dot(gat[...], wo_ref[s]).astype(BF16)
            gwo_ref[i] = dot(gft[...], ctx4[s]).astype(BF16)

    ff = w1.shape[-1]
    V = pltpu.VMEM
    pl.run_scoped(
        feed_forward, V((half, width), BF16), V((half, 1), F32), V((half, width), F32), V((half, 1), F32),
        V((half, width), BF16), V((width, half), BF16), V((4, half, ff), BF16), V((4, half, ff), BF16),
        V((half, width), F32), V((half, width), BF16), V((width, half), BF16), V((half, width), BF16))
    for b in range(6):
        owner, away, diag, near = ctx_send(b)

        @pl.when(c == owner)
        def _():
            away.wait_send()

        @pl.when(c != owner)
        def _():
            diag.wait_send()
            near.wait_send()
    for make, args in sent:
        make(*args).wait_send()


def forward(tok, seg, prev, og, rp, bias, fbo, wam, w1m, w2m, wom):
    packs, heads, plen, _ = prev.shape
    rows, width = tok.shape
    _, part, cols = wam.shape
    ff = w1m.shape[-1]
    v = pl.BlockSpec(memory_space=pltpu.VMEM)
    h = pl.BlockSpec(memory_space=pl.ANY)
    sds = jax.ShapeDtypeStruct
    V = pltpu.VMEM
    dma = pltpu.SemaphoreType.DMA
    half = rows // 2
    return pl.pallas_call(
        forward_kernel,
        out_shape=(sds((rows, cols), BF16),) * 3 + (
            sds((3, width, cols), BF16), sds((half, width), BF16), sds((half, width), F32), sds((2, half, cols), BF16),
            sds((2, width, ff), BF16), sds((2, width, ff), BF16), sds((2, width, cols), BF16),
            sds((8, width), F32), sds((2, 1, ff), F32), sds(prev.shape, F32)),
        in_specs=[v] * 9 + [h] * 2, out_specs=(v,) * 12 + (h,),
        scratch_shapes=[
            V((4, 1, ff), F32), V((4, width, cols), BF16), V((4, width, ff), BF16), V((4, width, ff), BF16),
            V((4, half, cols), BF16), V((rows, cols), BF16), V((8, plen), F32), V((plen, 8), F32), dma((2,)), dma((2,)),
            dma((6, 3)), dma((6, 3)), dma((6, 4)), dma((6, 4)), dma((2,)), dma((2,)),
            dma((4, 2)), dma((4, 2)), dma((2, 2)), dma((2, 2)), dma((3,)), dma((3,)), dma((3,)), dma((3,)),
            dma((6,)), dma((6,)), dma((3,)), dma((3,))],
        compiler_params=pltpu.CompilerParams(vmem_limit_bytes=62 << 20, collective_id=1, has_side_effects=True),
        name="forward_and_feed_forward",
    )(tok, seg, bias, fbo, rp, wam, w1m, w2m, wom, prev, og)


def backward_kernel(q_ref, k_ref, v_ref, wa_ref, grow_ref, gfb_ref, tok_hbm, gres1_hbm, g1_hbm, g2_hbm, go_hbm,
                    gctx_hbm, out_hbm, p_hbm,
                    s1_ref, s2_ref, so_ref, sa_ref, small_ref, norm_ref, tok_grad, out_sib, sg_hbm,
                    tok_ref, gres1_ref, o1, o2, oo, pbuf, stage, tokt, gts, gc, ga, gb, r1, r2, ro, rrow, rfb,
                    b1, b2, bo, ba, y1, y2, yo, ya, z1, z2, zo, za,
                    mine, ssend, srecv, cx, rx, tg, sm_send, sm_recv, sq, sqt, sqd,
                    insem, outsem, lsem, cs, cr, ys, yr, zs, zr, ts, tr, xs, xr, us, ur, ul, ms, mr, ns, nr):
    packs, heads, plen, _ = p_hbm.shape
    cols = wa_ref.shape[-1]
    hw = cols // heads
    scale = hw ** -0.5
    n = packs * heads
    blk = plen // 2
    half = out_hbm.shape[0]
    d = lax.axis_index("dp")
    t = lax.axis_index("tensor")
    z, y, x, c = d // 2, d % 2, t // 2, t % 2
    oy = 1 - y
    yn, xn, sib = (z * 2 + oy, t), (d, (1 - x) * 2 + c), (d, x * 2 + 1 - c)
    xd = (d, (1 - x) * 2 + 1 - c)
    zk = [(z + k) % 4 for k in range(4)]
    zp = [(zk[k] * 2 + y, t) for k in range(4)]
    dpp = [((d + m) % 8, t) for m in range(8)]
    part = y1.shape[1]
    masks = head_masks((plen, cols), heads, hw)

    def rc(src, dst, s, r, dev):
        return pltpu.make_async_remote_copy(src, dst, s, r, device_id=dev, device_id_type=MESH)

    peers = [xn, sib, xd] + dpp[1:]
    bar = pltpu.get_barrier_semaphore()
    for dev in peers:
        pl.semaphore_signal(bar, inc=1, device_id=dev, device_id_type=MESH)

    def p_in(i):
        return pltpu.make_async_copy(p_hbm.at[i // heads, i % heads], pbuf.at[i % 3], insem.at[i % 3])

    def s_out(i):
        return pltpu.make_async_copy(stage.at[i % 2], sg_hbm.at[i // heads, i % heads], outsem.at[i % 2])

    p_in(0).start()
    p_in(1).start()
    hrow = pl.ds(pl.multiple_of(c * half, half), half)
    gloc = pltpu.make_async_copy(gctx_hbm.at[0], gc.at[hrow, :], lsem.at[0])
    gloc.start()
    tcopy = pltpu.make_async_copy(tok_hbm, tok_ref, lsem.at[2])
    tcopy.start()
    ocopies = [pltpu.make_async_copy(src.at[0], dst, lsem.at[3 + i]) for i, (src, dst) in enumerate(((g1_hbm, o1), (g2_hbm, o2), (go_hbm, oo)))]
    rcopy = pltpu.make_async_copy(gres1_hbm, gres1_ref, lsem.at[6])
    for copy in ocopies:
        copy.start()
    rcopy.start()
    pl.semaphore_wait(bar, len(peers))
    sent = []

    def go(copy):
        copy.start()
        sent.append(copy)
        return copy

    gsib = go(rc(gctx_hbm.at[1], gc.at[hrow, :], cs.at[0], cr.at[0], sib))
    csib = [go(rc(src.at[1], dst, cs.at[i], cr.at[i], sib))
            for i, (src, dst) in enumerate(((g1_hbm, r1), (g2_hbm, r2), (go_hbm, ro), (gfb_ref, rfb)), 1)]
    csib.append(go(rc(grow_ref, rrow, cs.at[5], cr.at[5], sib)))
    osib = go(rc(out_hbm, out_sib, cs.at[6], cr.at[6], sib))

    own = (o1, o2, oo)
    sib_r = (r1, r2, ro)
    bufs = (b1, b2, bo, ba)
    yrec = (y1, y2, yo, ya)
    zrec = (z1, z2, zo, za)
    outs = (s1_ref, s2_ref, so_ref, sa_ref)

    def brow(dd):
        return pl.ds(pl.multiple_of(dd * part, 32), part)

    def bat(a, dd):
        return ba.at[:, brow(dd), :] if a == 3 else bufs[a].at[dd]

    def yc(a, k):
        return rc(bat(a, zk[k] * 2 + oy), yrec[a].at[k], ys.at[a, k], yr.at[a, k], yn)

    def zc(a, k):
        return rc(bat(a, zk[k] * 2 + y), zrec[a].at[k - 1], zs.at[a, k - 1], zr.at[a, k - 1], zp[k])

    def fold_core(a):
        def f():
            ocopies[a].wait()
            csib[a].wait_recv()

            @pl.loop(0, own[a].shape[0])
            def _(i):
                bufs[a][i] = (own[a][i].astype(F32) + sib_r[a][i].astype(F32)).astype(BF16)
            for k in (1, 2, 3, 0):
                go(yc(a, k))
        return f

    def load(a, dd):
        return ba[:, brow(dd), :] if a == 3 else bufs[a][dd]

    def fold_y(a, k):
        def f():
            yc(a, k).wait_recv()
            dd = zk[k] * 2 + y
            total = load(a, dd).astype(F32) + yrec[a][k].astype(F32)
            if k == 0:
                outs[a][...] = total
            else:
                low = total.astype(BF16)
                if a == 3:
                    ba[:, brow(dd), :] = low
                else:
                    bufs[a][dd] = low
                go(zc(a, k))
        return f

    def fold_z(a):
        def f():
            total = outs[a][...]
            for k in (1, 2, 3):
                zc(a, k).wait_recv()
                total = total + zrec[a][k - 1].astype(F32)
            outs[a][...] = total
        return f

    def tc(i):
        return rc(ssend.at[i], srecv.at[i], ts.at[i], tr.at[i], sib)

    def xc(i):
        return rc(cx.at[i], rx.at[i], xs.at[i], xr.at[i], xn)

    def trow(b):
        return pl.ds(b * blk, blk)

    def ucl(b):
        return pltpu.make_async_copy(tg.at[b % 3], tok_grad.at[trow(b), :], ul.at[b % 3])

    def ucr(b):
        return rc(tg.at[b % 3], tok_grad.at[trow(b), :], us.at[b % 3], ur.at[b % 3], sib)

    def part_ready(b, total):
        i = b % 3

        @pl.when(c == b // 3)
        def _():
            mine[i] = total

        @pl.when(c != b // 3)
        def _():
            ssend[i] = total.astype(BF16)
            tc(i).start()

    def part_chip(b):
        i = b % 3

        def f():
            @pl.when(c == b // 3)
            def _():
                tc(i).wait_recv()
                cx[i] = (mine[i] + srecv[i].astype(F32)).astype(BF16)
                xc(i).start()
        return f

    def part_done(b):
        i = b % 3

        def f():
            @pl.when(c == b // 3)
            def _():
                xc(i).wait_recv()
                tg[i] = gres1_ref[pl.ds(i * blk, blk), :] + (cx[i].astype(F32) + rx[i].astype(F32))
                ucl(b).start()
                ucr(b).start()
        return f

    steps = {0: [fold_core(0)], 1: [fold_core(1)], 2: [fold_core(2)],
             3: [part_chip(0), part_chip(1), fold_y(0, 1)], 4: [fold_y(0, 2)], 5: [fold_y(0, 3)],
             6: [part_chip(2), part_chip(3), fold_y(0, 0)], 7: [fold_y(1, 1)], 8: [fold_y(1, 2)]}

    tcopy.wait()
    for p in range(packs):
        tokt[:, p * plen:(p + 1) * plen] = tok_ref[pl.ds(p * plen, plen), :].T
    gloc.wait()
    gsib.wait_recv()
    for p in range(packs):
        rr = pl.ds(p * plen, plen)
        qt = q_ref[rr, :].T
        kt = k_ref[rr, :].T
        gct = gc[rr, :].T
        for h in range(heads):
            i = p * heads + h
            hh = slice(h * hw, (h + 1) * hw)
            p_in(i).wait()
            if i + 2 < n:
                p_in(i + 2).start()
            gm = jnp.where(masks[h], gc[rr, :], jnp.zeros((), BF16))
            pf = pbuf[i % 3]
            dp = dot_nt(gm, v_ref[rr, :])
            rd = jnp.sum(pf * dp, axis=-1, keepdims=True)
            ds = (pf * (dp - rd)).astype(BF16)
            if i >= 2:
                s_out(i - 2).wait()
            stage[i % 2] = ds
            s_out(i).start()
            gts[0, hh, :] = dot_nt(kt[hh, :], ds) * scale
            gts[1, hh, :] = dot(qt[hh, :], ds)
            gts[2, hh, :] = dot(gct[hh, :], pf.astype(BF16))
            for f in steps.get(i, ()):
                f()
        total = None
        for j in range(3):
            gcol = gts[j].T.astype(BF16)
            xx = dot_nt(gcol, wa_ref[j])
            total = xx if total is None else total + xx
            yy = dot(tokt[:, p * plen:(p + 1) * plen], gcol)
            bb = jnp.sum(gcol.astype(F32), axis=0, keepdims=True)
            if p == 0:
                ga[j] = yy
                gb[j] = bb
            elif p < packs - 1:
                ga[j] += yy
                gb[j] += bb
            else:
                ba[j] = (ga[j] + yy).astype(BF16)
                gb[j] += bb
        part_ready(2 * p, total[:blk])
        part_ready(2 * p + 1, total[blk:])
    for k in (1, 2, 3, 0):
        go(yc(3, k))
    rcopy.wait()
    part_chip(4)()
    part_chip(5)()

    csib[3].wait_recv()
    csib[4].wait_recv()
    sm_send[0:8, :] = grow_ref[...] + rrow[...]
    sm_send[8:16, :] = jnp.zeros_like(sm_send[8:16, :])
    sm_send[8:9, :] = gfb_ref[0] + rfb[...]
    sm_send[9:10, 0:cols] = gb[0]
    sm_send[10:11, 0:cols] = gb[2]

    def mc(m):
        return rc(sm_send, sm_recv.at[d], ms.at[m - 1], mr.at[m - 1], dpp[m])

    for m in range(1, 8):
        go(mc(m))
    sm_recv[d] = sm_send[...]

    fold_y(1, 3)()
    fold_y(1, 0)()
    part_done(0)()
    part_done(1)()
    for k in (1, 2, 3, 0):
        fold_y(2, k)()
    part_done(2)()
    part_done(3)()
    fold_z(0)()
    fold_y(3, 1)()
    part_done(4)()
    fold_y(3, 2)()
    part_done(5)()
    fold_y(3, 3)()
    fold_y(3, 0)()
    fold_z(1)()
    fold_z(2)()
    for m in range(1, 8):
        mc(m).wait_recv()
    small = sm_recv[0]
    for i in range(1, 8):
        small = small + sm_recv[i]
    small_ref[...] = small

    def square(v):
        return jnp.sum(v * v, keepdims=True)

    sh = square(small[8:16, :]) * (1.0 / 8.0)
    sh = sh + (square(s1_ref[...]) + square(s2_ref[...]) + square(so_ref[...]))
    fold_z(3)()
    for j in range(3):
        sh = sh + square(sa_ref[j])
    sq[...] = jnp.broadcast_to(sh, sq.shape)

    tp = [None, sib, xn, xd]

    def nc(m):
        return rc(sq, sqt.at[t], ns.at[m - 1], nr.at[m - 1], tp[m])

    for m in range(1, 4):
        go(nc(m))
    sqt[t] = sq[...]
    for m in range(1, 4):
        nc(m).wait_recv()
    tot = sqt[0] + sqt[1] + sqt[2] + sqt[3]
    sqd[8] = tot

    def nd(m):
        return rc(sqd.at[8], sqd.at[d], ns.at[2 + m], nr.at[2 + m], dpp[m])

    for m in range(1, 8):
        go(nd(m))
    sqd[d] = tot
    for m in range(1, 8):
        nd(m).wait_recv()
    tot = sqd[0]
    for i in range(1, 8):
        tot = tot + sqd[i]
    norm_ref[...] = jnp.sqrt(tot + square(small[0:8, :]))

    for b in range(6):
        i = b % 3

        @pl.when(c == b // 3)
        def _():
            xc(i).wait_send()
            ucl(b).wait()
            ucr(b).wait_send()

        @pl.when(c != b // 3)
        def _():
            tc(i).wait_send()
            ucr(b).wait_recv()
    s_out(n - 2).wait()
    s_out(n - 1).wait()
    osib.wait_recv()
    for copy in sent:
        copy.wait_send()


def backward(tok, q, k, v, wa, gres1, grow, gfb, g1, g2, go, gctx, out_half, pf):
    packs, heads, plen, _ = pf.shape
    rows, cols = q.shape
    width = tok.shape[1]
    ff = g1.shape[-1]
    part = width // 8
    vm = pl.BlockSpec(memory_space=pltpu.VMEM)
    h = pl.BlockSpec(memory_space=pl.ANY)
    sds = jax.ShapeDtypeStruct
    V = pltpu.VMEM
    dma = pltpu.SemaphoreType.DMA
    g1, g2, go = (g.reshape(2, 8, part, g.shape[-1]) for g in (g1, g2, go))
    blk = plen // 2
    return pl.pallas_call(backward_kernel,
        out_shape=(sds((part, ff), F32), sds((part, ff), F32), sds((part, cols), F32), sds((3, part, cols), F32),
                   sds((16, width), F32), sds((8, 128), F32), sds((rows, width), F32), sds((rows // 2, width), BF16), sds(pf.shape, BF16)),
        in_specs=[vm] * 6 + [h] * 8, out_specs=(vm,) * 6 + (h,) * 3,
        scratch_shapes=[
            V((rows, width), BF16), V((rows // 2, width), F32), V((8, part, ff), BF16), V((8, part, ff), BF16), V((8, part, cols), BF16),
            V((3, plen, plen), F32), V((2, plen, plen), BF16), V((width, rows), BF16), V((3, cols, plen), F32),
            V((rows, cols), BF16), V((3, width, cols), F32), V((3, 1, cols), F32),
            V((8, part, ff), BF16), V((8, part, ff), BF16), V((8, part, cols), BF16), V((8, width), F32), V((1, ff), F32),
            V((8, part, ff), BF16), V((8, part, ff), BF16), V((8, part, cols), BF16), V((3, width, cols), BF16),
            V((4, part, ff), BF16), V((4, part, ff), BF16), V((4, part, cols), BF16), V((4, 3, part, cols), BF16),

            V((3, part, ff), BF16), V((3, part, ff), BF16), V((3, part, cols), BF16), V((3, 3, part, cols), BF16),
            V((3, blk, width), F32), V((3, blk, width), BF16), V((3, blk, width), BF16), V((3, blk, width), BF16), V((3, blk, width), BF16),
            V((3, blk, width), F32), V((16, width), F32), V((8, 16, width), F32), V((8, 128), F32), V((4, 8, 128), F32), V((9, 8, 128), F32),
            dma((3,)), dma((2,)), dma((7,)), dma((7,)), dma((7,)), dma((4, 4)), dma((4, 4)), dma((4, 3)), dma((4, 3)),
            dma((3,)), dma((3,)), dma((3,)), dma((3,)), dma((3,)), dma((3,)), dma((3,)), dma((7,)), dma((7,)), dma((10,)), dma((10,))],
        compiler_params=pltpu.CompilerParams(vmem_limit_bytes=60 << 20, collective_id=2, has_side_effects=True),
        name="attention_backward",
    )(q, k, v, wa, grow, gfb, tok, gres1, g1, g2, go, gctx, out_half, pf)


def final_kernel(norm_ref, sa, s1, s2, so, small, wa, wo, w1, w2, wq, wf, wr, ma, mo, m1, m2, mq, mf, mr, va, vo, v1, v2, vq, vf, vr,
                 sg_hbm, tg_hbm, oh_hbm, os_hbm, *rest):
    outs, (sgo_hbm, tgo_hbm, oto_hbm, norm_out), (inb, outb, tbuf, obuf, insem, outsem, tis, tos, ois, oos) = rest[:25], rest[25:29], rest[29:]
    packs, heads = sg_hbm.shape[:2]
    n = packs * heads

    def s_in(i):
        return pltpu.make_async_copy(sg_hbm.at[i // heads, i % heads], inb.at[i % 3], insem.at[i % 3])

    def s_out(i):
        return pltpu.make_async_copy(outb.at[i % 3], sgo_hbm.at[i // heads, i % heads], outsem.at[i % 3])

    for i in range(3):
        s_in(i).start()
    c = lax.axis_index("tensor") % 2
    half = oh_hbm.shape[0]
    nt, trows = tis.shape[0], tbuf.shape[0] // tis.shape[0]
    tin = [pltpu.make_async_copy(tg_hbm.at[pl.ds(i * trows, trows), :], tbuf.at[pl.ds(i * trows, trows), :], tis.at[i]) for i in range(nt)]
    tout = [pltpu.make_async_copy(tbuf.at[pl.ds(i * trows, trows), :], tgo_hbm.at[pl.ds(i * trows, trows), :], tos.at[i]) for i in range(nt)]
    oin = [pltpu.make_async_copy(src, obuf.at[i], ois.at[i]) for i, src in enumerate((oh_hbm, os_hbm))]
    oout = [pltpu.make_async_copy(obuf.at[i], oto_hbm.at[pl.ds(pl.multiple_of(at * half, half), half), :], oos.at[i]) for i, at in enumerate((c, 1 - c))]
    moves = list(zip(oin + tin, oout + tout))
    for first, _ in moves:
        first.start()
    norm = norm_ref[0:1, 0:1]
    norm_out[...] = norm
    factor = 1.0 / jnp.maximum(norm, 1.0)
    big_rate = wr.shape[-1] ** -0.5
    cols = wq.shape[-1]

    def update(g, w, m, v, rate, decay, o):
        g = g * factor
        mn = beta_one * m + (1.0 - beta_one) * g
        vn = beta_two * v + (1.0 - beta_two) * g * g
        corr = mn / (1.0 - beta_one ** STEP) / (jnp.sqrt(vn / (1.0 - beta_two ** STEP)) + adam_eps)
        new = w - rate * (corr + decay * w)
        o[0][...], o[1][...], o[2][...] = new, mn, vn
        if len(o) > 3:
            o[3][...] = new.astype(BF16)

    oa, oo, o1, o2 = (outs[i:i + 4] for i in range(0, 16, 4))
    oq, of, orr = (outs[i:i + 3] for i in (16, 19, 22))

    def attn_in(j):
        return lambda: update(sa[j], wa[j], ma[j], va[j], big_rate, weight_decay, [o.at[j] for o in oa])

    def smalls():
        update(small[9:11, 0:cols], wq[...], mq[...], vq[...], small_rate, 0.0, oq)
        row = small[8:9, :] * factor
        mn = beta_one * mf[...].reshape(row.shape) + (1.0 - beta_one) * row
        vn = beta_two * vf[...].reshape(row.shape) + (1.0 - beta_two) * row * row
        corr = mn / (1.0 - beta_one ** STEP) / (jnp.sqrt(vn / (1.0 - beta_two ** STEP)) + adam_eps)
        new = wf[...].reshape(row.shape) - small_rate * corr
        for o, val in zip(of, (new, mn, vn)):
            o[...] = val.reshape(o.shape)
        update(small[0:6, :], wr[...], mr[...], vr[...], small_rate, 0.0, orr)

    work = [
        lambda: update(s1[...], w1[...], m1[...], v1[...], big_rate, weight_decay, o1),
        lambda: update(s2[...], w2[...], m2[...], v2[...], big_rate, weight_decay, o2),
        attn_in(0), attn_in(1), attn_in(2),
        lambda: update(so[...].T, wo[...], mo[...], vo[...], big_rate, weight_decay, oo),
        smalls]
    for i in range(n):
        s_in(i).wait()
        if i >= 3:
            s_out(i - 3).wait()
        outb[i % 3] = inb[i % 3].astype(F32)
        s_out(i).start()
        if i + 3 < n:
            s_in(i + 3).start()
        if i < len(work):
            work[i]()
        if i < len(moves):
            moves[i][0].wait()
            moves[i][1].start()
    for i in range(n - 3, n):
        s_out(i).wait()
    for _, last in moves:
        last.wait()


def finish(norm, sa, s1, s2, so, small, ws, ms, vs, sg, tg, oh, os):
    vm = pl.BlockSpec(memory_space=pltpu.VMEM)
    h = pl.BlockSpec(memory_space=pl.ANY)
    sds = jax.ShapeDtypeStruct
    shapes = []
    for i, w in enumerate(ws):
        shapes += [sds(w.shape, F32)] * 3 + ([sds(w.shape, BF16)] if i < 4 else [])
    shapes += [sds(sg.shape, F32), sds(tg.shape, F32), sds(tg.shape, BF16), sds((1, 1), F32)]
    plen = sg.shape[-1]
    dma = pltpu.SemaphoreType.DMA
    return pl.pallas_call(
        final_kernel, out_shape=tuple(shapes), in_specs=[vm] * 27 + [h] * 4, out_specs=(vm,) * 25 + (h,) * 3 + (vm,),
        scratch_shapes=[pltpu.VMEM((3, plen, plen), BF16), pltpu.VMEM((3, plen, plen), F32),
                        pltpu.VMEM(tg.shape, F32), pltpu.VMEM((2, *oh.shape), BF16),
                        dma((3,)), dma((3,)), dma((6,)), dma((6,)), dma((2,)), dma((2,))],
        compiler_params=pltpu.CompilerParams(vmem_limit_bytes=60 << 20), name="optimizer",
    )(norm, sa, s1, s2, so, small, *ws, *ms, *vs, sg, tg, oh, os)


def fast_layer(
    tokens, segment_ids, prev_scores, out_grad,
    attn_in_master, attn_out_master, ffn_in_master, ffn_out_master,
    attn_in_first, attn_out_first, ffn_in_first, ffn_out_first,
    attn_in_second, attn_out_second, ffn_in_second, ffn_out_second,
    qv_bias, ffn_bias, row_params,
    qv_bias_first, ffn_bias_first, row_params_first,
    qv_bias_second, ffn_bias_second, row_params_second,
):
    q, k, v, wa, out_half, gres1, gctx, g1, g2, go, grow, gfb, pf = forward(
        tokens, segment_ids, prev_scores, out_grad, row_params, qv_bias, ffn_bias,
        attn_in_master, ffn_in_master, ffn_out_master.T, attn_out_master)
    s1, s2, so, sa, small, norm, tokens_grad, out_other, scores_grad = backward(
        tokens, q, k, v, wa, gres1, grow, gfb, g1, g2, go, gctx, out_half, pf)
    new = finish(
        norm, sa, s1, s2, so, small,
        (attn_in_master, attn_out_master, ffn_in_master, ffn_out_master.T, qv_bias, ffn_bias, row_params),
        (attn_in_first, attn_out_first, ffn_in_first, ffn_out_first.T, qv_bias_first, ffn_bias_first, row_params_first),
        (attn_in_second, attn_out_second, ffn_in_second, ffn_out_second.T, qv_bias_second, ffn_bias_second, row_params_second),
        scores_grad, tokens_grad, out_half, out_other)
    big = [list(new[i:i + 4]) for i in range(0, 16, 4)]
    big[3] = [a.T for a in big[3]]
    small_new = [new[i:i + 3] for i in range(16, 25, 3)]
    return (
        new[27], new[26], new[25], new[28].reshape(()),
        *[b[0] for b in big], *[b[1] for b in big], *[b[2] for b in big], *[b[3] for b in big],
        *[s[0] for s in small_new], *[s[1] for s in small_new], *[s[2] for s in small_new],
    )


def solution(mesh):
    in_specs = (
        P("dp", None),
        P("dp", None),
        P("dp", "tensor", None, None),
        P("dp", None),
        P(None, "dp", "tensor"),
        P("tensor", "dp"),
        P("dp", "tensor"),
        P("tensor", "dp"),
        P(None, "dp", "tensor"),
        P("tensor", "dp"),
        P("dp", "tensor"),
        P("tensor", "dp"),
        P(None, "dp", "tensor"),
        P("tensor", "dp"),
        P("dp", "tensor"),
        P("tensor", "dp"),
        P(None, "tensor"),
        P("tensor"),
        P(),
        P(None, "tensor"),
        P("tensor"),
        P(),
        P(None, "tensor"),
        P("tensor"),
        P(),
    )
    out_specs = (
        P("dp", None),
        P("dp", None),
        P("dp", "tensor", None, None),
        P(),
        P(None, "dp", "tensor"),
        P("tensor", "dp"),
        P("dp", "tensor"),
        P("tensor", "dp"),
        P(None, "dp", "tensor"),
        P("tensor", "dp"),
        P("dp", "tensor"),
        P("tensor", "dp"),
        P(None, "dp", "tensor"),
        P("tensor", "dp"),
        P("dp", "tensor"),
        P("tensor", "dp"),
        P(None, "dp", "tensor"),
        P("tensor", "dp"),
        P("dp", "tensor"),
        P("tensor", "dp"),
        P(None, "tensor"),
        P("tensor"),
        P(),
        P(None, "tensor"),
        P("tensor"),
        P(),
        P(None, "tensor"),
        P("tensor"),
        P(),
    )
    layer = fast_layer if dict(mesh.shape) == {"dp": 8, "tensor": 4} else plain_layer
    return jax.shard_map(
        layer, mesh=mesh, in_specs=in_specs, out_specs=out_specs, check_vma=False
    )
```

```python
from functools import partial

import jax
import jax.numpy as jnp
from jax import lax
from jax.experimental import pallas as pl
from jax.experimental.pallas import tpu as pltpu
from jax.sharding import PartitionSpec as P

D = 768
STEP = 5


beta_one = 0.5
beta_two = 0.5
weight_decay = 0.01
adam_eps = 1e-08
norm_eps = 1e-06
small_rate = 0.5


def layer_norm(rows_in, gain_row, shift_row):
    row_mean = jnp.mean(rows_in, axis=-1, keepdims=True)
    centred = rows_in - row_mean
    spread = jnp.mean(centred * centred, axis=-1, keepdims=True)
    return centred * lax.rsqrt(spread + norm_eps) * gain_row + shift_row


def masked_scores(scale, query_heads, key_heads, prev_block, seg_ids):
    same_seq = seg_ids[:, None] == seg_ids[None, :]
    scores = jnp.einsum(
        "qhe,khe->hqk", query_heads, key_heads, preferred_element_type=jnp.float32
    ) * scale + prev_block.astype(jnp.float32)
    return jnp.where(same_seq[None], scores, -1000000000.0)


def attend(scale, pieces):
    query_heads, key_heads, value_heads, prev_block, seg_ids = pieces
    scores = masked_scores(scale, query_heads, key_heads, prev_block, seg_ids)
    row_top = jnp.max(scores, axis=-1, keepdims=True)
    expo = jnp.exp(scores - row_top)
    row_total = jnp.sum(expo, axis=-1, keepdims=True)
    weights_low = (expo / row_total).astype(jnp.bfloat16)
    context_heads = jnp.einsum(
        "hqk,khe->qhe", weights_low, value_heads, preferred_element_type=jnp.float32
    )
    return (context_heads.astype(jnp.bfloat16), row_top + jnp.log(row_total))


def attend_back(scale, pieces):
    query_heads, key_heads, value_heads, prev_block, seg_ids, row_lse, grad_heads = pieces
    scores = masked_scores(scale, query_heads, key_heads, prev_block, seg_ids)
    soft = jnp.exp(scores - row_lse)
    soft_low = soft.astype(jnp.bfloat16)
    grad_soft = jnp.einsum(
        "qhe,khe->hqk", grad_heads, value_heads, preferred_element_type=jnp.float32
    )
    row_dot = jnp.sum(soft * grad_soft, axis=-1, keepdims=True)
    score_grad = (soft * (grad_soft - row_dot)).astype(jnp.bfloat16)
    grad_query = (
        jnp.einsum("hqk,khe->qhe", score_grad, key_heads, preferred_element_type=jnp.float32)
        * scale
    ).astype(jnp.bfloat16)
    grad_key = (
        jnp.einsum("hqk,qhe->khe", score_grad, query_heads, preferred_element_type=jnp.float32)
        * scale
    ).astype(jnp.bfloat16)
    grad_value = jnp.einsum(
        "hqk,qhe->khe", soft_low, grad_heads, preferred_element_type=jnp.float32
    ).astype(jnp.bfloat16)
    return (grad_query, grad_key, grad_value, score_grad.astype(jnp.float32))


def adam_update(weight, gradient, first_moment, second_moment, decay_rate, learn_rate):
    first_new = beta_one * first_moment + (1.0 - beta_one) * gradient
    second_new = beta_two * second_moment + (1.0 - beta_two) * gradient * gradient
    corrected = (
        first_new
        / (1.0 - beta_one**STEP)
        / (jnp.sqrt(second_new / (1.0 - beta_two**STEP)) + adam_eps)
    )
    return (weight - learn_rate * (corrected + decay_rate * weight), first_new, second_new)


def plain_layer(
    tokens,
    segment_ids,
    prev_scores,
    out_grad,
    attn_in_master,
    attn_out_master,
    ffn_in_master,
    ffn_out_master,
    attn_in_first,
    attn_out_first,
    ffn_in_first,
    ffn_out_first,
    attn_in_second,
    attn_out_second,
    ffn_in_second,
    ffn_out_second,
    qv_bias,
    ffn_bias,
    row_params,
    qv_bias_first,
    ffn_bias_first,
    row_params_first,
    qv_bias_second,
    ffn_bias_second,
    row_params_second,
):
    attn_in, attn_out, ffn_in, ffn_out = (
        lax.all_gather(attn_in_master.astype(jnp.bfloat16), "dp", axis=1, tiled=True),
        lax.all_gather(attn_out_master.astype(jnp.bfloat16), "dp", axis=1, tiled=True),
        lax.all_gather(ffn_in_master.astype(jnp.bfloat16), "dp", axis=0, tiled=True),
        lax.all_gather(ffn_out_master.astype(jnp.bfloat16), "dp", axis=1, tiled=True),
    )
    pack_count, pack_len = segment_ids.shape
    head_count = prev_scores.shape[1]
    head_width = attn_in.shape[2] // head_count
    scale = head_width ** (-0.5)
    token_count = tokens.shape[0]
    dp_count = lax.axis_size("dp")
    tensor_count = lax.axis_size("tensor")

    def split_heads(matrix):
        return matrix.reshape(pack_count, pack_len, head_count, head_width)

    projected = jnp.einsum("td,cde->cte", tokens, attn_in, preferred_element_type=jnp.float32)
    query_rows = (projected[0] + qv_bias[0]).astype(jnp.bfloat16)
    key_rows = projected[1].astype(jnp.bfloat16)
    value_rows = (projected[2] + qv_bias[1]).astype(jnp.bfloat16)
    query_heads = split_heads(query_rows)
    key_heads = split_heads(key_rows)
    value_heads = split_heads(value_rows)
    context_heads, row_lse = lax.map(
        partial(attend, scale), (query_heads, key_heads, value_heads, prev_scores, segment_ids)
    )
    context = context_heads.reshape(token_count, -1)
    attn_partial = jnp.dot(context, attn_out, preferred_element_type=jnp.float32)
    live_whole = (segment_ids > 0).astype(jnp.float32).reshape(token_count, 1)
    rows_start = tokens.astype(jnp.float32)
    attended = lax.psum(attn_partial, "tensor") + row_params[2]
    cotangent = out_grad.astype(jnp.float32)
    residual_one = rows_start + attended
    normed, first_pull = jax.vjp(layer_norm, residual_one, row_params[0], row_params[3])
    normed_low = normed.astype(jnp.bfloat16)
    pre_act = jnp.dot(normed_low, ffn_in, preferred_element_type=jnp.float32) + ffn_bias
    activation, gelu_pull = jax.vjp(partial(jax.nn.gelu, approximate=False), pre_act)
    act_low = activation.astype(jnp.bfloat16)
    ffn_partial = jnp.dot(act_low, ffn_out, preferred_element_type=jnp.float32)
    ffn_output = lax.psum(ffn_partial, "tensor") + row_params[4]

    def final_norm(rows_in, gain_row, shift_row):
        return layer_norm(rows_in, gain_row, shift_row) * live_whole

    final_rows, second_pull = jax.vjp(final_norm, normed + ffn_output, row_params[1], row_params[5])
    final_low = final_rows.astype(jnp.bfloat16)
    grad_res_two, grad_gain_two, grad_shift_two = second_pull(cotangent)
    grad_ffn_low = grad_res_two.astype(jnp.bfloat16)
    grad_ffn_out_bias = jnp.sum(grad_ffn_low.astype(jnp.float32), axis=0)
    grad_ffn_out = jnp.einsum(
        "tf,td->fd", act_low, grad_ffn_low, preferred_element_type=jnp.float32
    )
    grad_act = jnp.einsum("td,fd->tf", grad_ffn_low, ffn_out, preferred_element_type=jnp.float32)
    (grad_pre,) = gelu_pull(grad_act)
    grad_pre_low = grad_pre.astype(jnp.bfloat16)
    grad_ffn_bias = jnp.sum(grad_pre_low.astype(jnp.float32), axis=0)
    grad_ffn_in = jnp.einsum(
        "td,tf->df", normed_low, grad_pre_low, preferred_element_type=jnp.float32
    )
    hidden_part = jnp.einsum("tf,df->td", grad_pre_low, ffn_in, preferred_element_type=jnp.float32)
    grad_normed = grad_res_two + lax.psum(hidden_part, "tensor")
    grad_res_one, grad_gain_one, grad_shift_one = first_pull(grad_normed)
    att_low = grad_res_one.astype(jnp.bfloat16)
    grad_att_bias = jnp.sum(att_low.astype(jnp.float32), axis=0)
    grad_attn_out = jnp.einsum("te,td->ed", context, att_low, preferred_element_type=jnp.float32)
    grad_context = jnp.einsum(
        "td,ed->te", att_low, attn_out, preferred_element_type=jnp.float32
    ).astype(jnp.bfloat16)
    grad_query, grad_key, grad_value, scores_grad = lax.map(
        partial(attend_back, scale),
        (
            query_heads,
            key_heads,
            value_heads,
            prev_scores,
            segment_ids,
            row_lse,
            split_heads(grad_context),
        ),
    )
    grad_proj = jnp.stack(
        [
            grad_query.reshape(token_count, -1),
            grad_key.reshape(token_count, -1),
            grad_value.reshape(token_count, -1),
        ]
    )
    grad_attn_in = jnp.einsum("td,cte->cde", tokens, grad_proj, preferred_element_type=jnp.float32)
    grad_qv_bias = jnp.stack(
        [
            jnp.sum(grad_proj[0].astype(jnp.float32), axis=0),
            jnp.sum(grad_proj[2].astype(jnp.float32), axis=0),
        ]
    )
    input_part = jnp.einsum("cte,cde->td", grad_proj, attn_in, preferred_element_type=jnp.float32)
    norm_stack = jnp.stack([grad_gain_one, grad_gain_two, grad_shift_one, grad_shift_two])
    tokens_grad = grad_res_one + lax.psum(input_part, "tensor")
    grad_rows = jnp.stack(
        [
            norm_stack[0],
            norm_stack[1],
            grad_att_bias,
            norm_stack[2],
            grad_ffn_out_bias,
            norm_stack[3],
        ]
    )
    summed = lax.psum(
        (
            grad_attn_in,
            grad_attn_out,
            grad_ffn_in,
            grad_ffn_out,
            grad_qv_bias,
            grad_ffn_bias,
            grad_rows,
        ),
        "dp",
    )
    dp_index = lax.axis_index("dp")

    def own_part(whole_grad, shard, along):
        extent = shard.shape[along]
        return lax.dynamic_slice_in_dim(whole_grad, dp_index * extent, extent, along)

    shares = (
        own_part(summed[0], attn_in_master, 1),
        own_part(summed[1], attn_out_master, 1),
        own_part(summed[2], ffn_in_master, 0),
        own_part(summed[3], ffn_out_master, 1),
    )
    small_sums = (summed[4], summed[5], summed[6])
    local_squares = jnp.float32(0.0)
    for share in shares:
        local_squares = local_squares + jnp.sum(share * share)
    local_squares = (
        local_squares
        + (jnp.sum(small_sums[0] * small_sums[0]) + jnp.sum(small_sums[1] * small_sums[1]))
        / dp_count
    )
    local_squares = local_squares + jnp.sum(small_sums[2] * small_sums[2]) / (
        dp_count * tensor_count
    )
    total_squares = lax.psum(local_squares, ("dp", "tensor"))
    grad_norm = jnp.sqrt(total_squares)
    factor = 1.0 / jnp.maximum(grad_norm, 1.0)
    olds = (
        attn_in_master,
        attn_out_master,
        ffn_in_master,
        ffn_out_master,
        qv_bias,
        ffn_bias,
        row_params,
    )
    firsts = (
        attn_in_first,
        attn_out_first,
        ffn_in_first,
        ffn_out_first,
        qv_bias_first,
        ffn_bias_first,
        row_params_first,
    )
    seconds = (
        attn_in_second,
        attn_out_second,
        ffn_in_second,
        ffn_out_second,
        qv_bias_second,
        ffn_bias_second,
        row_params_second,
    )
    gradients = (
        shares[0],
        shares[1],
        shares[2],
        shares[3],
        small_sums[0],
        small_sums[1],
        small_sums[2],
    )
    decays = (weight_decay, weight_decay, weight_decay, weight_decay, 0.0, 0.0, 0.0)
    big_rate = D ** (-0.5)
    rates = (big_rate, big_rate, big_rate, big_rate, small_rate, small_rate, small_rate)
    updated = [
        adam_update(
            olds[place],
            gradients[place] * factor,
            firsts[place],
            seconds[place],
            decays[place],
            rates[place],
        )
        for place in range(7)
    ]
    return (
        final_low,
        tokens_grad,
        scores_grad,
        grad_norm,
        updated[0][0],
        updated[1][0],
        updated[2][0],
        updated[3][0],
        updated[0][1],
        updated[1][1],
        updated[2][1],
        updated[3][1],
        updated[0][2],
        updated[1][2],
        updated[2][2],
        updated[3][2],
        updated[0][0].astype(jnp.bfloat16),
        updated[1][0].astype(jnp.bfloat16),
        updated[2][0].astype(jnp.bfloat16),
        updated[3][0].astype(jnp.bfloat16),
        updated[4][0],
        updated[5][0],
        updated[6][0],
        updated[4][1],
        updated[5][1],
        updated[6][1],
        updated[4][2],
        updated[5][2],
        updated[6][2],
    )


F32 = jnp.float32
BF16 = jnp.bfloat16
NT = (((1,), (1,)), ((), ()))
def dot(a, b):
    return jnp.dot(a, b, preferred_element_type=F32)
def dot_nt(a, b):
    return lax.dot_general(a, b, NT, preferred_element_type=F32)

def head_masks(shape, heads, hw):
    lane = lax.broadcasted_iota(jnp.int32, shape, len(shape) - 1)
    return [(lane >= h * hw) & (lane < (h + 1) * hw) for h in range(heads)]

def pick_heads(masks, parts):
    out = parts[-1]
    for m, p in zip(masks[:-1][::-1], parts[:-1][::-1]):
        out = jnp.where(m, p, out)
    return out

MESH = pl.DeviceIdType.MESH
ROWS = 256


def gelu_parts(pre):
    z = jnp.abs(pre)
    a = 1.0 + (0.3275911 * 0.7071067811865476) * z
    t = pl.reciprocal(a, approx=True)
    t = t * (2.0 - a * t)
    e = jnp.exp(-0.5 * pre * pre)
    half = (0.5 * t) * (0.254829592 + t * (-0.284496736 + t * (1.421413741 + t * (-1.453152027 + t * 1.061405429)))) * e
    cdf = jnp.where(pre >= 0.0, 1.0 - half, half)
    return pre * cdf, cdf + pre * (0.3989422804014327 * e)


def remote(src, dst, s, r, dev):
    return pltpu.make_async_remote_copy(src, dst, s, r, device_id=dev, device_id_type=MESH)


def layer_kernel(tok_ref, seg_ref, bias_ref, fbo_ref, rp_ref, wam_ref, w1m_ref, w2m_ref, wom_ref, prev_hbm, og_hbm,
                 s1_ref, s2_ref, so_ref, sa_ref, small_ref, norm_ref, tok_grad, out_full, sg_hbm, p_hbm,
                 q_ref, k_ref, v_ref, wa_ref, fb_ref, wo_ref, w1, w2, ctx4, ctx_loc, seg8, segt,
                 out_ref, gres1_ref, gctx, gw1, gw2, gwo, grow_ref, gfb_ref, ro, rrow, rfb, bo_buf, ba, yo, ya, zo, za,
                 sm_send, sm_recv, sq, sqt, sqd, lsem, psems,
                 zs, zr, ys, yr, xs, xr, x2s, x2r, cs, cr, os_, or_, fs, fr, xcs, xcr, dcs, dcr,
                 free, gs, gr_, es, er, hs, hr, ts, tr, xxs, xxr, us, ur, ul, ms, mr, ns, nr_, insem, outsem):
    packs, heads, plen, _ = prev_hbm.shape
    hw = wa_ref.shape[-1] // heads
    scale = hw ** -0.5
    d = lax.axis_index("dp")
    t = lax.axis_index("tensor")
    z, y, x, c = d // 2, d % 2, t // 2, t % 2
    oy = 1 - y
    ot = (1 - x) * 2 + c
    yn, xn, sib, xd = (z * 2 + oy, t), (d, ot), (d, x * 2 + 1 - c), (d, (1 - x) * 2 + 1 - c)
    zp = [None] + [(((z + k) % 4) * 2 + y, t) for k in (1, 2, 3)]
    line = [((z + 4 - j) % 4) * 2 + y for j in range(4)]
    oline = [((z + 4 - j) % 4) * 2 + oy for j in range(4)]
    part = wam_ref.shape[1]
    rows, width = tok_ref.shape
    half = rows // 2

    def drows(dd):
        return pl.ds(pl.multiple_of(dd * part, 32), part)

    def at(a, dd):
        if a == 0:
            return wa_ref.at[:, drows(dd), :]
        ref, slot = ((w1, t), (w2, t), (w1, ot), (wo_ref, t), (wo_ref, ot))[a - 1]
        return ref.at[slot, drows(dd), :]

    def zc(a, k):
        return remote(at(a, d), at(a, d), zs.at[a, k - 1], zr.at[a, k - 1], zp[k])

    def yc(a, j):
        return remote(at(a, line[j]), at(a, line[j]), ys.at[a, j], yr.at[a, j], yn)

    def x1c():
        return remote(at(1, d), at(1, d), xs.at[0], xr.at[0], xn)

    def x2c(j, yy):
        ref = at(2, oline[j] if yy else line[j])
        return remote(ref, ref, x2s.at[j, yy], x2r.at[j, yy], xn)

    def xoc():
        return remote(at(4, d), at(4, d), xs.at[1], xr.at[1], xn)

    def oc(i):
        src = wo_ref.at[ot if i else t]
        return remote(src, src, os_.at[i], or_.at[i], sib)

    def cc(a, i):
        ref = (w1, w2)[a - 1].at[ot if i else t]
        return remote(ref, ref, cs.at[a - 1, i], cr.at[a - 1, i], sib)

    dpp = [((d + i) % 8, t) for i in range(8)]
    peers = [xn, sib, xd] + dpp[1:]
    bar = pltpu.get_barrier_semaphore()
    for dev in peers:
        pl.semaphore_signal(bar, inc=1, device_id=dev, device_id_type=MESH)
    wa_ref[:, drows(d), :] = wam_ref[...].astype(BF16)
    wo_ref[t, drows(d), :] = wom_ref[...].T.astype(BF16)
    w1[t, drows(d), :] = w1m_ref[...].astype(BF16)
    w2[t, drows(d), :] = w2m_ref[...].astype(BF16)
    fb_ref[t] = fbo_ref[...].reshape(1, -1)
    pl.semaphore_wait(bar, len(peers))

    sent = []

    def go(make, *args):
        make(*args).start()
        sent.append((make, args))

    def line_out(a):
        for k in (1, 3, 2):
            go(zc, a, k)

    def out_y(a):
        go(yc, a, 0)

    def pass_y(a, k):
        zc(a, k).wait_recv()
        go(yc, a, k)

    def pass_w2(k):
        pass_y(2, k)
        go(x2c, k, 0)

    def pass_x(k):
        yc(2, k).wait_recv()
        go(x2c, k, 1)

    def pass_wo(k):
        pass_y(4, k)
        pass_y(5, k)

    def core_w1(i):
        for j in range(4):
            yc(3 if i else 1, j).wait_recv()
        go(cc, 1, i)

    def core_w2(i):
        if i:
            for j in range(4):
                x2c(j, 0).wait_recv()
                x2c(j, 1).wait_recv()
        go(cc, 2, i)

    def core_wo():
        for j in range(4):
            yc(4, j).wait_recv()
            yc(5, j).wait_recv()
        go(oc, 0)
        go(oc, 1)

    def run(*steps):
        for f, *args in steps:
            f(*args)

    run((line_out, 0), (go, xoc), (out_y, 4), (out_y, 0), (out_y, 2), (go, x1c))

    def fc(i):
        return remote(fb_ref.at[t], fb_ref.at[t], fs.at[i], fr.at[i], (sib, xn, xd)[i])

    for i in range(3):
        go(fc, i)

    blk = plen // 2

    def ctx_send(b):
        owner, i = b // 3, b % 3
        src = ctx_loc.at[pl.ds(b * blk, blk), :]
        dst = ctx4.at[t, pl.ds(i * blk, blk), :]
        far = (d, (1 - x) * 2 + owner)
        return (owner, remote(src, dst, xcs.at[i], xcr.at[i], far), remote(src, dst, xcs.at[3 + i], xcr.at[3 + i], far),
                remote(src, dst, dcs.at[i], dcr.at[i], sib))

    hrow = pl.ds(pl.multiple_of(c * half, half), half)
    zk = [(z + k) % 4 for k in range(4)]

    def core_grad(i):
        src, dst = ((gw1.at[1], w1.at[0]), (gw2.at[1], w1.at[1]), (gwo.at[1], ro), (gctx, ctx_loc.at[hrow, :]),
                    (gfb_ref.at[1], rfb), (grow_ref, rrow))[i]
        return remote(src, dst, hs.at[i], hr.at[i], sib)

    def out_send():
        return remote(out_ref, out_full.at[hrow, :], hs.at[6], hr.at[6], sib)

    def out_local():
        return pltpu.make_async_copy(out_ref, out_full.at[hrow, :], lsem.at[2])

    outs = (s1_ref, s2_ref, so_ref, sa_ref)

    def summed(a, dd):
        if a < 2:
            return w2.at[2 + a, drows(dd), :]
        return bo_buf.at[drows(dd), :] if a == 2 else ba.at[:, drows(dd), :]

    def from_y(a, k):
        return w1.at[2, pl.ds((4 * a + k) * part, part), :] if a < 2 else (yo, ya)[a - 2].at[k]

    def from_z(a, k):
        return w1.at[3, pl.ds((4 * a + k - 1) * part, part), :] if a < 2 else (zo, za)[a - 2].at[k - 1]

    def grad_y(a, k):
        return remote(summed(a, zk[k] * 2 + oy), from_y(a, k), gs.at[a, k], gr_.at[a, k], yn)

    def grad_z(a, k):
        return remote(summed(a, zk[k] * 2 + y), from_z(a, k), es.at[a, k - 1], er.at[a, k - 1], zp[k])

    def fold_core(a):
        mine, theirs = ((gw1, w1.at[0]), (gw2, w1.at[1]), (gwo, ro))[a]

        def f():
            core_grad(a).wait_recv()

            @pl.loop(0, width // part)
            def _(i):
                rr = drows(i)
                summed(a, i)[...] = (mine[0, rr, :].astype(F32) + theirs[rr, :].astype(F32)).astype(BF16)
            for k in (1, 2, 3, 0):
                go(grad_y, a, k)
        return f

    def fold_y(a, k):
        def f():
            grad_y(a, k).wait_recv()
            at_ = summed(a, zk[k] * 2 + y)
            total = at_[...].astype(F32) + from_y(a, k)[...].astype(F32)
            if k == 0:
                outs[a][...] = total
            else:
                at_[...] = total.astype(BF16)
                go(grad_z, a, k)
        return f

    def fold_z(a):
        def f():
            total = outs[a][...]
            for k in (1, 2, 3):
                grad_z(a, k).wait_recv()
                total = total + from_z(a, k)[...].astype(F32)
            outs[a][...] = total
        return f

    def settle():
        for b in range(6):
            owner, away, diag, near = ctx_send(b)

            @pl.when(c == owner)
            def _():
                away.wait_send()

            @pl.when(c != owner)
            def _():
                diag.wait_send()
                near.wait_send()
        early = [s for s in sent if s[0] is not out_send]
        late = [s for s in sent if s[0] is out_send]
        for make, args in early:
            make(*args).wait_send()
        sent[:] = late

    def attention(prev, stage, mask):
        def p_copy(i):
            return pltpu.make_async_copy(stage.at[i % 2], p_hbm.at[i // heads, i % heads], psems.at[i % 2])

        pcopy = pltpu.make_async_copy(prev_hbm, prev, lsem.at[0])
        pcopy.start()
        seg8[...] = jnp.zeros_like(seg8)
        seg8[0:packs, :] = seg_ref[...].astype(F32)
        segt[...] = seg8[...].T
        run((pass_y, 0, 3), (line_out, 2), (pass_y, 0, 1))
        xoc().wait_recv()
        run((line_out, 5), (pass_y, 0, 2), (pass_x, 0), (out_y, 1))
        x1c().wait_recv()
        line_out(4)
        for j in range(4):
            yc(0, j).wait_recv()
        run((out_y, 3), (pass_w2, 1), (out_y, 5), (go, x2c, 0, 0))
        steps = {0: [(line_out, 1), (pass_w2, 3)], 3: [(pass_w2, 2)], 4: [(pass_wo, 2)], 6: [(pass_wo, 1)]}
        masks = head_masks((plen, heads * hw), heads, hw)
        pcopy.wait()
        n = packs * heads
        for p in range(packs):
            rr = pl.ds(p * plen, plen)
            tok = tok_ref[rr, :]
            q_ref[rr, :] = ((dot(tok, wa_ref[0]) + bias_ref[0:1, :]).astype(BF16) * scale).astype(BF16)
            k_ref[rr, :] = dot(tok, wa_ref[1]).astype(BF16)
            v_ref[rr, :] = (dot(tok, wa_ref[2]) + bias_ref[1:2, :]).astype(BF16)
            mask[...] = jnp.where(segt[:, p:p + 1] == seg8[p:p + 1, :], 0.0, -1e9)
            outs = []
            for h in range(heads):
                i = p * heads + h
                qm = jnp.where(masks[h], q_ref[rr, :], jnp.zeros((), BF16))
                s = dot_nt(qm, k_ref[rr, :]) + (prev[p, h].astype(F32) + mask[...])
                m = jnp.max(s, axis=-1, keepdims=True)
                e = jnp.exp(s - m)
                pr = e * (1.0 / jnp.sum(e, axis=-1, keepdims=True))
                if i >= 2:
                    p_copy(i - 2).wait()
                stage[i % 2] = pr
                p_copy(i).start()
                outs.append(dot(pr.astype(BF16), v_ref[rr, :]))
                run(*steps.get(i, ()))
            ctx_loc[rr, :] = pick_heads(masks, outs).astype(BF16)
            for b in (2 * p, 2 * p + 1):
                owner, away, diag, near = ctx_send(b)

                @pl.when(c == owner)
                def _():
                    away.start()
                    ctx4[t, pl.ds(b % 3 * blk, blk), :] = ctx_loc[pl.ds(b * blk, blk), :]

                @pl.when(c != owner)
                def _():
                    diag.start()
                    near.start()
        p_copy(n - 2).wait()
        p_copy(n - 1).wait()

    pl.run_scoped(attention, pltpu.VMEM(prev_hbm.shape, BF16), pltpu.VMEM((2, plen, plen), F32), pltpu.VMEM((plen, plen), F32))

    def feed_forward(og_ref, live_ref, xhat, rstd, hid, hidt, act, dg, acc, gft):
        ogc = pltpu.make_async_copy(og_hbm.at[pl.ds(pl.multiple_of(c * half, half), half), :], og_ref, lsem.at[1])
        ogc.start()
        nr = half // ROWS
        gain1, gain2, bo, shift1, b2, shift2 = (rp_ref[i:i + 1, :] for i in range(6))
        inv = 1.0 / width

        def blkr(r):
            return pl.ds(pl.multiple_of(r * ROWS, ROWS), ROWS)

        run((pass_y, 1, 1), (pass_wo, 3), (pass_x, 3), (pass_y, 1, 3), (line_out, 3), (pass_x, 1), (pass_x, 2),
            (core_w2, 0), (pass_y, 1, 2), (core_wo,), (pass_y, 3, 1))
        for b in range(6):
            pack = b // 2
            col = (segt[b % 2 * blk:(b % 2 + 1) * blk, pack:pack + 1] > 0.0).astype(F32)

            @pl.when(c == b // 3)
            def _():
                live_ref[pl.ds(b % 3 * blk, blk), :] = col
        oc(0).wait_recv()
        oc(1).wait_recv()
        for b in range(6):
            owner, away, diag, near = ctx_send(b)

            @pl.when(c == owner)
            def _():
                away.wait_recv()
                diag.wait_recv()
                near.wait_recv()
        att = dot_nt(ctx4[0], wo_ref[0])
        for s in range(1, 4):
            att = att + dot_nt(ctx4[s], wo_ref[s])
        acc[...] = att
        run((core_w1, 0), (pass_y, 3, 3))

        @pl.loop(0, nr)
        def _(r):
            rr = blkr(r)
            trow = pl.ds(pl.multiple_of(c * half + r * ROWS, ROWS), ROWS)
            r1 = (tok_ref[trow, :].astype(F32) + bo) + acc[rr, :]
            mean = jnp.sum(r1, axis=-1, keepdims=True) * inv
            cen = r1 - mean
            rs = lax.rsqrt(jnp.sum(cen * cen, axis=-1, keepdims=True) * inv + norm_eps)
            xh = cen * rs
            xhat[rr, :] = xh
            rstd[rr, :] = rs
            h = (xh * gain1 + shift1).astype(BF16)
            hid[rr, :] = h
            hidt[:, rr] = h.T

        run((pass_y, 3, 2), (core_w2, 1))
        for i in range(3):
            fc(i).wait_recv()
        cc(1, 0).wait_recv()
        cc(2, 0).wait_recv()

        def unit_ff(s, out, first):
            pre = dot(hid[...], w1[s]) + fb_ref[s]
            a, g = gelu_parts(pre)
            act[s] = a.astype(BF16)
            dg[s] = g.astype(BF16)
            low = dot_nt(act[s], w2[s])
            if first:
                out[...] = low
            else:
                out[...] += low

        unit_ff(x * 2, acc, True)
        core_w1(1)
        unit_ff(x * 2 + 1, acc, False)
        cc(1, 1).wait_recv()
        cc(2, 1).wait_recv()
        unit_ff((1 - x) * 2, gres1_ref, True)
        unit_ff((1 - x) * 2 + 1, gres1_ref, False)

        grow_ref[...] = jnp.zeros_like(grow_ref)
        ogc.wait()

        @pl.loop(0, nr)
        def _(r):
            rr = blkr(r)
            r2 = (xhat[rr, :] * gain1 + shift1) + ((acc[rr, :] + gres1_ref[rr, :]) + b2)
            mean = jnp.sum(r2, axis=-1, keepdims=True) * inv
            cen = r2 - mean
            rs = lax.rsqrt(jnp.sum(cen * cen, axis=-1, keepdims=True) * inv + norm_eps)
            xh = cen * rs
            live = live_ref[rr, :]
            out_ref[rr, :] = (live * (xh * gain2 + shift2)).astype(BF16)
            g = og_ref[rr, :].astype(F32) * live
            grow_ref[1:2, :] += jnp.sum(g * xh, axis=0, keepdims=True)
            grow_ref[5:6, :] += jnp.sum(g, axis=0, keepdims=True)
            dx = g * gain2
            m1 = jnp.sum(dx, axis=-1, keepdims=True) * inv
            m2 = jnp.sum(dx * xh, axis=-1, keepdims=True) * inv
            gr = rs * (dx - m1 - xh * m2)
            acc[rr, :] = gr
            low = gr.astype(BF16)
            hid[rr, :] = low
            gft[:, rr] = low.T
            grow_ref[4:5, :] += jnp.sum(low.astype(F32), axis=0, keepdims=True)

        out_local().start()
        go(out_send)

        @pl.loop(0, 4)
        def _(s):
            dg[s] = (dot(hid[...], w2[s]) * dg[s].astype(F32)).astype(BF16)
            acc[...] += dot_nt(dg[s], w1[s])

        settle()
        for dev in (sib, xn, yn, zp[1], zp[2], zp[3]):
            pl.semaphore_signal(free, inc=1, device_id=dev, device_id_type=MESH)

        def weight_grads(i):
            s = x * 2 + (1 - c if i else c)
            gp = dg[s]
            gw1[i] = dot(hidt[...], gp).astype(BF16)
            gw2[i] = dot(gft[...], act[s]).astype(BF16)
            gfb_ref[i] = jnp.sum(gp.astype(F32), axis=0, keepdims=True)

        weight_grads(1)
        pl.semaphore_wait(free, 6)
        go(core_grad, 0)
        go(core_grad, 1)
        weight_grads(0)
        fold_core(0)()
        fold_core(1)()

        @pl.loop(0, nr)
        def _(r):
            rr = blkr(r)
            xh = xhat[rr, :]
            g = acc[rr, :]
            grow_ref[0:1, :] += jnp.sum(g * xh, axis=0, keepdims=True)
            grow_ref[3:4, :] += jnp.sum(g, axis=0, keepdims=True)
            dx = g * gain1
            m1 = jnp.sum(dx, axis=-1, keepdims=True) * inv
            m2 = jnp.sum(dx * xh, axis=-1, keepdims=True) * inv
            gr = rstd[rr, :] * (dx - m1 - xh * m2)
            gres1_ref[rr, :] = gr
            low = gr.astype(BF16)
            og_ref[rr, :] = low
            gft[:, rr] = low.T
            grow_ref[2:3, :] += jnp.sum(low.astype(F32), axis=0, keepdims=True)

        so_ = x * 2 + 1 - c
        gctx[...] = dot(og_ref[...], wo_ref[so_]).astype(BF16)
        go(core_grad, 3)
        ctx_loc[hrow, :] = dot(og_ref[...], wo_ref[t]).astype(BF16)
        gwo[1] = dot(gft[...], ctx4[so_]).astype(BF16)
        go(core_grad, 2)
        go(core_grad, 4)
        go(core_grad, 5)
        gwo[0] = dot(gft[...], ctx4[t]).astype(BF16)
        fold_y(0, 1)()

    ff = w1.shape[-1]
    V = pltpu.VMEM
    pl.run_scoped(
        feed_forward, V((half, width), BF16), V((half, 1), F32), V((half, width), F32), V((half, 1), F32),
        V((half, width), BF16), V((width, half), BF16), V((4, half, ff), BF16), V((4, half, ff), BF16),
        V((half, width), F32), V((width, half), BF16))
    def attention_back(pbuf, stage, tokt, gts, ga, gb, mine, ssend, cx, tg):
        def tc(i):
            return remote(ssend.at[i], w2.at[0, pl.ds(i * blk, blk), :], ts.at[i], tr.at[i], sib)

        def xc(i):
            return remote(cx.at[i], w2.at[1, pl.ds(i * blk, blk), :], xxs.at[i], xxr.at[i], xn)

        def trow(b):
            return pl.ds(b * blk, blk)

        def ucl(b):
            return pltpu.make_async_copy(tg.at[b % 3], tok_grad.at[trow(b), :], ul.at[b % 3])

        def ucr(b):
            return remote(tg.at[b % 3], tok_grad.at[trow(b), :], us.at[b % 3], ur.at[b % 3], sib)

        def part_ready(b, total):
            i = b % 3

            @pl.when(c == b // 3)
            def _():
                mine[i] = total

            @pl.when(c != b // 3)
            def _():
                ssend[i] = total.astype(BF16)
                tc(i).start()

        def part_chip(b):
            i = b % 3

            def f():
                @pl.when(c == b // 3)
                def _():
                    tc(i).wait_recv()
                    cx[i] = (mine[i] + w2[0, pl.ds(i * blk, blk), :].astype(F32)).astype(BF16)
                    xc(i).start()
            return f

        def part_done(b):
            i = b % 3

            def f():
                @pl.when(c == b // 3)
                def _():
                    xc(i).wait_recv()
                    tg[i] = gres1_ref[pl.ds(i * blk, blk), :] + (cx[i].astype(F32) + w2[1, pl.ds(i * blk, blk), :].astype(F32))
                    ucl(b).start()
                    ucr(b).start()
            return f

        cols = wa_ref.shape[-1]
        n = packs * heads
        masks = head_masks((plen, cols), heads, hw)
        steps = {0: [fold_core(2)], 1: [fold_y(0, 2)], 2: [fold_y(0, 3)], 3: [fold_y(0, 0), part_chip(0), part_chip(1)], 4: [fold_y(1, 1)],
                 5: [fold_y(1, 2)], 6: [part_chip(2), part_chip(3)], 7: [fold_y(1, 3)], 8: [fold_y(1, 0)]}

        def p_in(i):
            return pltpu.make_async_copy(p_hbm.at[i // heads, i % heads], pbuf.at[i % 3], insem.at[i % 3])

        def s_out(i):
            return pltpu.make_async_copy(stage.at[i % 2], sg_hbm.at[i // heads, i % heads], outsem.at[i % 2])

        p_in(0).start()
        p_in(1).start()
        for p in range(packs):
            tokt[:, p * plen:(p + 1) * plen] = tok_ref[pl.ds(p * plen, plen), :].T
        core_grad(3).wait_recv()
        for p in range(packs):
            rr = pl.ds(p * plen, plen)
            qt = q_ref[rr, :].T
            kt = k_ref[rr, :].T
            gct = ctx_loc[rr, :].T
            for h in range(heads):
                i = p * heads + h
                hh = slice(h * hw, (h + 1) * hw)
                p_in(i).wait()
                if i + 2 < n:
                    p_in(i + 2).start()
                gm = jnp.where(masks[h], ctx_loc[rr, :], jnp.zeros((), BF16))
                pf = pbuf[i % 3]
                dp = dot_nt(gm, v_ref[rr, :])
                rd = jnp.sum(pf * dp, axis=-1, keepdims=True)
                ds = (pf * (dp - rd)).astype(BF16)
                if i >= 2:
                    s_out(i - 2).wait()
                stage[i % 2] = ds
                s_out(i).start()
                gts[0, hh, :] = dot_nt(kt[hh, :], ds) * scale
                gts[1, hh, :] = dot(qt[hh, :], ds)
                gts[2, hh, :] = dot(gct[hh, :], pf.astype(BF16))
                for f in steps.get(i, ()):
                    f()
            total = None
            for j in range(3):
                gcol = gts[j].T.astype(BF16)
                xx = dot_nt(gcol, wa_ref[j])
                total = xx if total is None else total + xx
                yy = dot(tokt[:, p * plen:(p + 1) * plen], gcol)
                bb = jnp.sum(gcol.astype(F32), axis=0, keepdims=True)
                if p == 0:
                    ga[j] = yy
                    gb[j] = bb
                elif p < packs - 1:
                    ga[j] += yy
                    gb[j] += bb
                else:
                    ba[j] = (ga[j] + yy).astype(BF16)
                    gb[j] += bb
            part_ready(2 * p, total[:blk])
            part_ready(2 * p + 1, total[blk:])
        for k in (1, 2, 3, 0):
            go(grad_y, 3, k)
        part_chip(4)()
        part_chip(5)()

        core_grad(4).wait_recv()
        core_grad(5).wait_recv()
        sm_send[0:8, :] = grow_ref[...] + rrow[...]
        sm_send[8:16, :] = jnp.zeros_like(sm_send[8:16, :])
        sm_send[8:9, :] = gfb_ref[0] + rfb[...]
        sm_send[9:10, 0:cols] = gb[0]
        sm_send[10:11, 0:cols] = gb[2]

        def mc(m):
            return remote(sm_send, sm_recv.at[d], ms.at[m - 1], mr.at[m - 1], dpp[m])

        for m in range(1, 8):
            go(mc, m)
        sm_recv[d] = sm_send[...]

        for k in (1, 2, 3, 0):
            fold_y(2, k)()
        part_done(0)()
        part_done(1)()
        fold_y(3, 1)()
        part_done(2)()
        fold_y(3, 2)()
        part_done(3)()
        fold_y(3, 3)()
        fold_z(0)()
        fold_y(3, 0)()
        part_done(4)()
        fold_z(1)()
        part_done(5)()
        fold_z(2)()
        for m in range(1, 8):
            mc(m).wait_recv()
        small = sm_recv[0]
        for i in range(1, 8):
            small = small + sm_recv[i]
        small_ref[...] = small

        def square(v):
            return jnp.sum(v * v, keepdims=True)

        sh = square(small[8:16, :]) * (1.0 / 8.0)
        sh = sh + (square(s1_ref[...]) + square(s2_ref[...]) + square(so_ref[...]))
        fold_z(3)()
        for j in range(3):
            sh = sh + square(sa_ref[j])
        sq[...] = jnp.broadcast_to(sh, sq.shape)

        tp = [None, sib, xn, xd]

        def nc(m):
            return remote(sq, sqt.at[t], ns.at[m - 1], nr_.at[m - 1], tp[m])

        for m in range(1, 4):
            go(nc, m)
        sqt[t] = sq[...]
        for m in range(1, 4):
            nc(m).wait_recv()
        tot = sqt[0] + sqt[1] + sqt[2] + sqt[3]
        sqd[8] = tot

        def nd(m):
            return remote(sqd.at[8], sqd.at[d], ns.at[2 + m], nr_.at[2 + m], dpp[m])

        for m in range(1, 8):
            go(nd, m)
        sqd[d] = tot
        for m in range(1, 8):
            nd(m).wait_recv()
        tot = sqd[0]
        for i in range(1, 8):
            tot = tot + sqd[i]
        norm_ref[...] = jnp.sqrt(tot + square(small[0:8, :]))

        for b in range(6):
            i = b % 3

            @pl.when(c == b // 3)
            def _():
                xc(i).wait_send()
                ucl(b).wait()
                ucr(b).wait_send()

            @pl.when(c != b // 3)
            def _():
                tc(i).wait_send()
                ucr(b).wait_recv()
        s_out(n - 2).wait()
        s_out(n - 1).wait()
        out_local().wait()
        out_send().wait_recv()
        for make, args in sent:
            make(*args).wait_send()


    cols = wa_ref.shape[-1]
    pl.run_scoped(
        attention_back, V((3, plen, plen), F32), V((2, plen, plen), BF16), V((width, rows), BF16), V((3, cols, plen), F32),
        V((3, width, cols), F32), V((3, 1, cols), F32), V((3, blk, width), F32), V((3, blk, width), BF16), V((3, blk, width), BF16),
        V((3, blk, width), F32))


def layer(tok, seg, prev, og, rp, bias, fbo, wam, w1m, w2m, wom):
    packs, heads, plen, _ = prev.shape
    rows, width = tok.shape
    _, part, cols = wam.shape
    ff = w1m.shape[-1]
    v = pl.BlockSpec(memory_space=pltpu.VMEM)
    h = pl.BlockSpec(memory_space=pl.ANY)
    sds = jax.ShapeDtypeStruct
    V = pltpu.VMEM
    dma = pltpu.SemaphoreType.DMA
    half = rows // 2
    return pl.pallas_call(
        layer_kernel,
        out_shape=(sds((part, ff), F32), sds((part, ff), F32), sds((part, cols), F32), sds((3, part, cols), F32),
                   sds((16, width), F32), sds((8, 128), F32), sds((rows, width), F32), sds((rows, width), BF16),
                   sds(prev.shape, BF16), sds(prev.shape, F32)),
        in_specs=[v] * 9 + [h] * 2, out_specs=(v,) * 6 + (h,) * 4,
        scratch_shapes=[
            V((rows, cols), BF16), V((rows, cols), BF16), V((rows, cols), BF16), V((3, width, cols), BF16),
            V((4, 1, ff), F32), V((4, width, cols), BF16), V((4, width, ff), BF16), V((4, width, ff), BF16),
            V((4, half, cols), BF16), V((rows, cols), BF16), V((8, plen), F32), V((plen, 8), F32),
            V((half, width), BF16), V((half, width), F32), V((half, cols), BF16), V((2, width, ff), BF16), V((2, width, ff), BF16),
            V((2, width, cols), BF16), V((8, width), F32), V((2, 1, ff), F32),
            V((width, cols), BF16), V((8, width), F32), V((1, ff), F32), V((width, cols), BF16), V((3, width, cols), BF16),
            V((4, part, cols), BF16), V((4, 3, part, cols), BF16), V((3, part, cols), BF16), V((3, 3, part, cols), BF16),
            V((16, width), F32), V((8, 16, width), F32), V((8, 128), F32), V((4, 8, 128), F32), V((9, 8, 128), F32), dma((3,)), dma((2,)),
            dma((6, 3)), dma((6, 3)), dma((6, 4)), dma((6, 4)), dma((2,)), dma((2,)),
            dma((4, 2)), dma((4, 2)), dma((2, 2)), dma((2, 2)), dma((3,)), dma((3,)), dma((3,)), dma((3,)),
            dma((6,)), dma((6,)), dma((3,)), dma((3,)),
            pltpu.SemaphoreType.REGULAR, dma((4, 4)), dma((4, 4)), dma((4, 3)), dma((4, 3)), dma((7,)), dma((7,)),
            dma((3,)), dma((3,)), dma((3,)), dma((3,)), dma((3,)), dma((3,)), dma((3,)), dma((7,)), dma((7,)), dma((10,)), dma((10,)),
            dma((3,)), dma((2,))],
        compiler_params=pltpu.CompilerParams(vmem_limit_bytes=63 << 20, collective_id=1, has_side_effects=True),
        name="layer",
    )(tok, seg, bias, fbo, rp, wam, w1m, w2m, wom, prev, og)


def final_kernel(norm_ref, sa, s1, s2, so, small, wa, wo, w1, w2, wq, wf, wr, ma, mo, m1, m2, mq, mf, mr, va, vo, v1, v2, vq, vf, vr,
                 sg_hbm, tg_hbm, ot_hbm, *rest):
    outs, (sgo_hbm, tgo_hbm, oto_hbm, norm_out), (inb, outb, tbuf, obuf, insem, outsem, tis, tos, ois, oos) = rest[:25], rest[25:29], rest[29:]
    packs, heads = sg_hbm.shape[:2]
    n = packs * heads

    def s_in(i):
        return pltpu.make_async_copy(sg_hbm.at[i // heads, i % heads], inb.at[i % 3], insem.at[i % 3])

    def s_out(i):
        return pltpu.make_async_copy(outb.at[i % 3], sgo_hbm.at[i // heads, i % heads], outsem.at[i % 3])

    for i in range(3):
        s_in(i).start()
    half = ot_hbm.shape[0] // 2
    nt, trows = tis.shape[0], tbuf.shape[0] // tis.shape[0]
    tin = [pltpu.make_async_copy(tg_hbm.at[pl.ds(i * trows, trows), :], tbuf.at[pl.ds(i * trows, trows), :], tis.at[i]) for i in range(nt)]
    tout = [pltpu.make_async_copy(tbuf.at[pl.ds(i * trows, trows), :], tgo_hbm.at[pl.ds(i * trows, trows), :], tos.at[i]) for i in range(nt)]
    oin = [pltpu.make_async_copy(ot_hbm.at[pl.ds(i * half, half), :], obuf.at[i], ois.at[i]) for i in range(2)]
    oout = [pltpu.make_async_copy(obuf.at[i], oto_hbm.at[pl.ds(i * half, half), :], oos.at[i]) for i in range(2)]
    moves = list(zip(oin + tin, oout + tout))
    for first, _ in moves:
        first.start()
    norm = norm_ref[0:1, 0:1]
    norm_out[...] = norm
    factor = 1.0 / jnp.maximum(norm, 1.0)
    big_rate = wr.shape[-1] ** -0.5
    cols = wq.shape[-1]

    def update(g, w, m, v, rate, decay, o):
        g = g * factor
        mn = beta_one * m + (1.0 - beta_one) * g
        vn = beta_two * v + (1.0 - beta_two) * g * g
        corr = mn / (1.0 - beta_one ** STEP) / (jnp.sqrt(vn / (1.0 - beta_two ** STEP)) + adam_eps)
        new = w - rate * (corr + decay * w)
        o[0][...], o[1][...], o[2][...] = new, mn, vn
        if len(o) > 3:
            o[3][...] = new.astype(BF16)

    oa, oo, o1, o2 = (outs[i:i + 4] for i in range(0, 16, 4))
    oq, of, orr = (outs[i:i + 3] for i in (16, 19, 22))

    def attn_in(j):
        return lambda: update(sa[j], wa[j], ma[j], va[j], big_rate, weight_decay, [o.at[j] for o in oa])

    def smalls():
        update(small[9:11, 0:cols], wq[...], mq[...], vq[...], small_rate, 0.0, oq)
        row = small[8:9, :] * factor
        mn = beta_one * mf[...].reshape(row.shape) + (1.0 - beta_one) * row
        vn = beta_two * vf[...].reshape(row.shape) + (1.0 - beta_two) * row * row
        corr = mn / (1.0 - beta_one ** STEP) / (jnp.sqrt(vn / (1.0 - beta_two ** STEP)) + adam_eps)
        new = wf[...].reshape(row.shape) - small_rate * corr
        for o, val in zip(of, (new, mn, vn)):
            o[...] = val.reshape(o.shape)
        update(small[0:6, :], wr[...], mr[...], vr[...], small_rate, 0.0, orr)

    work = [
        lambda: update(s1[...], w1[...], m1[...], v1[...], big_rate, weight_decay, o1),
        lambda: update(s2[...], w2[...], m2[...], v2[...], big_rate, weight_decay, o2),
        attn_in(0), attn_in(1), attn_in(2),
        lambda: update(so[...].T, wo[...], mo[...], vo[...], big_rate, weight_decay, oo),
        smalls]
    for i in range(n):
        s_in(i).wait()
        if i >= 3:
            s_out(i - 3).wait()
        outb[i % 3] = inb[i % 3].astype(F32)
        s_out(i).start()
        if i + 3 < n:
            s_in(i + 3).start()
        if i < len(work):
            work[i]()
        if i < len(moves):
            moves[i][0].wait()
            moves[i][1].start()
    for i in range(n - 3, n):
        s_out(i).wait()
    for _, last in moves:
        last.wait()


def finish(norm, sa, s1, s2, so, small, ws, ms, vs, sg, tg, ot):
    vm = pl.BlockSpec(memory_space=pltpu.VMEM)
    h = pl.BlockSpec(memory_space=pl.ANY)
    sds = jax.ShapeDtypeStruct
    shapes = []
    for i, w in enumerate(ws):
        shapes += [sds(w.shape, F32)] * 3 + ([sds(w.shape, BF16)] if i < 4 else [])
    shapes += [sds(sg.shape, F32), sds(tg.shape, F32), sds(tg.shape, BF16), sds((1, 1), F32)]
    plen = sg.shape[-1]
    dma = pltpu.SemaphoreType.DMA
    return pl.pallas_call(
        final_kernel, out_shape=tuple(shapes), in_specs=[vm] * 27 + [h] * 3, out_specs=(vm,) * 25 + (h,) * 3 + (vm,),
        scratch_shapes=[pltpu.VMEM((3, plen, plen), BF16), pltpu.VMEM((3, plen, plen), F32),
                        pltpu.VMEM(tg.shape, F32), pltpu.VMEM((2, ot.shape[0] // 2, ot.shape[1]), BF16),
                        dma((3,)), dma((3,)), dma((6,)), dma((6,)), dma((2,)), dma((2,))],
        compiler_params=pltpu.CompilerParams(vmem_limit_bytes=60 << 20), name="optimizer",
    )(norm, sa, s1, s2, so, small, *ws, *ms, *vs, sg, tg, ot)


def fast_layer(
    tokens, segment_ids, prev_scores, out_grad,
    attn_in_master, attn_out_master, ffn_in_master, ffn_out_master,
    attn_in_first, attn_out_first, ffn_in_first, ffn_out_first,
    attn_in_second, attn_out_second, ffn_in_second, ffn_out_second,
    qv_bias, ffn_bias, row_params,
    qv_bias_first, ffn_bias_first, row_params_first,
    qv_bias_second, ffn_bias_second, row_params_second,
):
    s1, s2, so, sa, small, norm, tokens_grad, out_tokens, scores_grad, _ = layer(
        tokens, segment_ids, prev_scores, out_grad, row_params, qv_bias, ffn_bias,
        attn_in_master, ffn_in_master, ffn_out_master.T, attn_out_master)
    new = finish(
        norm, sa, s1, s2, so, small,
        (attn_in_master, attn_out_master, ffn_in_master, ffn_out_master.T, qv_bias, ffn_bias, row_params),
        (attn_in_first, attn_out_first, ffn_in_first, ffn_out_first.T, qv_bias_first, ffn_bias_first, row_params_first),
        (attn_in_second, attn_out_second, ffn_in_second, ffn_out_second.T, qv_bias_second, ffn_bias_second, row_params_second),
        scores_grad, tokens_grad, out_tokens)
    big = [list(new[i:i + 4]) for i in range(0, 16, 4)]
    big[3] = [a.T for a in big[3]]
    small_new = [new[i:i + 3] for i in range(16, 25, 3)]
    return (
        new[27], new[26], new[25], new[28].reshape(()),
        *[b[0] for b in big], *[b[1] for b in big], *[b[2] for b in big], *[b[3] for b in big],
        *[s[0] for s in small_new], *[s[1] for s in small_new], *[s[2] for s in small_new],
    )


def solution(mesh):
    in_specs = (
        P("dp", None),
        P("dp", None),
        P("dp", "tensor", None, None),
        P("dp", None),
        P(None, "dp", "tensor"),
        P("tensor", "dp"),
        P("dp", "tensor"),
        P("tensor", "dp"),
        P(None, "dp", "tensor"),
        P("tensor", "dp"),
        P("dp", "tensor"),
        P("tensor", "dp"),
        P(None, "dp", "tensor"),
        P("tensor", "dp"),
        P("dp", "tensor"),
        P("tensor", "dp"),
        P(None, "tensor"),
        P("tensor"),
        P(),
        P(None, "tensor"),
        P("tensor"),
        P(),
        P(None, "tensor"),
        P("tensor"),
        P(),
    )
    out_specs = (
        P("dp", None),
        P("dp", None),
        P("dp", "tensor", None, None),
        P(),
        P(None, "dp", "tensor"),
        P("tensor", "dp"),
        P("dp", "tensor"),
        P("tensor", "dp"),
        P(None, "dp", "tensor"),
        P("tensor", "dp"),
        P("dp", "tensor"),
        P("tensor", "dp"),
        P(None, "dp", "tensor"),
        P("tensor", "dp"),
        P("dp", "tensor"),
        P("tensor", "dp"),
        P(None, "dp", "tensor"),
        P("tensor", "dp"),
        P("dp", "tensor"),
        P("tensor", "dp"),
        P(None, "tensor"),
        P("tensor"),
        P(),
        P(None, "tensor"),
        P("tensor"),
        P(),
        P(None, "tensor"),
        P("tensor"),
        P(),
    )
    layer = fast_layer if dict(mesh.shape) == {"dp": 8, "tensor": 4} else plain_layer
    return jax.shard_map(
        layer, mesh=mesh, in_specs=in_specs, out_specs=out_specs, check_vma=False
    )
```

```python
from functools import partial

import jax
import jax.numpy as jnp
from jax import lax
from jax.experimental import pallas as pl
from jax.experimental.pallas import tpu as pltpu
from jax.sharding import PartitionSpec as P

D = 768
STEP = 5


beta_one = 0.5
beta_two = 0.5
weight_decay = 0.01
adam_eps = 1e-08
norm_eps = 1e-06
small_rate = 0.5


def layer_norm(rows_in, gain_row, shift_row):
    row_mean = jnp.mean(rows_in, axis=-1, keepdims=True)
    centred = rows_in - row_mean
    spread = jnp.mean(centred * centred, axis=-1, keepdims=True)
    return centred * lax.rsqrt(spread + norm_eps) * gain_row + shift_row


def masked_scores(scale, query_heads, key_heads, prev_block, seg_ids):
    same_seq = seg_ids[:, None] == seg_ids[None, :]
    scores = jnp.einsum(
        "qhe,khe->hqk", query_heads, key_heads, preferred_element_type=jnp.float32
    ) * scale + prev_block.astype(jnp.float32)
    return jnp.where(same_seq[None], scores, -1000000000.0)


def attend(scale, pieces):
    query_heads, key_heads, value_heads, prev_block, seg_ids = pieces
    scores = masked_scores(scale, query_heads, key_heads, prev_block, seg_ids)
    row_top = jnp.max(scores, axis=-1, keepdims=True)
    expo = jnp.exp(scores - row_top)
    row_total = jnp.sum(expo, axis=-1, keepdims=True)
    weights_low = (expo / row_total).astype(jnp.bfloat16)
    context_heads = jnp.einsum(
        "hqk,khe->qhe", weights_low, value_heads, preferred_element_type=jnp.float32
    )
    return (context_heads.astype(jnp.bfloat16), row_top + jnp.log(row_total))


def attend_back(scale, pieces):
    query_heads, key_heads, value_heads, prev_block, seg_ids, row_lse, grad_heads = pieces
    scores = masked_scores(scale, query_heads, key_heads, prev_block, seg_ids)
    soft = jnp.exp(scores - row_lse)
    soft_low = soft.astype(jnp.bfloat16)
    grad_soft = jnp.einsum(
        "qhe,khe->hqk", grad_heads, value_heads, preferred_element_type=jnp.float32
    )
    row_dot = jnp.sum(soft * grad_soft, axis=-1, keepdims=True)
    score_grad = (soft * (grad_soft - row_dot)).astype(jnp.bfloat16)
    grad_query = (
        jnp.einsum("hqk,khe->qhe", score_grad, key_heads, preferred_element_type=jnp.float32)
        * scale
    ).astype(jnp.bfloat16)
    grad_key = (
        jnp.einsum("hqk,qhe->khe", score_grad, query_heads, preferred_element_type=jnp.float32)
        * scale
    ).astype(jnp.bfloat16)
    grad_value = jnp.einsum(
        "hqk,qhe->khe", soft_low, grad_heads, preferred_element_type=jnp.float32
    ).astype(jnp.bfloat16)
    return (grad_query, grad_key, grad_value, score_grad.astype(jnp.float32))


def adam_update(weight, gradient, first_moment, second_moment, decay_rate, learn_rate):
    first_new = beta_one * first_moment + (1.0 - beta_one) * gradient
    second_new = beta_two * second_moment + (1.0 - beta_two) * gradient * gradient
    corrected = (
        first_new
        / (1.0 - beta_one**STEP)
        / (jnp.sqrt(second_new / (1.0 - beta_two**STEP)) + adam_eps)
    )
    return (weight - learn_rate * (corrected + decay_rate * weight), first_new, second_new)


def plain_layer(
    tokens,
    segment_ids,
    prev_scores,
    out_grad,
    attn_in_master,
    attn_out_master,
    ffn_in_master,
    ffn_out_master,
    attn_in_first,
    attn_out_first,
    ffn_in_first,
    ffn_out_first,
    attn_in_second,
    attn_out_second,
    ffn_in_second,
    ffn_out_second,
    qv_bias,
    ffn_bias,
    row_params,
    qv_bias_first,
    ffn_bias_first,
    row_params_first,
    qv_bias_second,
    ffn_bias_second,
    row_params_second,
):
    attn_in, attn_out, ffn_in, ffn_out = (
        lax.all_gather(attn_in_master.astype(jnp.bfloat16), "dp", axis=1, tiled=True),
        lax.all_gather(attn_out_master.astype(jnp.bfloat16), "dp", axis=1, tiled=True),
        lax.all_gather(ffn_in_master.astype(jnp.bfloat16), "dp", axis=0, tiled=True),
        lax.all_gather(ffn_out_master.astype(jnp.bfloat16), "dp", axis=1, tiled=True),
    )
    pack_count, pack_len = segment_ids.shape
    head_count = prev_scores.shape[1]
    head_width = attn_in.shape[2] // head_count
    scale = head_width ** (-0.5)
    token_count = tokens.shape[0]
    dp_count = lax.axis_size("dp")
    tensor_count = lax.axis_size("tensor")

    def split_heads(matrix):
        return matrix.reshape(pack_count, pack_len, head_count, head_width)

    projected = jnp.einsum("td,cde->cte", tokens, attn_in, preferred_element_type=jnp.float32)
    query_rows = (projected[0] + qv_bias[0]).astype(jnp.bfloat16)
    key_rows = projected[1].astype(jnp.bfloat16)
    value_rows = (projected[2] + qv_bias[1]).astype(jnp.bfloat16)
    query_heads = split_heads(query_rows)
    key_heads = split_heads(key_rows)
    value_heads = split_heads(value_rows)
    context_heads, row_lse = lax.map(
        partial(attend, scale), (query_heads, key_heads, value_heads, prev_scores, segment_ids)
    )
    context = context_heads.reshape(token_count, -1)
    attn_partial = jnp.dot(context, attn_out, preferred_element_type=jnp.float32)
    live_whole = (segment_ids > 0).astype(jnp.float32).reshape(token_count, 1)
    rows_start = tokens.astype(jnp.float32)
    attended = lax.psum(attn_partial, "tensor") + row_params[2]
    cotangent = out_grad.astype(jnp.float32)
    residual_one = rows_start + attended
    normed, first_pull = jax.vjp(layer_norm, residual_one, row_params[0], row_params[3])
    normed_low = normed.astype(jnp.bfloat16)
    pre_act = jnp.dot(normed_low, ffn_in, preferred_element_type=jnp.float32) + ffn_bias
    activation, gelu_pull = jax.vjp(partial(jax.nn.gelu, approximate=False), pre_act)
    act_low = activation.astype(jnp.bfloat16)
    ffn_partial = jnp.dot(act_low, ffn_out, preferred_element_type=jnp.float32)
    ffn_output = lax.psum(ffn_partial, "tensor") + row_params[4]

    def final_norm(rows_in, gain_row, shift_row):
        return layer_norm(rows_in, gain_row, shift_row) * live_whole

    final_rows, second_pull = jax.vjp(final_norm, normed + ffn_output, row_params[1], row_params[5])
    final_low = final_rows.astype(jnp.bfloat16)
    grad_res_two, grad_gain_two, grad_shift_two = second_pull(cotangent)
    grad_ffn_low = grad_res_two.astype(jnp.bfloat16)
    grad_ffn_out_bias = jnp.sum(grad_ffn_low.astype(jnp.float32), axis=0)
    grad_ffn_out = jnp.einsum(
        "tf,td->fd", act_low, grad_ffn_low, preferred_element_type=jnp.float32
    )
    grad_act = jnp.einsum("td,fd->tf", grad_ffn_low, ffn_out, preferred_element_type=jnp.float32)
    (grad_pre,) = gelu_pull(grad_act)
    grad_pre_low = grad_pre.astype(jnp.bfloat16)
    grad_ffn_bias = jnp.sum(grad_pre_low.astype(jnp.float32), axis=0)
    grad_ffn_in = jnp.einsum(
        "td,tf->df", normed_low, grad_pre_low, preferred_element_type=jnp.float32
    )
    hidden_part = jnp.einsum("tf,df->td", grad_pre_low, ffn_in, preferred_element_type=jnp.float32)
    grad_normed = grad_res_two + lax.psum(hidden_part, "tensor")
    grad_res_one, grad_gain_one, grad_shift_one = first_pull(grad_normed)
    att_low = grad_res_one.astype(jnp.bfloat16)
    grad_att_bias = jnp.sum(att_low.astype(jnp.float32), axis=0)
    grad_attn_out = jnp.einsum("te,td->ed", context, att_low, preferred_element_type=jnp.float32)
    grad_context = jnp.einsum(
        "td,ed->te", att_low, attn_out, preferred_element_type=jnp.float32
    ).astype(jnp.bfloat16)
    grad_query, grad_key, grad_value, scores_grad = lax.map(
        partial(attend_back, scale),
        (
            query_heads,
            key_heads,
            value_heads,
            prev_scores,
            segment_ids,
            row_lse,
            split_heads(grad_context),
        ),
    )
    grad_proj = jnp.stack(
        [
            grad_query.reshape(token_count, -1),
            grad_key.reshape(token_count, -1),
            grad_value.reshape(token_count, -1),
        ]
    )
    grad_attn_in = jnp.einsum("td,cte->cde", tokens, grad_proj, preferred_element_type=jnp.float32)
    grad_qv_bias = jnp.stack(
        [
            jnp.sum(grad_proj[0].astype(jnp.float32), axis=0),
            jnp.sum(grad_proj[2].astype(jnp.float32), axis=0),
        ]
    )
    input_part = jnp.einsum("cte,cde->td", grad_proj, attn_in, preferred_element_type=jnp.float32)
    norm_stack = jnp.stack([grad_gain_one, grad_gain_two, grad_shift_one, grad_shift_two])
    tokens_grad = grad_res_one + lax.psum(input_part, "tensor")
    grad_rows = jnp.stack(
        [
            norm_stack[0],
            norm_stack[1],
            grad_att_bias,
            norm_stack[2],
            grad_ffn_out_bias,
            norm_stack[3],
        ]
    )
    summed = lax.psum(
        (
            grad_attn_in,
            grad_attn_out,
            grad_ffn_in,
            grad_ffn_out,
            grad_qv_bias,
            grad_ffn_bias,
            grad_rows,
        ),
        "dp",
    )
    dp_index = lax.axis_index("dp")

    def own_part(whole_grad, shard, along):
        extent = shard.shape[along]
        return lax.dynamic_slice_in_dim(whole_grad, dp_index * extent, extent, along)

    shares = (
        own_part(summed[0], attn_in_master, 1),
        own_part(summed[1], attn_out_master, 1),
        own_part(summed[2], ffn_in_master, 0),
        own_part(summed[3], ffn_out_master, 1),
    )
    small_sums = (summed[4], summed[5], summed[6])
    local_squares = jnp.float32(0.0)
    for share in shares:
        local_squares = local_squares + jnp.sum(share * share)
    local_squares = (
        local_squares
        + (jnp.sum(small_sums[0] * small_sums[0]) + jnp.sum(small_sums[1] * small_sums[1]))
        / dp_count
    )
    local_squares = local_squares + jnp.sum(small_sums[2] * small_sums[2]) / (
        dp_count * tensor_count
    )
    total_squares = lax.psum(local_squares, ("dp", "tensor"))
    grad_norm = jnp.sqrt(total_squares)
    factor = 1.0 / jnp.maximum(grad_norm, 1.0)
    olds = (
        attn_in_master,
        attn_out_master,
        ffn_in_master,
        ffn_out_master,
        qv_bias,
        ffn_bias,
        row_params,
    )
    firsts = (
        attn_in_first,
        attn_out_first,
        ffn_in_first,
        ffn_out_first,
        qv_bias_first,
        ffn_bias_first,
        row_params_first,
    )
    seconds = (
        attn_in_second,
        attn_out_second,
        ffn_in_second,
        ffn_out_second,
        qv_bias_second,
        ffn_bias_second,
        row_params_second,
    )
    gradients = (
        shares[0],
        shares[1],
        shares[2],
        shares[3],
        small_sums[0],
        small_sums[1],
        small_sums[2],
    )
    decays = (weight_decay, weight_decay, weight_decay, weight_decay, 0.0, 0.0, 0.0)
    big_rate = D ** (-0.5)
    rates = (big_rate, big_rate, big_rate, big_rate, small_rate, small_rate, small_rate)
    updated = [
        adam_update(
            olds[place],
            gradients[place] * factor,
            firsts[place],
            seconds[place],
            decays[place],
            rates[place],
        )
        for place in range(7)
    ]
    return (
        final_low,
        tokens_grad,
        scores_grad,
        grad_norm,
        updated[0][0],
        updated[1][0],
        updated[2][0],
        updated[3][0],
        updated[0][1],
        updated[1][1],
        updated[2][1],
        updated[3][1],
        updated[0][2],
        updated[1][2],
        updated[2][2],
        updated[3][2],
        updated[0][0].astype(jnp.bfloat16),
        updated[1][0].astype(jnp.bfloat16),
        updated[2][0].astype(jnp.bfloat16),
        updated[3][0].astype(jnp.bfloat16),
        updated[4][0],
        updated[5][0],
        updated[6][0],
        updated[4][1],
        updated[5][1],
        updated[6][1],
        updated[4][2],
        updated[5][2],
        updated[6][2],
    )


F32 = jnp.float32
BF16 = jnp.bfloat16
NT = (((1,), (1,)), ((), ()))
def dot(a, b):
    return jnp.dot(a, b, preferred_element_type=F32)
def dot_nt(a, b):
    return lax.dot_general(a, b, NT, preferred_element_type=F32)

def head_masks(shape, heads, hw):
    lane = lax.broadcasted_iota(jnp.int32, shape, len(shape) - 1)
    return [(lane >= h * hw) & (lane < (h + 1) * hw) for h in range(heads)]

def pick_heads(masks, parts):
    out = parts[-1]
    for m, p in zip(masks[:-1][::-1], parts[:-1][::-1]):
        out = jnp.where(m, p, out)
    return out

MESH = pl.DeviceIdType.MESH
ROWS = 256


def gelu_parts(pre):
    z = jnp.abs(pre)
    a = 1.0 + (0.3275911 * 0.7071067811865476) * z
    t = pl.reciprocal(a, approx=True)
    t = t * (2.0 - a * t)
    e = jnp.exp(-0.5 * pre * pre)
    half = (0.5 * t) * (0.254829592 + t * (-0.284496736 + t * (1.421413741 + t * (-1.453152027 + t * 1.061405429)))) * e
    cdf = jnp.where(pre >= 0.0, 1.0 - half, half)
    return pre * cdf, cdf + pre * (0.3989422804014327 * e)


def remote(src, dst, s, r, dev):
    return pltpu.make_async_remote_copy(src, dst, s, r, device_id=dev, device_id_type=MESH)


def layer_kernel(tok_ref, seg_ref, bias_ref, fbo_ref, rp_ref, wam_ref, w1m_ref, w2m_ref, wom_ref, prev_hbm, og_hbm,
                 s1_ref, s2_ref, so_ref, sa_ref, small_ref, norm_ref, tok_grad, out_full, sg_hbm, p_hbm,
                 r1, r2, y1, y2, q_ref, k_ref, v_ref, wa_ref, fb_ref, wo_ref, w1, w2, ctx4, ctx_loc, seg8, segt,
                 out_ref, gres1_ref, gctx, gw1, gw2, gwo, grow_ref, gfb_ref, ro, rrow, rfb, ba, yo, ya, zo, za,
                 sm_send, sm_recv, sq, sqt, sqd, lsem, psems,
                 zs, zr, ys, yr, xs, xr, x2s, x2r, cs, cr, os_, or_, fs, fr, xcs, xcr, dcs, dcr,
                 free, gs, gr_, es, er, hs, hr, ts, tr, xxs, xxr, us, ur, ul, ms, mr, ns, nr_, insem, outsem):
    packs, heads, plen, _ = prev_hbm.shape
    hw = wa_ref.shape[-1] // heads
    scale = hw ** -0.5
    d = lax.axis_index("dp")
    t = lax.axis_index("tensor")
    z, y, x, c = d // 2, d % 2, t // 2, t % 2
    oy = 1 - y
    ot = (1 - x) * 2 + c
    yn, xn, sib, xd = (z * 2 + oy, t), (d, ot), (d, x * 2 + 1 - c), (d, (1 - x) * 2 + 1 - c)
    zp = [None] + [(((z + k) % 4) * 2 + y, t) for k in (1, 2, 3)]
    line = [((z + 4 - j) % 4) * 2 + y for j in range(4)]
    oline = [((z + 4 - j) % 4) * 2 + oy for j in range(4)]
    part = wam_ref.shape[1]
    rows, width = tok_ref.shape
    half = rows // 2

    def drows(dd):
        return pl.ds(pl.multiple_of(dd * part, 32), part)

    def at(a, dd):
        if a == 0:
            return wa_ref.at[:, drows(dd), :]
        ref, slot = ((w1, t), (w2, t), (w1, ot), (wo_ref, t), (wo_ref, ot))[a - 1]
        return ref.at[slot, drows(dd), :]

    def zc(a, k):
        return remote(at(a, d), at(a, d), zs.at[a, k - 1], zr.at[a, k - 1], zp[k])

    def yc(a, j):
        return remote(at(a, line[j]), at(a, line[j]), ys.at[a, j], yr.at[a, j], yn)

    def x1c():
        return remote(at(1, d), at(1, d), xs.at[0], xr.at[0], xn)

    def x2c(j, yy):
        ref = at(2, oline[j] if yy else line[j])
        return remote(ref, ref, x2s.at[j, yy], x2r.at[j, yy], xn)

    def xoc():
        return remote(at(4, d), at(4, d), xs.at[1], xr.at[1], xn)

    def oc(i):
        src = wo_ref.at[ot if i else t]
        return remote(src, src, os_.at[i], or_.at[i], sib)

    def cc(a, i):
        ref = (w1, w2)[a - 1].at[ot if i else t]
        return remote(ref, ref, cs.at[a - 1, i], cr.at[a - 1, i], sib)

    dpp = [((d + i) % 8, t) for i in range(8)]
    peers = [xn, sib, xd] + dpp[1:] + [((d + i) % 8, ot) for i in range(1, 8)]
    bar = pltpu.get_barrier_semaphore()
    for dev in peers:
        pl.semaphore_signal(bar, inc=1, device_id=dev, device_id_type=MESH)
    wa_ref[:, drows(d), :] = wam_ref[...].astype(BF16)
    wo_ref[t, drows(d), :] = wom_ref[...].T.astype(BF16)
    w1[t, drows(d), :] = w1m_ref[...].astype(BF16)
    w2[t, drows(d), :] = w2m_ref[...].astype(BF16)
    fb_ref[t] = fbo_ref[...].reshape(1, -1)
    pl.semaphore_wait(bar, len(peers))

    sent = []

    def go(make, *args):
        make(*args).start()
        sent.append((make, args))

    def line_out(a):
        for k in (1, 3, 2):
            go(zc, a, k)

    def out_y(a):
        go(yc, a, 0)

    def pass_y(a, k):
        zc(a, k).wait_recv()
        go(yc, a, k)

    def pass_w2(k):
        pass_y(2, k)
        go(x2c, k, 0)

    def pass_x(k):
        yc(2, k).wait_recv()
        go(x2c, k, 1)

    def pass_wo(k):
        pass_y(4, k)
        pass_y(5, k)

    def core_w1(i):
        for j in range(4):
            yc(3 if i else 1, j).wait_recv()
        go(cc, 1, i)

    def core_w2(i):
        if i:
            for j in range(4):
                x2c(j, 0).wait_recv()
                x2c(j, 1).wait_recv()
        go(cc, 2, i)

    def core_wo():
        for j in range(4):
            yc(4, j).wait_recv()
            yc(5, j).wait_recv()
        go(oc, 0)
        go(oc, 1)

    def run(*steps):
        for f, *args in steps:
            f(*args)

    run((line_out, 0), (go, xoc), (out_y, 4), (out_y, 0), (out_y, 2), (go, x1c))

    def fc(i):
        return remote(fb_ref.at[t], fb_ref.at[t], fs.at[i], fr.at[i], (sib, xn, xd)[i])

    for i in range(3):
        go(fc, i)

    blk = plen // 2

    def ctx_send(b):
        owner, i = b // 3, b % 3
        src = ctx_loc.at[pl.ds(b * blk, blk), :]
        dst = ctx4.at[t, pl.ds(i * blk, blk), :]
        far = (d, (1 - x) * 2 + owner)
        return (owner, remote(src, dst, xcs.at[i], xcr.at[i], far), remote(src, dst, xcs.at[3 + i], xcr.at[3 + i], far),
                remote(src, dst, dcs.at[i], dcr.at[i], sib))

    hrow = pl.ds(pl.multiple_of(c * half, half), half)
    zk = [(z + k) % 4 for k in range(4)]

    def core_grad(i):
        src, dst = ((gw1.at[1], r1), (gw2.at[1], r2), (gwo.at[1], ro), (gctx, ctx_loc.at[hrow, :]),
                    (gfb_ref.at[1], rfb), (grow_ref, rrow))[i]
        return remote(src, dst, hs.at[i], hr.at[i], sib)

    def out_send():
        return remote(out_ref, out_full.at[hrow, :], hs.at[6], hr.at[6], sib)

    def out_local():
        return pltpu.make_async_copy(out_ref, out_full.at[hrow, :], lsem.at[2])

    outs = (s1_ref, s2_ref, so_ref, sa_ref)

    def summed(a, dd):
        return ba.at[:, drows(dd), :] if a == 3 else (gw1, gw2, gwo)[a].at[0, drows(dd), :]

    def from_y(a, k):
        return (y1, y2, yo, ya)[a].at[k]

    def from_z(a, k):
        return w1.at[3, pl.ds((4 * a + k - 1) * part, part), :] if a < 2 else (zo, za)[a - 2].at[k - 1]

    def grad_y(a, k):
        return remote(summed(a, zk[k] * 2 + oy), from_y(a, k), gs.at[a, k], gr_.at[a, k], yn)

    def grad_z(a, k):
        return remote(summed(a, zk[k] * 2 + y), from_z(a, k), es.at[a, k - 1], er.at[a, k - 1], zp[k])

    def fold_core(a):
        theirs = (r1, r2, ro)[a]

        def f():
            core_grad(a).wait_recv()

            @pl.loop(0, width // part)
            def _(i):
                ref = summed(a, i)
                ref[...] = (ref[...].astype(F32) + theirs[drows(i), :].astype(F32)).astype(BF16)
            for k in (1, 2, 3, 0):
                go(grad_y, a, k)
        return f

    def fold_y(a, k):
        def f():
            grad_y(a, k).wait_recv()
            at_ = summed(a, zk[k] * 2 + y)
            total = at_[...].astype(F32) + from_y(a, k)[...].astype(F32)
            if k == 0:
                outs[a][...] = total
            else:
                at_[...] = total.astype(BF16)
                go(grad_z, a, k)
        return f

    def fold_z(a):
        def f():
            total = outs[a][...]
            for k in (1, 2, 3):
                grad_z(a, k).wait_recv()
                total = total + from_z(a, k)[...].astype(F32)
            outs[a][...] = total
        return f

    def settle():
        for b in range(6):
            owner, away, diag, near = ctx_send(b)

            @pl.when(c == owner)
            def _():
                away.wait_send()

            @pl.when(c != owner)
            def _():
                diag.wait_send()
                near.wait_send()
        grads = (out_send, core_grad, grad_y)
        early = [s for s in sent if s[0] not in grads]
        late = [s for s in sent if s[0] in grads]
        for make, args in early:
            make(*args).wait_send()
        sent[:] = late

    def attention(prev, stage, mask):
        def p_copy(i):
            return pltpu.make_async_copy(stage.at[i % 2], p_hbm.at[i // heads, i % heads], psems.at[i % 2])

        pcopy = pltpu.make_async_copy(prev_hbm, prev, lsem.at[0])
        pcopy.start()
        seg8[...] = jnp.zeros_like(seg8)
        seg8[0:packs, :] = seg_ref[...].astype(F32)
        segt[...] = seg8[...].T
        run((pass_y, 0, 3), (line_out, 2), (pass_y, 0, 1))
        xoc().wait_recv()
        run((line_out, 5), (pass_y, 0, 2), (pass_x, 0), (out_y, 1))
        x1c().wait_recv()
        line_out(4)
        for j in range(4):
            yc(0, j).wait_recv()
        run((out_y, 3), (pass_w2, 1), (out_y, 5), (go, x2c, 0, 0))
        steps = {0: [(line_out, 1), (pass_w2, 3)], 3: [(pass_w2, 2)], 4: [(pass_wo, 2)], 6: [(pass_wo, 1)]}
        masks = head_masks((plen, heads * hw), heads, hw)
        pcopy.wait()
        n = packs * heads
        for p in range(packs):
            rr = pl.ds(p * plen, plen)
            tok = tok_ref[rr, :]
            q_ref[rr, :] = ((dot(tok, wa_ref[0]) + bias_ref[0:1, :]).astype(BF16) * scale).astype(BF16)
            k_ref[rr, :] = dot(tok, wa_ref[1]).astype(BF16)
            v_ref[rr, :] = (dot(tok, wa_ref[2]) + bias_ref[1:2, :]).astype(BF16)
            mask[...] = jnp.where(segt[:, p:p + 1] == seg8[p:p + 1, :], 0.0, -1e9)
            outs = []
            for h in range(heads):
                i = p * heads + h
                qm = jnp.where(masks[h], q_ref[rr, :], jnp.zeros((), BF16))
                s = dot_nt(qm, k_ref[rr, :]) + (prev[p, h].astype(F32) + mask[...])
                m = jnp.max(s, axis=-1, keepdims=True)
                e = jnp.exp(s - m)
                pr = e * (1.0 / jnp.sum(e, axis=-1, keepdims=True))
                if i >= 2:
                    p_copy(i - 2).wait()
                stage[i % 2] = pr
                p_copy(i).start()
                outs.append(dot(pr.astype(BF16), v_ref[rr, :]))
                run(*steps.get(i, ()))
            ctx_loc[rr, :] = pick_heads(masks, outs).astype(BF16)
            for b in (2 * p, 2 * p + 1):
                owner, away, diag, near = ctx_send(b)

                @pl.when(c == owner)
                def _():
                    away.start()
                    ctx4[t, pl.ds(b % 3 * blk, blk), :] = ctx_loc[pl.ds(b * blk, blk), :]

                @pl.when(c != owner)
                def _():
                    diag.start()
                    near.start()
        p_copy(n - 2).wait()
        p_copy(n - 1).wait()

    pl.run_scoped(attention, pltpu.VMEM(prev_hbm.shape, BF16), pltpu.VMEM((2, plen, plen), F32), pltpu.VMEM((plen, plen), F32))

    def feed_forward(og_ref, live_ref, xhat, rstd, hid, hidt, act, dg, acc, gft):
        ogc = pltpu.make_async_copy(og_hbm.at[pl.ds(pl.multiple_of(c * half, half), half), :], og_ref, lsem.at[1])
        ogc.start()
        nr = half // ROWS
        gain1, gain2, bo, shift1, b2, shift2 = (rp_ref[i:i + 1, :] for i in range(6))
        inv = 1.0 / width

        def blkr(r):
            return pl.ds(pl.multiple_of(r * ROWS, ROWS), ROWS)

        run((pass_y, 1, 1), (pass_wo, 3), (pass_x, 3), (pass_y, 1, 3), (line_out, 3), (pass_x, 1), (pass_x, 2),
            (core_w2, 0), (pass_y, 1, 2), (core_wo,), (pass_y, 3, 1))
        for b in range(6):
            pack = b // 2
            col = (segt[b % 2 * blk:(b % 2 + 1) * blk, pack:pack + 1] > 0.0).astype(F32)

            @pl.when(c == b // 3)
            def _():
                live_ref[pl.ds(b % 3 * blk, blk), :] = col
        oc(0).wait_recv()
        oc(1).wait_recv()
        for b in range(6):
            owner, away, diag, near = ctx_send(b)

            @pl.when(c == owner)
            def _():
                away.wait_recv()
                diag.wait_recv()
                near.wait_recv()
        att = dot_nt(ctx4[0], wo_ref[0])
        for s in range(1, 4):
            att = att + dot_nt(ctx4[s], wo_ref[s])
        acc[...] = att
        run((core_w1, 0), (pass_y, 3, 3))

        @pl.loop(0, nr)
        def _(r):
            rr = blkr(r)
            trow = pl.ds(pl.multiple_of(c * half + r * ROWS, ROWS), ROWS)
            r1 = (tok_ref[trow, :].astype(F32) + bo) + acc[rr, :]
            mean = jnp.sum(r1, axis=-1, keepdims=True) * inv
            cen = r1 - mean
            rs = lax.rsqrt(jnp.sum(cen * cen, axis=-1, keepdims=True) * inv + norm_eps)
            xh = cen * rs
            xhat[rr, :] = xh
            rstd[rr, :] = rs
            h = (xh * gain1 + shift1).astype(BF16)
            hid[rr, :] = h
            hidt[:, rr] = h.T

        run((pass_y, 3, 2), (core_w2, 1))
        for i in range(3):
            fc(i).wait_recv()
        cc(1, 0).wait_recv()
        cc(2, 0).wait_recv()

        def unit_ff(s, out, first):
            pre = dot(hid[...], w1[s]) + fb_ref[s]
            a, g = gelu_parts(pre)
            act[s] = a.astype(BF16)
            dg[s] = g.astype(BF16)
            low = dot_nt(act[s], w2[s])
            if first:
                out[...] = low
            else:
                out[...] += low

        unit_ff(x * 2, acc, True)
        core_w1(1)
        unit_ff(x * 2 + 1, acc, False)
        cc(1, 1).wait_recv()
        cc(2, 1).wait_recv()
        unit_ff((1 - x) * 2, gres1_ref, True)
        unit_ff((1 - x) * 2 + 1, gres1_ref, False)

        grow_ref[...] = jnp.zeros_like(grow_ref)
        ogc.wait()

        @pl.loop(0, nr)
        def _(r):
            rr = blkr(r)
            r2 = (xhat[rr, :] * gain1 + shift1) + ((acc[rr, :] + gres1_ref[rr, :]) + b2)
            mean = jnp.sum(r2, axis=-1, keepdims=True) * inv
            cen = r2 - mean
            rs = lax.rsqrt(jnp.sum(cen * cen, axis=-1, keepdims=True) * inv + norm_eps)
            xh = cen * rs
            live = live_ref[rr, :]
            out_ref[rr, :] = (live * (xh * gain2 + shift2)).astype(BF16)
            g = og_ref[rr, :].astype(F32) * live
            grow_ref[1:2, :] += jnp.sum(g * xh, axis=0, keepdims=True)
            grow_ref[5:6, :] += jnp.sum(g, axis=0, keepdims=True)
            dx = g * gain2
            m1 = jnp.sum(dx, axis=-1, keepdims=True) * inv
            m2 = jnp.sum(dx * xh, axis=-1, keepdims=True) * inv
            gr = rs * (dx - m1 - xh * m2)
            acc[rr, :] = gr
            low = gr.astype(BF16)
            hid[rr, :] = low
            gft[:, rr] = low.T
            grow_ref[4:5, :] += jnp.sum(low.astype(F32), axis=0, keepdims=True)

        out_local().start()
        go(out_send)

        def hidden_grad(s):
            dg[s] = (dot(hid[...], w2[s]) * dg[s].astype(F32)).astype(BF16)

        def grad_w1(i, s):
            gp = dg[s]
            gw1[i] = dot(hidt[...], gp).astype(BF16)
            gfb_ref[i] = jnp.sum(gp.astype(F32), axis=0, keepdims=True)

        def grad_w2(i, s):
            gw2[i] = dot(gft[...], act[s]).astype(BF16)

        st = x * 2 + 1 - c
        grad_w2(1, st)
        go(core_grad, 1)
        hidden_grad(st)
        grad_w1(1, st)
        go(core_grad, 0)
        grad_w2(0, t)
        hidden_grad(t)
        grad_w1(0, t)
        fold_core(1)()
        fold_core(0)()

        @pl.loop(0, 2)
        def _(i):
            hidden_grad((1 - x) * 2 + i)

        @pl.loop(0, 4)
        def _(s):
            acc[...] += dot_nt(dg[s], w1[s])

        settle()
        for dev in (sib, xn, zp[1], zp[2], zp[3]):
            pl.semaphore_signal(free, inc=1, device_id=dev, device_id_type=MESH)

        @pl.loop(0, nr)
        def _(r):
            rr = blkr(r)
            xh = xhat[rr, :]
            g = acc[rr, :]
            grow_ref[0:1, :] += jnp.sum(g * xh, axis=0, keepdims=True)
            grow_ref[3:4, :] += jnp.sum(g, axis=0, keepdims=True)
            dx = g * gain1
            m1 = jnp.sum(dx, axis=-1, keepdims=True) * inv
            m2 = jnp.sum(dx * xh, axis=-1, keepdims=True) * inv
            gr = rstd[rr, :] * (dx - m1 - xh * m2)
            gres1_ref[rr, :] = gr
            low = gr.astype(BF16)
            og_ref[rr, :] = low
            gft[:, rr] = low.T
            grow_ref[2:3, :] += jnp.sum(low.astype(F32), axis=0, keepdims=True)

        pl.semaphore_wait(free, 5)
        so_ = st
        gctx[...] = dot(og_ref[...], wo_ref[so_]).astype(BF16)
        go(core_grad, 3)
        ctx_loc[hrow, :] = dot(og_ref[...], wo_ref[t]).astype(BF16)
        gwo[1] = dot(gft[...], ctx4[so_]).astype(BF16)
        go(core_grad, 2)
        go(core_grad, 4)
        go(core_grad, 5)
        gwo[0] = dot(gft[...], ctx4[t]).astype(BF16)
        fold_y(1, 1)()
        fold_y(1, 2)()

    ff = w1.shape[-1]
    V = pltpu.VMEM
    pl.run_scoped(
        feed_forward, V((half, width), BF16), V((half, 1), F32), V((half, width), F32), V((half, 1), F32),
        V((half, width), BF16), V((width, half), BF16), V((4, half, ff), BF16), V((4, half, ff), BF16),
        V((half, width), F32), V((width, half), BF16))
    def attention_back(pbuf, stage, tokt, gts, ga, gb, mine, ssend, cx, tg):
        def tc(i):
            return remote(ssend.at[i], w2.at[0, pl.ds(i * blk, blk), :], ts.at[i], tr.at[i], sib)

        def xc(i):
            return remote(cx.at[i], w2.at[1, pl.ds(i * blk, blk), :], xxs.at[i], xxr.at[i], xn)

        def trow(b):
            return pl.ds(b * blk, blk)

        def ucl(b):
            return pltpu.make_async_copy(tg.at[b % 3], tok_grad.at[trow(b), :], ul.at[b % 3])

        def ucr(b):
            return remote(tg.at[b % 3], tok_grad.at[trow(b), :], us.at[b % 3], ur.at[b % 3], sib)

        def part_ready(b, total):
            i = b % 3

            @pl.when(c == b // 3)
            def _():
                mine[i] = total

            @pl.when(c != b // 3)
            def _():
                ssend[i] = total.astype(BF16)
                tc(i).start()

        def part_chip(b):
            i = b % 3

            def f():
                @pl.when(c == b // 3)
                def _():
                    tc(i).wait_recv()
                    cx[i] = (mine[i] + w2[0, pl.ds(i * blk, blk), :].astype(F32)).astype(BF16)
                    xc(i).start()
            return f

        def part_done(b):
            i = b % 3

            def f():
                @pl.when(c == b // 3)
                def _():
                    xc(i).wait_recv()
                    tg[i] = gres1_ref[pl.ds(i * blk, blk), :] + (cx[i].astype(F32) + w2[1, pl.ds(i * blk, blk), :].astype(F32))
                    ucl(b).start()
                    ucr(b).start()
            return f

        cols = wa_ref.shape[-1]
        n = packs * heads
        masks = head_masks((plen, cols), heads, hw)
        steps = {0: [fold_core(2), fold_y(1, 3)], 1: [fold_y(1, 0)], 2: [fold_y(0, 1)], 3: [fold_y(0, 2), part_chip(0)], 4: [fold_y(0, 3), part_chip(1)],
                 5: [fold_y(0, 0)], 6: [fold_y(2, 1), part_chip(2), part_chip(3)], 7: [fold_y(2, 2), fold_y(2, 3)], 8: [fold_y(2, 0)]}

        def p_in(i):
            return pltpu.make_async_copy(p_hbm.at[i // heads, i % heads], pbuf.at[i % 3], insem.at[i % 3])

        def s_out(i):
            return pltpu.make_async_copy(stage.at[i % 2], sg_hbm.at[i // heads, i % heads], outsem.at[i % 2])

        p_in(0).start()
        p_in(1).start()
        for p in range(packs):
            tokt[:, p * plen:(p + 1) * plen] = tok_ref[pl.ds(p * plen, plen), :].T
        core_grad(3).wait_recv()
        for p in range(packs):
            rr = pl.ds(p * plen, plen)
            qt = q_ref[rr, :].T
            kt = k_ref[rr, :].T
            gct = ctx_loc[rr, :].T
            for h in range(heads):
                i = p * heads + h
                hh = slice(h * hw, (h + 1) * hw)
                p_in(i).wait()
                if i + 2 < n:
                    p_in(i + 2).start()
                gm = jnp.where(masks[h], ctx_loc[rr, :], jnp.zeros((), BF16))
                pf = pbuf[i % 3]
                dp = dot_nt(gm, v_ref[rr, :])
                rd = jnp.sum(pf * dp, axis=-1, keepdims=True)
                ds = (pf * (dp - rd)).astype(BF16)
                if i >= 2:
                    s_out(i - 2).wait()
                stage[i % 2] = ds
                s_out(i).start()
                gts[0, hh, :] = dot_nt(kt[hh, :], ds) * scale
                gts[1, hh, :] = dot(qt[hh, :], ds)
                gts[2, hh, :] = dot(gct[hh, :], pf.astype(BF16))
                for f in steps.get(i, ()):
                    f()
            total = None
            for j in range(3):
                gcol = gts[j].T.astype(BF16)
                xx = dot_nt(gcol, wa_ref[j])
                total = xx if total is None else total + xx
                yy = dot(tokt[:, p * plen:(p + 1) * plen], gcol)
                bb = jnp.sum(gcol.astype(F32), axis=0, keepdims=True)
                if p == 0:
                    ga[j] = yy
                    gb[j] = bb
                elif p < packs - 1:
                    ga[j] += yy
                    gb[j] += bb
                else:
                    ba[j] = (ga[j] + yy).astype(BF16)
                    gb[j] += bb
            part_ready(2 * p, total[:blk])
            part_ready(2 * p + 1, total[blk:])
        for k in (1, 2, 3, 0):
            go(grad_y, 3, k)
        for f in (part_chip(4), part_chip(5)):
            f()
        part_done(0)()
        part_done(1)()

        core_grad(4).wait_recv()
        core_grad(5).wait_recv()
        sm_send[0:8, :] = grow_ref[...] + rrow[...]
        sm_send[8:16, :] = jnp.zeros_like(sm_send[8:16, :])
        sm_send[8:9, :] = gfb_ref[0] + rfb[...]
        sm_send[9:10, 0:cols] = gb[0]
        sm_send[10:11, 0:cols] = gb[2]

        def mc(m):
            return remote(sm_send, sm_recv.at[d], ms.at[m - 1], mr.at[m - 1], dpp[m])

        for m in range(1, 8):
            go(mc, m)
        sm_recv[d] = sm_send[...]

        for f in (fold_y(3, 1), part_done(2), fold_y(3, 2), part_done(3), fold_z(0), fold_z(1), fold_z(2), fold_y(3, 3), fold_y(3, 0),
                  part_done(4), part_done(5)):
            f()
        for m in range(1, 8):
            mc(m).wait_recv()
        small = sm_recv[0]
        for i in range(1, 8):
            small = small + sm_recv[i]
        small_ref[...] = small

        def square(v):
            return jnp.sum(v * v, keepdims=True)

        sh = square(small[8:16, :]) * (1.0 / 8.0)
        sh = sh + (square(s1_ref[...]) + square(s2_ref[...]) + square(so_ref[...]))
        fold_z(3)()
        for j in range(3):
            sh = sh + square(sa_ref[j])
        sq[...] = jnp.broadcast_to(sh, sq.shape)

        def norm_core():
            return remote(sq, sqt, ns.at[15], nr_.at[15], sib)

        def norm_chip(i):
            return remote(sqd.at[16], sqd.at[d * 2 + x], ns.at[i - 1], nr_.at[i - 1], ((d + i // 2) % 8, (x + i % 2) % 2 * 2 + c))

        go(norm_core)
        norm_core().wait_recv()
        pair = sq[...] + sqt[...]
        sqd[16] = pair
        for i in range(1, 16):
            go(norm_chip, i)
        sqd[d * 2 + x] = pair
        for i in range(1, 16):
            norm_chip(i).wait_recv()
        tot = sqd[0]
        for i in range(1, 16):
            tot = tot + sqd[i]
        tot = tot[0:1, 0:1]
        norm_ref[...] = jnp.broadcast_to(jnp.sqrt(tot + square(small[0:8, :])), norm_ref.shape)

        for b in range(6):
            i = b % 3

            @pl.when(c == b // 3)
            def _():
                xc(i).wait_send()
                ucl(b).wait()
                ucr(b).wait_send()

            @pl.when(c != b // 3)
            def _():
                tc(i).wait_send()
                ucr(b).wait_recv()
        s_out(n - 2).wait()
        s_out(n - 1).wait()
        out_local().wait()
        out_send().wait_recv()
        for make, args in sent:
            make(*args).wait_send()


    cols = wa_ref.shape[-1]
    pl.run_scoped(
        attention_back, V((3, plen, plen), F32), V((2, plen, plen), BF16), V((width, rows), BF16), V((3, cols, plen), F32),
        V((3, width, cols), F32), V((3, 1, cols), F32), V((3, blk, width), F32), V((3, blk, width), BF16), V((3, blk, width), BF16),
        V((3, blk, width), F32))


def layer(tok, seg, prev, og, rp, bias, fbo, wam, w1m, w2m, wom):
    packs, heads, plen, _ = prev.shape
    rows, width = tok.shape
    _, part, cols = wam.shape
    ff = w1m.shape[-1]
    v = pl.BlockSpec(memory_space=pltpu.VMEM)
    h = pl.BlockSpec(memory_space=pl.ANY)
    sds = jax.ShapeDtypeStruct
    V = pltpu.VMEM
    dma = pltpu.SemaphoreType.DMA
    half = rows // 2
    return pl.pallas_call(
        layer_kernel,
        out_shape=(sds((part, ff), F32), sds((part, ff), F32), sds((part, cols), F32), sds((3, part, cols), F32),
                   sds((16, width), F32), sds((8, 128), F32), sds((rows, width), F32), sds((rows, width), BF16),
                   sds(prev.shape, BF16), sds(prev.shape, F32)),
        in_specs=[v] * 9 + [h] * 2, out_specs=(v,) * 6 + (h,) * 4,
        scratch_shapes=[
            V((width, ff), BF16), V((width, ff), BF16), V((4, part, ff), BF16), V((4, part, ff), BF16),
            V((rows, cols), BF16), V((rows, cols), BF16), V((rows, cols), BF16), V((3, width, cols), BF16),
            V((4, 1, ff), F32), V((4, width, cols), BF16), V((4, width, ff), BF16), V((4, width, ff), BF16),
            V((4, half, cols), BF16), V((rows, cols), BF16), V((8, plen), F32), V((plen, 8), F32),
            V((half, width), BF16), V((half, width), F32), V((half, cols), BF16), V((2, width, ff), BF16), V((2, width, ff), BF16),
            V((2, width, cols), BF16), V((8, width), F32), V((2, 1, ff), F32),
            V((width, cols), BF16), V((8, width), F32), V((1, ff), F32), V((3, width, cols), BF16),
            V((4, part, cols), BF16), V((4, 3, part, cols), BF16), V((3, part, cols), BF16), V((3, 3, part, cols), BF16),
            V((16, width), F32), V((8, 16, width), F32), V((8, 128), F32), V((8, 128), F32), V((17, 8, 128), F32), dma((3,)), dma((2,)),
            dma((6, 3)), dma((6, 3)), dma((6, 4)), dma((6, 4)), dma((2,)), dma((2,)),
            dma((4, 2)), dma((4, 2)), dma((2, 2)), dma((2, 2)), dma((3,)), dma((3,)), dma((3,)), dma((3,)),
            dma((6,)), dma((6,)), dma((3,)), dma((3,)),
            pltpu.SemaphoreType.REGULAR, dma((4, 4)), dma((4, 4)), dma((4, 3)), dma((4, 3)), dma((7,)), dma((7,)),
            dma((3,)), dma((3,)), dma((3,)), dma((3,)), dma((3,)), dma((3,)), dma((3,)), dma((7,)), dma((7,)), dma((16,)), dma((16,)),
            dma((3,)), dma((2,))],
        compiler_params=pltpu.CompilerParams(vmem_limit_bytes=63 << 20, collective_id=1, has_side_effects=True),
        name="layer",
    )(tok, seg, bias, fbo, rp, wam, w1m, w2m, wom, prev, og)


def final_kernel(norm_ref, sa, s1, s2, so, small, wa, wo, w1, w2, wq, wf, wr, ma, mo, m1, m2, mq, mf, mr, va, vo, v1, v2, vq, vf, vr,
                 sg_hbm, tg_hbm, ot_hbm, *rest):
    outs, (sgo_hbm, tgo_hbm, oto_hbm, norm_out), (inb, outb, tbuf, obuf, insem, outsem, tis, tos, ois, oos) = rest[:25], rest[25:29], rest[29:]
    packs, heads = sg_hbm.shape[:2]
    n = packs * heads

    def s_in(i):
        return pltpu.make_async_copy(sg_hbm.at[i // heads, i % heads], inb.at[i], insem.at[i])

    def s_out(i):
        return pltpu.make_async_copy(outb.at[i], sgo_hbm.at[i // heads, i % heads], outsem.at[i])

    for i in range(n):
        s_in(i).start()
    half = ot_hbm.shape[0] // 2
    nt, trows = tis.shape[0], tbuf.shape[0] // tis.shape[0]
    tin = [pltpu.make_async_copy(tg_hbm.at[pl.ds(i * trows, trows), :], tbuf.at[pl.ds(i * trows, trows), :], tis.at[i]) for i in range(nt)]
    tout = [pltpu.make_async_copy(tbuf.at[pl.ds(i * trows, trows), :], tgo_hbm.at[pl.ds(i * trows, trows), :], tos.at[i]) for i in range(nt)]
    oin = [pltpu.make_async_copy(ot_hbm.at[pl.ds(i * half, half), :], obuf.at[i], ois.at[i]) for i in range(2)]
    oout = [pltpu.make_async_copy(obuf.at[i], oto_hbm.at[pl.ds(i * half, half), :], oos.at[i]) for i in range(2)]
    moves = list(zip(oin + tin, oout + tout))
    for first, _ in moves:
        first.start()
    norm = norm_ref[0:1, 0:1]
    norm_out[...] = norm
    factor = 1.0 / jnp.maximum(norm, 1.0)
    big_rate = wr.shape[-1] ** -0.5
    cols = wq.shape[-1]

    def update(g, w, m, v, rate, decay, o):
        g = g * factor
        mn = beta_one * m + (1.0 - beta_one) * g
        vn = beta_two * v + (1.0 - beta_two) * g * g
        corr = mn / (1.0 - beta_one ** STEP) / (jnp.sqrt(vn / (1.0 - beta_two ** STEP)) + adam_eps)
        new = w - rate * (corr + decay * w)
        o[0][...], o[1][...], o[2][...] = new, mn, vn
        if len(o) > 3:
            o[3][...] = new.astype(BF16)

    oa, oo, o1, o2 = (outs[i:i + 4] for i in range(0, 16, 4))
    oq, of, orr = (outs[i:i + 3] for i in (16, 19, 22))

    def attn_in(j):
        return lambda: update(sa[j], wa[j], ma[j], va[j], big_rate, weight_decay, [o.at[j] for o in oa])

    def smalls():
        update(small[9:11, 0:cols], wq[...], mq[...], vq[...], small_rate, 0.0, oq)
        row = small[8:9, :] * factor
        mn = beta_one * mf[...].reshape(row.shape) + (1.0 - beta_one) * row
        vn = beta_two * vf[...].reshape(row.shape) + (1.0 - beta_two) * row * row
        corr = mn / (1.0 - beta_one ** STEP) / (jnp.sqrt(vn / (1.0 - beta_two ** STEP)) + adam_eps)
        new = wf[...].reshape(row.shape) - small_rate * corr
        for o, val in zip(of, (new, mn, vn)):
            o[...] = val.reshape(o.shape)
        update(small[0:6, :], wr[...], mr[...], vr[...], small_rate, 0.0, orr)

    work = [
        lambda: update(s1[...], w1[...], m1[...], v1[...], big_rate, weight_decay, o1),
        lambda: update(s2[...], w2[...], m2[...], v2[...], big_rate, weight_decay, o2),
        attn_in(0), attn_in(1), attn_in(2),
        lambda: update(so[...].T, wo[...], mo[...], vo[...], big_rate, weight_decay, oo),
        smalls]
    for i in range(n):
        s_in(i).wait()
        outb[i] = inb[i].astype(F32)
        s_out(i).start()
        if i < len(work):
            work[i]()
        if i < len(moves):
            moves[i][0].wait()
            moves[i][1].start()
    for i in range(n):
        s_out(i).wait()
    for _, last in moves:
        last.wait()


def finish(norm, sa, s1, s2, so, small, ws, ms, vs, sg, tg, ot):
    vm = pl.BlockSpec(memory_space=pltpu.VMEM)
    h = pl.BlockSpec(memory_space=pl.ANY)
    sds = jax.ShapeDtypeStruct
    shapes = []
    for i, w in enumerate(ws):
        shapes += [sds(w.shape, F32)] * 3 + ([sds(w.shape, BF16)] if i < 4 else [])
    shapes += [sds(sg.shape, F32), sds(tg.shape, F32), sds(tg.shape, BF16), sds((1, 1), F32)]
    plen = sg.shape[-1]
    n = sg.shape[0] * sg.shape[1]
    dma = pltpu.SemaphoreType.DMA
    return pl.pallas_call(
        final_kernel, out_shape=tuple(shapes), in_specs=[vm] * 27 + [h] * 3, out_specs=(vm,) * 25 + (h,) * 3 + (vm,),
        scratch_shapes=[pltpu.VMEM((n, plen, plen), BF16), pltpu.VMEM((n, plen, plen), F32),
                        pltpu.VMEM(tg.shape, F32), pltpu.VMEM((2, ot.shape[0] // 2, ot.shape[1]), BF16),
                        dma((n,)), dma((n,)), dma((6,)), dma((6,)), dma((2,)), dma((2,))],
        compiler_params=pltpu.CompilerParams(vmem_limit_bytes=60 << 20), name="optimizer",
    )(norm, sa, s1, s2, so, small, *ws, *ms, *vs, sg, tg, ot)


def fast_layer(
    tokens, segment_ids, prev_scores, out_grad,
    attn_in_master, attn_out_master, ffn_in_master, ffn_out_master,
    attn_in_first, attn_out_first, ffn_in_first, ffn_out_first,
    attn_in_second, attn_out_second, ffn_in_second, ffn_out_second,
    qv_bias, ffn_bias, row_params,
    qv_bias_first, ffn_bias_first, row_params_first,
    qv_bias_second, ffn_bias_second, row_params_second,
):
    s1, s2, so, sa, small, norm, tokens_grad, out_tokens, scores_grad, _ = layer(
        tokens, segment_ids, prev_scores, out_grad, row_params, qv_bias, ffn_bias,
        attn_in_master, ffn_in_master, ffn_out_master.T, attn_out_master)
    new = finish(
        norm, sa, s1, s2, so, small,
        (attn_in_master, attn_out_master, ffn_in_master, ffn_out_master.T, qv_bias, ffn_bias, row_params),
        (attn_in_first, attn_out_first, ffn_in_first, ffn_out_first.T, qv_bias_first, ffn_bias_first, row_params_first),
        (attn_in_second, attn_out_second, ffn_in_second, ffn_out_second.T, qv_bias_second, ffn_bias_second, row_params_second),
        scores_grad, tokens_grad, out_tokens)
    big = [list(new[i:i + 4]) for i in range(0, 16, 4)]
    big[3] = [a.T for a in big[3]]
    small_new = [new[i:i + 3] for i in range(16, 25, 3)]
    return (
        new[27], new[26], new[25], new[28].reshape(()),
        *[b[0] for b in big], *[b[1] for b in big], *[b[2] for b in big], *[b[3] for b in big],
        *[s[0] for s in small_new], *[s[1] for s in small_new], *[s[2] for s in small_new],
    )


def solution(mesh):
    in_specs = (
        P("dp", None),
        P("dp", None),
        P("dp", "tensor", None, None),
        P("dp", None),
        P(None, "dp", "tensor"),
        P("tensor", "dp"),
        P("dp", "tensor"),
        P("tensor", "dp"),
        P(None, "dp", "tensor"),
        P("tensor", "dp"),
        P("dp", "tensor"),
        P("tensor", "dp"),
        P(None, "dp", "tensor"),
        P("tensor", "dp"),
        P("dp", "tensor"),
        P("tensor", "dp"),
        P(None, "tensor"),
        P("tensor"),
        P(),
        P(None, "tensor"),
        P("tensor"),
        P(),
        P(None, "tensor"),
        P("tensor"),
        P(),
    )
    out_specs = (
        P("dp", None),
        P("dp", None),
        P("dp", "tensor", None, None),
        P(),
        P(None, "dp", "tensor"),
        P("tensor", "dp"),
        P("dp", "tensor"),
        P("tensor", "dp"),
        P(None, "dp", "tensor"),
        P("tensor", "dp"),
        P("dp", "tensor"),
        P("tensor", "dp"),
        P(None, "dp", "tensor"),
        P("tensor", "dp"),
        P("dp", "tensor"),
        P("tensor", "dp"),
        P(None, "dp", "tensor"),
        P("tensor", "dp"),
        P("dp", "tensor"),
        P("tensor", "dp"),
        P(None, "tensor"),
        P("tensor"),
        P(),
        P(None, "tensor"),
        P("tensor"),
        P(),
        P(None, "tensor"),
        P("tensor"),
        P(),
    )
    layer = fast_layer if dict(mesh.shape) == {"dp": 8, "tensor": 4} else plain_layer
    return jax.shard_map(
        layer, mesh=mesh, in_specs=in_specs, out_specs=out_specs, check_vma=False
    )
```

```python
from functools import partial

import jax
import jax.numpy as jnp
from jax import lax
from jax.experimental import pallas as pl
from jax.experimental.pallas import tpu as pltpu
from jax.sharding import PartitionSpec as P

D = 768
STEP = 5


beta_one = 0.5
beta_two = 0.5
weight_decay = 0.01
adam_eps = 1e-08
norm_eps = 1e-06
small_rate = 0.5


def layer_norm(rows_in, gain_row, shift_row):
    row_mean = jnp.mean(rows_in, axis=-1, keepdims=True)
    centred = rows_in - row_mean
    spread = jnp.mean(centred * centred, axis=-1, keepdims=True)
    return centred * lax.rsqrt(spread + norm_eps) * gain_row + shift_row


def masked_scores(scale, query_heads, key_heads, prev_block, seg_ids):
    same_seq = seg_ids[:, None] == seg_ids[None, :]
    scores = jnp.einsum(
        "qhe,khe->hqk", query_heads, key_heads, preferred_element_type=jnp.float32
    ) * scale + prev_block.astype(jnp.float32)
    return jnp.where(same_seq[None], scores, -1000000000.0)


def attend(scale, pieces):
    query_heads, key_heads, value_heads, prev_block, seg_ids = pieces
    scores = masked_scores(scale, query_heads, key_heads, prev_block, seg_ids)
    row_top = jnp.max(scores, axis=-1, keepdims=True)
    expo = jnp.exp(scores - row_top)
    row_total = jnp.sum(expo, axis=-1, keepdims=True)
    weights_low = (expo / row_total).astype(jnp.bfloat16)
    context_heads = jnp.einsum(
        "hqk,khe->qhe", weights_low, value_heads, preferred_element_type=jnp.float32
    )
    return (context_heads.astype(jnp.bfloat16), row_top + jnp.log(row_total))


def attend_back(scale, pieces):
    query_heads, key_heads, value_heads, prev_block, seg_ids, row_lse, grad_heads = pieces
    scores = masked_scores(scale, query_heads, key_heads, prev_block, seg_ids)
    soft = jnp.exp(scores - row_lse)
    soft_low = soft.astype(jnp.bfloat16)
    grad_soft = jnp.einsum(
        "qhe,khe->hqk", grad_heads, value_heads, preferred_element_type=jnp.float32
    )
    row_dot = jnp.sum(soft * grad_soft, axis=-1, keepdims=True)
    score_grad = (soft * (grad_soft - row_dot)).astype(jnp.bfloat16)
    grad_query = (
        jnp.einsum("hqk,khe->qhe", score_grad, key_heads, preferred_element_type=jnp.float32)
        * scale
    ).astype(jnp.bfloat16)
    grad_key = (
        jnp.einsum("hqk,qhe->khe", score_grad, query_heads, preferred_element_type=jnp.float32)
        * scale
    ).astype(jnp.bfloat16)
    grad_value = jnp.einsum(
        "hqk,qhe->khe", soft_low, grad_heads, preferred_element_type=jnp.float32
    ).astype(jnp.bfloat16)
    return (grad_query, grad_key, grad_value, score_grad.astype(jnp.float32))


def adam_update(weight, gradient, first_moment, second_moment, decay_rate, learn_rate):
    first_new = beta_one * first_moment + (1.0 - beta_one) * gradient
    second_new = beta_two * second_moment + (1.0 - beta_two) * gradient * gradient
    corrected = (
        first_new
        / (1.0 - beta_one**STEP)
        / (jnp.sqrt(second_new / (1.0 - beta_two**STEP)) + adam_eps)
    )
    return (weight - learn_rate * (corrected + decay_rate * weight), first_new, second_new)


def plain_layer(
    tokens,
    segment_ids,
    prev_scores,
    out_grad,
    attn_in_master,
    attn_out_master,
    ffn_in_master,
    ffn_out_master,
    attn_in_first,
    attn_out_first,
    ffn_in_first,
    ffn_out_first,
    attn_in_second,
    attn_out_second,
    ffn_in_second,
    ffn_out_second,
    qv_bias,
    ffn_bias,
    row_params,
    qv_bias_first,
    ffn_bias_first,
    row_params_first,
    qv_bias_second,
    ffn_bias_second,
    row_params_second,
):
    attn_in, attn_out, ffn_in, ffn_out = (
        lax.all_gather(attn_in_master.astype(jnp.bfloat16), "dp", axis=1, tiled=True),
        lax.all_gather(attn_out_master.astype(jnp.bfloat16), "dp", axis=1, tiled=True),
        lax.all_gather(ffn_in_master.astype(jnp.bfloat16), "dp", axis=0, tiled=True),
        lax.all_gather(ffn_out_master.astype(jnp.bfloat16), "dp", axis=1, tiled=True),
    )
    pack_count, pack_len = segment_ids.shape
    head_count = prev_scores.shape[1]
    head_width = attn_in.shape[2] // head_count
    scale = head_width ** (-0.5)
    token_count = tokens.shape[0]
    dp_count = lax.axis_size("dp")
    tensor_count = lax.axis_size("tensor")

    def split_heads(matrix):
        return matrix.reshape(pack_count, pack_len, head_count, head_width)

    projected = jnp.einsum("td,cde->cte", tokens, attn_in, preferred_element_type=jnp.float32)
    query_rows = (projected[0] + qv_bias[0]).astype(jnp.bfloat16)
    key_rows = projected[1].astype(jnp.bfloat16)
    value_rows = (projected[2] + qv_bias[1]).astype(jnp.bfloat16)
    query_heads = split_heads(query_rows)
    key_heads = split_heads(key_rows)
    value_heads = split_heads(value_rows)
    context_heads, row_lse = lax.map(
        partial(attend, scale), (query_heads, key_heads, value_heads, prev_scores, segment_ids)
    )
    context = context_heads.reshape(token_count, -1)
    attn_partial = jnp.dot(context, attn_out, preferred_element_type=jnp.float32)
    live_whole = (segment_ids > 0).astype(jnp.float32).reshape(token_count, 1)
    rows_start = tokens.astype(jnp.float32)
    attended = lax.psum(attn_partial, "tensor") + row_params[2]
    cotangent = out_grad.astype(jnp.float32)
    residual_one = rows_start + attended
    normed, first_pull = jax.vjp(layer_norm, residual_one, row_params[0], row_params[3])
    normed_low = normed.astype(jnp.bfloat16)
    pre_act = jnp.dot(normed_low, ffn_in, preferred_element_type=jnp.float32) + ffn_bias
    activation, gelu_pull = jax.vjp(partial(jax.nn.gelu, approximate=False), pre_act)
    act_low = activation.astype(jnp.bfloat16)
    ffn_partial = jnp.dot(act_low, ffn_out, preferred_element_type=jnp.float32)
    ffn_output = lax.psum(ffn_partial, "tensor") + row_params[4]

    def final_norm(rows_in, gain_row, shift_row):
        return layer_norm(rows_in, gain_row, shift_row) * live_whole

    final_rows, second_pull = jax.vjp(final_norm, normed + ffn_output, row_params[1], row_params[5])
    final_low = final_rows.astype(jnp.bfloat16)
    grad_res_two, grad_gain_two, grad_shift_two = second_pull(cotangent)
    grad_ffn_low = grad_res_two.astype(jnp.bfloat16)
    grad_ffn_out_bias = jnp.sum(grad_ffn_low.astype(jnp.float32), axis=0)
    grad_ffn_out = jnp.einsum(
        "tf,td->fd", act_low, grad_ffn_low, preferred_element_type=jnp.float32
    )
    grad_act = jnp.einsum("td,fd->tf", grad_ffn_low, ffn_out, preferred_element_type=jnp.float32)
    (grad_pre,) = gelu_pull(grad_act)
    grad_pre_low = grad_pre.astype(jnp.bfloat16)
    grad_ffn_bias = jnp.sum(grad_pre_low.astype(jnp.float32), axis=0)
    grad_ffn_in = jnp.einsum(
        "td,tf->df", normed_low, grad_pre_low, preferred_element_type=jnp.float32
    )
    hidden_part = jnp.einsum("tf,df->td", grad_pre_low, ffn_in, preferred_element_type=jnp.float32)
    grad_normed = grad_res_two + lax.psum(hidden_part, "tensor")
    grad_res_one, grad_gain_one, grad_shift_one = first_pull(grad_normed)
    att_low = grad_res_one.astype(jnp.bfloat16)
    grad_att_bias = jnp.sum(att_low.astype(jnp.float32), axis=0)
    grad_attn_out = jnp.einsum("te,td->ed", context, att_low, preferred_element_type=jnp.float32)
    grad_context = jnp.einsum(
        "td,ed->te", att_low, attn_out, preferred_element_type=jnp.float32
    ).astype(jnp.bfloat16)
    grad_query, grad_key, grad_value, scores_grad = lax.map(
        partial(attend_back, scale),
        (
            query_heads,
            key_heads,
            value_heads,
            prev_scores,
            segment_ids,
            row_lse,
            split_heads(grad_context),
        ),
    )
    grad_proj = jnp.stack(
        [
            grad_query.reshape(token_count, -1),
            grad_key.reshape(token_count, -1),
            grad_value.reshape(token_count, -1),
        ]
    )
    grad_attn_in = jnp.einsum("td,cte->cde", tokens, grad_proj, preferred_element_type=jnp.float32)
    grad_qv_bias = jnp.stack(
        [
            jnp.sum(grad_proj[0].astype(jnp.float32), axis=0),
            jnp.sum(grad_proj[2].astype(jnp.float32), axis=0),
        ]
    )
    input_part = jnp.einsum("cte,cde->td", grad_proj, attn_in, preferred_element_type=jnp.float32)
    norm_stack = jnp.stack([grad_gain_one, grad_gain_two, grad_shift_one, grad_shift_two])
    tokens_grad = grad_res_one + lax.psum(input_part, "tensor")
    grad_rows = jnp.stack(
        [
            norm_stack[0],
            norm_stack[1],
            grad_att_bias,
            norm_stack[2],
            grad_ffn_out_bias,
            norm_stack[3],
        ]
    )
    summed = lax.psum(
        (
            grad_attn_in,
            grad_attn_out,
            grad_ffn_in,
            grad_ffn_out,
            grad_qv_bias,
            grad_ffn_bias,
            grad_rows,
        ),
        "dp",
    )
    dp_index = lax.axis_index("dp")

    def own_part(whole_grad, shard, along):
        extent = shard.shape[along]
        return lax.dynamic_slice_in_dim(whole_grad, dp_index * extent, extent, along)

    shares = (
        own_part(summed[0], attn_in_master, 1),
        own_part(summed[1], attn_out_master, 1),
        own_part(summed[2], ffn_in_master, 0),
        own_part(summed[3], ffn_out_master, 1),
    )
    small_sums = (summed[4], summed[5], summed[6])
    local_squares = jnp.float32(0.0)
    for share in shares:
        local_squares = local_squares + jnp.sum(share * share)
    local_squares = (
        local_squares
        + (jnp.sum(small_sums[0] * small_sums[0]) + jnp.sum(small_sums[1] * small_sums[1]))
        / dp_count
    )
    local_squares = local_squares + jnp.sum(small_sums[2] * small_sums[2]) / (
        dp_count * tensor_count
    )
    total_squares = lax.psum(local_squares, ("dp", "tensor"))
    grad_norm = jnp.sqrt(total_squares)
    factor = 1.0 / jnp.maximum(grad_norm, 1.0)
    olds = (
        attn_in_master,
        attn_out_master,
        ffn_in_master,
        ffn_out_master,
        qv_bias,
        ffn_bias,
        row_params,
    )
    firsts = (
        attn_in_first,
        attn_out_first,
        ffn_in_first,
        ffn_out_first,
        qv_bias_first,
        ffn_bias_first,
        row_params_first,
    )
    seconds = (
        attn_in_second,
        attn_out_second,
        ffn_in_second,
        ffn_out_second,
        qv_bias_second,
        ffn_bias_second,
        row_params_second,
    )
    gradients = (
        shares[0],
        shares[1],
        shares[2],
        shares[3],
        small_sums[0],
        small_sums[1],
        small_sums[2],
    )
    decays = (weight_decay, weight_decay, weight_decay, weight_decay, 0.0, 0.0, 0.0)
    big_rate = D ** (-0.5)
    rates = (big_rate, big_rate, big_rate, big_rate, small_rate, small_rate, small_rate)
    updated = [
        adam_update(
            olds[place],
            gradients[place] * factor,
            firsts[place],
            seconds[place],
            decays[place],
            rates[place],
        )
        for place in range(7)
    ]
    return (
        final_low,
        tokens_grad,
        scores_grad,
        grad_norm,
        updated[0][0],
        updated[1][0],
        updated[2][0],
        updated[3][0],
        updated[0][1],
        updated[1][1],
        updated[2][1],
        updated[3][1],
        updated[0][2],
        updated[1][2],
        updated[2][2],
        updated[3][2],
        updated[0][0].astype(jnp.bfloat16),
        updated[1][0].astype(jnp.bfloat16),
        updated[2][0].astype(jnp.bfloat16),
        updated[3][0].astype(jnp.bfloat16),
        updated[4][0],
        updated[5][0],
        updated[6][0],
        updated[4][1],
        updated[5][1],
        updated[6][1],
        updated[4][2],
        updated[5][2],
        updated[6][2],
    )


F32 = jnp.float32
BF16 = jnp.bfloat16
NT = (((1,), (1,)), ((), ()))
def dot(a, b):
    return jnp.dot(a, b, preferred_element_type=F32)
def dot_nt(a, b):
    return lax.dot_general(a, b, NT, preferred_element_type=F32)

def head_masks(shape, heads, hw):
    lane = lax.broadcasted_iota(jnp.int32, shape, len(shape) - 1)
    return [(lane >= h * hw) & (lane < (h + 1) * hw) for h in range(heads)]

def pick_heads(masks, parts):
    out = parts[-1]
    for m, p in zip(masks[:-1][::-1], parts[:-1][::-1]):
        out = jnp.where(m, p, out)
    return out

MESH = pl.DeviceIdType.MESH
ROWS = 256


def gelu_parts(pre):
    z = jnp.abs(pre)
    a = 1.0 + (0.3275911 * 0.7071067811865476) * z
    t = pl.reciprocal(a, approx=True)
    t = t * (2.0 - a * t)
    e = jnp.exp(-0.5 * pre * pre)
    half = (0.5 * t) * (0.254829592 + t * (-0.284496736 + t * (1.421413741 + t * (-1.453152027 + t * 1.061405429)))) * e
    cdf = jnp.where(pre >= 0.0, 1.0 - half, half)
    return pre * cdf, cdf + pre * (0.3989422804014327 * e)


def remote(src, dst, s, r, dev):
    return pltpu.make_async_remote_copy(src, dst, s, r, device_id=dev, device_id_type=MESH)


def layer_kernel(tok_ref, seg_ref, bias_ref, fbo_ref, rp_ref, wam_ref, w1m_ref, w2m_ref, wom_ref, prev_hbm, og_hbm,
                 s1_ref, s2_ref, so_ref, sa_ref, small_ref, norm_ref, tok_grad, out_full, sg_hbm, p_hbm,
                 r1, r2, y1, y2, q_ref, k_ref, v_ref, wa_ref, fb_ref, wo_ref, w1, w2, ctx4, ctx_loc, seg8, segt,
                 out_ref, gres1_ref, gctx, gw1, gw2, gwo, grow_ref, gfb_ref, ro, rrow, rfb, ba, yo, ya, zo, za,
                 sm_send, sm_recv, sq, sqt, sqd, lsem, psems,
                 zs, zr, ys, yr, xs, xr, x2s, x2r, cs, cr, os_, or_, fs, fr, xcs, xcr, dcs, dcr,
                 free, zfree, gs, gr_, es, er, hs, hr, ts, tr, xxs, xxr, us, ur, ul, ms, mr, ns, nr_, insem, outsem):
    packs, heads, plen, _ = prev_hbm.shape
    hw = wa_ref.shape[-1] // heads
    scale = hw ** -0.5
    d = lax.axis_index("dp")
    t = lax.axis_index("tensor")
    z, y, x, c = d // 2, d % 2, t // 2, t % 2
    oy = 1 - y
    ot = (1 - x) * 2 + c
    yn, xn, sib, xd = (z * 2 + oy, t), (d, ot), (d, x * 2 + 1 - c), (d, (1 - x) * 2 + 1 - c)
    zp = [None] + [(((z + k) % 4) * 2 + y, t) for k in (1, 2, 3)]
    line = [((z + 4 - j) % 4) * 2 + y for j in range(4)]
    oline = [((z + 4 - j) % 4) * 2 + oy for j in range(4)]
    part = wam_ref.shape[1]
    rows, width = tok_ref.shape
    half = rows // 2

    def drows(dd):
        return pl.ds(pl.multiple_of(dd * part, 32), part)

    def at(a, dd):
        if a == 0:
            return wa_ref.at[:, drows(dd), :]
        ref, slot = ((w1, t), (w2, t), (w1, ot), (wo_ref, t), (wo_ref, ot))[a - 1]
        return ref.at[slot, drows(dd), :]

    def zc(a, k):
        return remote(at(a, d), at(a, d), zs.at[a, k - 1], zr.at[a, k - 1], zp[k])

    def yc(a, j):
        return remote(at(a, line[j]), at(a, line[j]), ys.at[a, j], yr.at[a, j], yn)

    def x1c():
        return remote(at(1, d), at(1, d), xs.at[0], xr.at[0], xn)

    def x2c(j, yy):
        ref = at(2, oline[j] if yy else line[j])
        return remote(ref, ref, x2s.at[j, yy], x2r.at[j, yy], xn)

    def xoc():
        return remote(at(4, d), at(4, d), xs.at[1], xr.at[1], xn)

    def oc(i):
        src = wo_ref.at[ot if i else t]
        return remote(src, src, os_.at[i], or_.at[i], sib)

    def cc(a, i):
        ref = (w1, w2)[a - 1].at[ot if i else t]
        return remote(ref, ref, cs.at[a - 1, i], cr.at[a - 1, i], sib)

    dpp = [((d + i) % 8, t) for i in range(8)]
    peers = [xn, sib, xd] + dpp[1:] + [((d + i) % 8, ot) for i in range(1, 8)]
    bar = pltpu.get_barrier_semaphore()
    for dev in peers:
        pl.semaphore_signal(bar, inc=1, device_id=dev, device_id_type=MESH)
    wa_ref[:, drows(d), :] = wam_ref[...].astype(BF16)
    wo_ref[t, drows(d), :] = wom_ref[...].T.astype(BF16)
    w1[t, drows(d), :] = w1m_ref[...].astype(BF16)
    w2[t, drows(d), :] = w2m_ref[...].astype(BF16)
    fb_ref[t] = fbo_ref[...].reshape(1, -1)
    pl.semaphore_wait(bar, len(peers))

    sent = []

    def go(make, *args):
        make(*args).start()
        sent.append((make, args))

    def line_out(a):
        for k in (1, 3, 2):
            go(zc, a, k)

    def out_y(a):
        go(yc, a, 0)

    def pass_y(a, k):
        zc(a, k).wait_recv()
        go(yc, a, k)

    def pass_w2(k):
        pass_y(2, k)
        go(x2c, k, 0)

    def pass_x(k):
        yc(2, k).wait_recv()
        go(x2c, k, 1)

    def pass_wo(k):
        pass_y(4, k)
        pass_y(5, k)

    def core_w1(i):
        for j in range(4):
            yc(3 if i else 1, j).wait_recv()
        go(cc, 1, i)

    def core_w2(i):
        if i:
            for j in range(4):
                x2c(j, 0).wait_recv()
                x2c(j, 1).wait_recv()
        go(cc, 2, i)

    def core_wo():
        for j in range(4):
            yc(4, j).wait_recv()
            yc(5, j).wait_recv()
        go(oc, 0)
        go(oc, 1)

    def run(*steps):
        for f, *args in steps:
            f(*args)

    run((line_out, 0), (go, xoc), (out_y, 4), (out_y, 0), (out_y, 2), (go, x1c))

    def fc(i):
        return remote(fb_ref.at[t], fb_ref.at[t], fs.at[i], fr.at[i], (sib, xn, xd)[i])

    for i in range(3):
        go(fc, i)

    blk = plen // 2

    def ctx_send(b):
        owner, i = b // 3, b % 3
        src = ctx_loc.at[pl.ds(b * blk, blk), :]
        dst = ctx4.at[t, pl.ds(i * blk, blk), :]
        far = (d, (1 - x) * 2 + owner)
        return (owner, remote(src, dst, xcs.at[i], xcr.at[i], far), remote(src, dst, xcs.at[3 + i], xcr.at[3 + i], far),
                remote(src, dst, dcs.at[i], dcr.at[i], sib))

    hrow = pl.ds(pl.multiple_of(c * half, half), half)
    zk = [(z + k) % 4 for k in range(4)]

    def core_grad(i):
        src, dst = ((gw1.at[1], r1), (gw2.at[1], r2), (gwo.at[1], ro), (gctx, ctx_loc.at[hrow, :]),
                    (gfb_ref.at[1], rfb), (grow_ref, rrow))[i]
        return remote(src, dst, hs.at[i], hr.at[i], sib)

    def out_send():
        return remote(out_ref, out_full.at[hrow, :], hs.at[6], hr.at[6], sib)

    def out_local():
        return pltpu.make_async_copy(out_ref, out_full.at[hrow, :], lsem.at[2])

    outs = (s1_ref, s2_ref, so_ref, sa_ref)

    def summed(a, dd):
        return ba.at[:, drows(dd), :] if a == 3 else (gw1, gw2, gwo)[a].at[0, drows(dd), :]

    def from_y(a, k):
        return (y1, y2, yo, ya)[a].at[k]

    def from_z(a, k):
        return (r1, r2)[a].at[pl.ds((k - 1) * part, part), :] if a < 2 else (zo, za)[a - 2].at[k - 1]

    def grad_y(a, k):
        return remote(summed(a, zk[k] * 2 + oy), from_y(a, k), gs.at[a, k], gr_.at[a, k], yn)

    def grad_z(a, k):
        return remote(summed(a, zk[k] * 2 + y), from_z(a, k), es.at[a, k - 1], er.at[a, k - 1], zp[k])

    def fold_core(a):
        theirs = (r1, r2, ro)[a]

        def f():
            core_grad(a).wait_recv()

            @pl.loop(0, width // part)
            def _(i):
                ref = summed(a, i)
                ref[...] = (ref[...].astype(F32) + theirs[drows(i), :].astype(F32)).astype(BF16)
            for k in (1, 2, 3, 0):
                go(grad_y, a, k)
        return f

    def fold_y(a, k):
        def f():
            grad_y(a, k).wait_recv()
            at_ = summed(a, zk[k] * 2 + y)
            total = at_[...].astype(F32) + from_y(a, k)[...].astype(F32)
            if k == 0:
                outs[a][...] = total
            else:
                at_[...] = total.astype(BF16)
                go(grad_z, a, k)
        return f

    def fold_z(a):
        def f():
            total = outs[a][...]
            for k in (1, 2, 3):
                grad_z(a, k).wait_recv()
                total = total + from_z(a, k)[...].astype(F32)
            outs[a][...] = total
        return f

    def settle():
        for b in range(6):
            owner, away, diag, near = ctx_send(b)

            @pl.when(c == owner)
            def _():
                away.wait_send()

            @pl.when(c != owner)
            def _():
                diag.wait_send()
                near.wait_send()
        grads = (out_send, core_grad, grad_y, grad_z)
        early = [s for s in sent if s[0] not in grads]
        late = [s for s in sent if s[0] in grads]
        for make, args in early:
            make(*args).wait_send()
        sent[:] = late

    def attention(prev, stage, mask):
        def p_copy(i):
            return pltpu.make_async_copy(stage.at[i % 2], p_hbm.at[i // heads, i % heads], psems.at[i % 2])

        pcopy = pltpu.make_async_copy(prev_hbm, prev, lsem.at[0])
        pcopy.start()
        seg8[...] = jnp.zeros_like(seg8)
        seg8[0:packs, :] = seg_ref[...].astype(F32)
        segt[...] = seg8[...].T
        run((pass_y, 0, 3), (line_out, 2), (pass_y, 0, 1))
        xoc().wait_recv()
        run((line_out, 5), (pass_y, 0, 2), (pass_x, 0), (out_y, 1))
        x1c().wait_recv()
        line_out(4)
        for j in range(4):
            yc(0, j).wait_recv()
        run((out_y, 3), (pass_w2, 1), (out_y, 5), (go, x2c, 0, 0))
        steps = {0: [(line_out, 1), (pass_w2, 3)], 3: [(pass_w2, 2)], 4: [(pass_wo, 2)], 6: [(pass_wo, 1)]}
        masks = head_masks((plen, heads * hw), heads, hw)
        pcopy.wait()
        n = packs * heads
        for p in range(packs):
            rr = pl.ds(p * plen, plen)
            tok = tok_ref[rr, :]
            q_ref[rr, :] = ((dot(tok, wa_ref[0]) + bias_ref[0:1, :]).astype(BF16) * scale).astype(BF16)
            k_ref[rr, :] = dot(tok, wa_ref[1]).astype(BF16)
            v_ref[rr, :] = (dot(tok, wa_ref[2]) + bias_ref[1:2, :]).astype(BF16)
            mask[...] = jnp.where(segt[:, p:p + 1] == seg8[p:p + 1, :], 0.0, -1e9)
            outs = []
            for h in range(heads):
                i = p * heads + h
                qm = jnp.where(masks[h], q_ref[rr, :], jnp.zeros((), BF16))
                s = dot_nt(qm, k_ref[rr, :]) + (prev[p, h].astype(F32) + mask[...])
                m = jnp.max(s, axis=-1, keepdims=True)
                e = jnp.exp(s - m)
                pr = e * (1.0 / jnp.sum(e, axis=-1, keepdims=True))
                if i >= 2:
                    p_copy(i - 2).wait()
                stage[i % 2] = pr
                p_copy(i).start()
                outs.append(dot(pr.astype(BF16), v_ref[rr, :]))
                run(*steps.get(i, ()))
            ctx_loc[rr, :] = pick_heads(masks, outs).astype(BF16)
            for b in (2 * p, 2 * p + 1):
                owner, away, diag, near = ctx_send(b)

                @pl.when(c == owner)
                def _():
                    away.start()
                    ctx4[t, pl.ds(b % 3 * blk, blk), :] = ctx_loc[pl.ds(b * blk, blk), :]

                @pl.when(c != owner)
                def _():
                    diag.start()
                    near.start()
        p_copy(n - 2).wait()
        p_copy(n - 1).wait()

    pl.run_scoped(attention, pltpu.VMEM(prev_hbm.shape, BF16), pltpu.VMEM((2, plen, plen), F32), pltpu.VMEM((plen, plen), F32))

    def feed_forward(og_ref, live_ref, xhat, rstd, hid, hidt, act, dg, acc, gft):
        ogc = pltpu.make_async_copy(og_hbm.at[pl.ds(pl.multiple_of(c * half, half), half), :], og_ref, lsem.at[1])
        ogc.start()
        nr = half // ROWS
        gain1, gain2, bo, shift1, b2, shift2 = (rp_ref[i:i + 1, :] for i in range(6))
        inv = 1.0 / width

        def blkr(r):
            return pl.ds(pl.multiple_of(r * ROWS, ROWS), ROWS)

        run((pass_y, 1, 1), (pass_wo, 3), (pass_x, 3), (pass_y, 1, 3), (line_out, 3), (pass_x, 1), (pass_x, 2),
            (core_w2, 0), (pass_y, 1, 2), (core_wo,), (pass_y, 3, 1))
        for b in range(6):
            pack = b // 2
            col = (segt[b % 2 * blk:(b % 2 + 1) * blk, pack:pack + 1] > 0.0).astype(F32)

            @pl.when(c == b // 3)
            def _():
                live_ref[pl.ds(b % 3 * blk, blk), :] = col
        oc(0).wait_recv()
        oc(1).wait_recv()
        for b in range(6):
            owner, away, diag, near = ctx_send(b)

            @pl.when(c == owner)
            def _():
                away.wait_recv()
                diag.wait_recv()
                near.wait_recv()
        att = dot_nt(ctx4[0], wo_ref[0])
        for s in range(1, 4):
            att = att + dot_nt(ctx4[s], wo_ref[s])
        acc[...] = att
        run((core_w1, 0), (pass_y, 3, 3))

        @pl.loop(0, nr)
        def _(r):
            rr = blkr(r)
            trow = pl.ds(pl.multiple_of(c * half + r * ROWS, ROWS), ROWS)
            r1 = (tok_ref[trow, :].astype(F32) + bo) + acc[rr, :]
            mean = jnp.sum(r1, axis=-1, keepdims=True) * inv
            cen = r1 - mean
            rs = lax.rsqrt(jnp.sum(cen * cen, axis=-1, keepdims=True) * inv + norm_eps)
            xh = cen * rs
            xhat[rr, :] = xh
            rstd[rr, :] = rs
            h = (xh * gain1 + shift1).astype(BF16)
            hid[rr, :] = h
            hidt[:, rr] = h.T

        run((pass_y, 3, 2), (core_w2, 1))
        for i in range(3):
            fc(i).wait_recv()
        cc(1, 0).wait_recv()
        cc(2, 0).wait_recv()

        def unit_ff(s, out, first):
            pre = dot(hid[...], w1[s]) + fb_ref[s]
            a, g = gelu_parts(pre)
            act[s] = a.astype(BF16)
            dg[s] = g.astype(BF16)
            low = dot_nt(act[s], w2[s])
            if first:
                out[...] = low
            else:
                out[...] += low

        unit_ff(x * 2, acc, True)
        core_w1(1)
        unit_ff(x * 2 + 1, acc, False)
        cc(1, 1).wait_recv()
        cc(2, 1).wait_recv()
        unit_ff((1 - x) * 2, gres1_ref, True)
        unit_ff((1 - x) * 2 + 1, gres1_ref, False)

        grow_ref[...] = jnp.zeros_like(grow_ref)
        ogc.wait()

        @pl.loop(0, nr)
        def _(r):
            rr = blkr(r)
            r2 = (xhat[rr, :] * gain1 + shift1) + ((acc[rr, :] + gres1_ref[rr, :]) + b2)
            mean = jnp.sum(r2, axis=-1, keepdims=True) * inv
            cen = r2 - mean
            rs = lax.rsqrt(jnp.sum(cen * cen, axis=-1, keepdims=True) * inv + norm_eps)
            xh = cen * rs
            live = live_ref[rr, :]
            out_ref[rr, :] = (live * (xh * gain2 + shift2)).astype(BF16)
            g = og_ref[rr, :].astype(F32) * live
            grow_ref[1:2, :] += jnp.sum(g * xh, axis=0, keepdims=True)
            grow_ref[5:6, :] += jnp.sum(g, axis=0, keepdims=True)
            dx = g * gain2
            m1 = jnp.sum(dx, axis=-1, keepdims=True) * inv
            m2 = jnp.sum(dx * xh, axis=-1, keepdims=True) * inv
            gr = rs * (dx - m1 - xh * m2)
            acc[rr, :] = gr
            low = gr.astype(BF16)
            hid[rr, :] = low
            gft[:, rr] = low.T
            grow_ref[4:5, :] += jnp.sum(low.astype(F32), axis=0, keepdims=True)

        out_local().start()
        go(out_send)

        def hidden_grad(s):
            dg[s] = (dot(hid[...], w2[s]) * dg[s].astype(F32)).astype(BF16)

        def grad_w1(i, s):
            gp = dg[s]
            gw1[i] = dot(hidt[...], gp).astype(BF16)
            gfb_ref[i] = jnp.sum(gp.astype(F32), axis=0, keepdims=True)

        def grad_w2(i, s):
            gw2[i] = dot(gft[...], act[s]).astype(BF16)

        st = x * 2 + 1 - c
        grad_w2(1, st)
        go(core_grad, 1)
        hidden_grad(st)
        grad_w1(1, st)
        go(core_grad, 0)
        grad_w2(0, t)
        hidden_grad(t)
        grad_w1(0, t)
        fold_core(1)()
        fold_core(0)()
        for dev in zp[1:]:
            pl.semaphore_signal(zfree, inc=1, device_id=dev, device_id_type=MESH)

        @pl.loop(0, 2)
        def _(i):
            hidden_grad((1 - x) * 2 + i)

        @pl.loop(0, 4)
        def _(s):
            acc[...] += dot_nt(dg[s], w1[s])

        settle()
        for dev in (sib, xn):
            pl.semaphore_signal(free, inc=1, device_id=dev, device_id_type=MESH)
        pl.semaphore_wait(zfree, 3)
        fold_y(1, 1)()

        @pl.loop(0, nr)
        def _(r):
            rr = blkr(r)
            xh = xhat[rr, :]
            g = acc[rr, :]
            grow_ref[0:1, :] += jnp.sum(g * xh, axis=0, keepdims=True)
            grow_ref[3:4, :] += jnp.sum(g, axis=0, keepdims=True)
            dx = g * gain1
            m1 = jnp.sum(dx, axis=-1, keepdims=True) * inv
            m2 = jnp.sum(dx * xh, axis=-1, keepdims=True) * inv
            gr = rstd[rr, :] * (dx - m1 - xh * m2)
            gres1_ref[rr, :] = gr
            low = gr.astype(BF16)
            og_ref[rr, :] = low
            gft[:, rr] = low.T
            grow_ref[2:3, :] += jnp.sum(low.astype(F32), axis=0, keepdims=True)

        fold_y(1, 2)()
        pl.semaphore_wait(free, 2)
        so_ = st
        gctx[...] = dot(og_ref[...], wo_ref[so_]).astype(BF16)
        go(core_grad, 3)
        ctx_loc[hrow, :] = dot(og_ref[...], wo_ref[t]).astype(BF16)
        gwo[1] = dot(gft[...], ctx4[so_]).astype(BF16)
        go(core_grad, 2)
        go(core_grad, 4)
        go(core_grad, 5)
        gwo[0] = dot(gft[...], ctx4[t]).astype(BF16)
        fold_y(1, 3)()

    ff = w1.shape[-1]
    V = pltpu.VMEM
    pl.run_scoped(
        feed_forward, V((half, width), BF16), V((half, 1), F32), V((half, width), F32), V((half, 1), F32),
        V((half, width), BF16), V((width, half), BF16), V((4, half, ff), BF16), V((4, half, ff), BF16),
        V((half, width), F32), V((width, half), BF16))
    def attention_back(pbuf, stage, tokt, gts, ga, gb, mine, ssend, cx, tg):
        def tc(i):
            return remote(ssend.at[i], w2.at[0, pl.ds(i * blk, blk), :], ts.at[i], tr.at[i], sib)

        def xc(i):
            return remote(cx.at[i], w2.at[1, pl.ds(i * blk, blk), :], xxs.at[i], xxr.at[i], xn)

        def trow(b):
            return pl.ds(b * blk, blk)

        def ucl(b):
            return pltpu.make_async_copy(tg.at[b % 3], tok_grad.at[trow(b), :], ul.at[b % 3])

        def ucr(b):
            return remote(tg.at[b % 3], tok_grad.at[trow(b), :], us.at[b % 3], ur.at[b % 3], sib)

        def part_ready(b, total):
            i = b % 3

            @pl.when(c == b // 3)
            def _():
                mine[i] = total

            @pl.when(c != b // 3)
            def _():
                ssend[i] = total.astype(BF16)
                tc(i).start()

        def part_chip(b):
            i = b % 3

            def f():
                @pl.when(c == b // 3)
                def _():
                    tc(i).wait_recv()
                    cx[i] = (mine[i] + w2[0, pl.ds(i * blk, blk), :].astype(F32)).astype(BF16)
                    xc(i).start()
            return f

        def part_done(b):
            i = b % 3

            def f():
                @pl.when(c == b // 3)
                def _():
                    xc(i).wait_recv()
                    tg[i] = gres1_ref[pl.ds(i * blk, blk), :] + (cx[i].astype(F32) + w2[1, pl.ds(i * blk, blk), :].astype(F32))
                    ucl(b).start()
                    ucr(b).start()
            return f

        cols = wa_ref.shape[-1]
        n = packs * heads
        masks = head_masks((plen, cols), heads, hw)
        steps = {0: [fold_core(2)], 1: [fold_y(1, 0)], 2: [fold_y(0, 1)], 3: [fold_y(0, 2), part_chip(0)], 4: [fold_y(0, 3), part_chip(1)],
                 5: [fold_y(0, 0)], 6: [fold_y(2, 1), part_chip(2), part_chip(3)], 7: [fold_y(2, 2), fold_y(2, 3)], 8: [fold_y(2, 0)]}

        def p_in(i):
            return pltpu.make_async_copy(p_hbm.at[i // heads, i % heads], pbuf.at[i % 3], insem.at[i % 3])

        def s_out(i):
            return pltpu.make_async_copy(stage.at[i % 2], sg_hbm.at[i // heads, i % heads], outsem.at[i % 2])

        p_in(0).start()
        p_in(1).start()
        for p in range(packs):
            tokt[:, p * plen:(p + 1) * plen] = tok_ref[pl.ds(p * plen, plen), :].T
        core_grad(3).wait_recv()
        for p in range(packs):
            rr = pl.ds(p * plen, plen)
            qt = q_ref[rr, :].T
            kt = k_ref[rr, :].T
            gct = ctx_loc[rr, :].T
            for h in range(heads):
                i = p * heads + h
                hh = slice(h * hw, (h + 1) * hw)
                p_in(i).wait()
                if i + 2 < n:
                    p_in(i + 2).start()
                gm = jnp.where(masks[h], ctx_loc[rr, :], jnp.zeros((), BF16))
                pf = pbuf[i % 3]
                dp = dot_nt(gm, v_ref[rr, :])
                rd = jnp.sum(pf * dp, axis=-1, keepdims=True)
                ds = (pf * (dp - rd)).astype(BF16)
                if i >= 2:
                    s_out(i - 2).wait()
                stage[i % 2] = ds
                s_out(i).start()
                gts[0, hh, :] = dot_nt(kt[hh, :], ds) * scale
                gts[1, hh, :] = dot(qt[hh, :], ds)
                gts[2, hh, :] = dot(gct[hh, :], pf.astype(BF16))
                for f in steps.get(i, ()):
                    f()
            total = None
            for j in range(3):
                gcol = gts[j].T.astype(BF16)
                xx = dot_nt(gcol, wa_ref[j])
                total = xx if total is None else total + xx
                yy = dot(tokt[:, p * plen:(p + 1) * plen], gcol)
                bb = jnp.sum(gcol.astype(F32), axis=0, keepdims=True)
                if p == 0:
                    ga[j] = yy
                    gb[j] = bb
                elif p < packs - 1:
                    ga[j] += yy
                    gb[j] += bb
                else:
                    ba[j] = (ga[j] + yy).astype(BF16)
                    gb[j] += bb
            part_ready(2 * p, total[:blk])
            part_ready(2 * p + 1, total[blk:])
        for k in (1, 2, 3, 0):
            go(grad_y, 3, k)
        for f in (part_chip(4), part_chip(5)):
            f()
        part_done(0)()
        part_done(1)()

        core_grad(4).wait_recv()
        core_grad(5).wait_recv()
        sm_send[0:8, :] = grow_ref[...] + rrow[...]
        sm_send[8:16, :] = jnp.zeros_like(sm_send[8:16, :])
        sm_send[8:9, :] = gfb_ref[0] + rfb[...]
        sm_send[9:10, 0:cols] = gb[0]
        sm_send[10:11, 0:cols] = gb[2]

        def mc(m):
            return remote(sm_send, sm_recv.at[d], ms.at[m - 1], mr.at[m - 1], dpp[m])

        for m in range(1, 8):
            go(mc, m)
        sm_recv[d] = sm_send[...]

        for f in (fold_y(3, 1), part_done(2), fold_y(3, 2), part_done(3), fold_z(0), fold_z(1), fold_z(2), fold_y(3, 3), fold_y(3, 0),
                  part_done(4), part_done(5)):
            f()
        for m in range(1, 8):
            mc(m).wait_recv()
        small = sm_recv[0]
        for i in range(1, 8):
            small = small + sm_recv[i]
        small_ref[...] = small

        def square(v):
            return jnp.sum(v * v, keepdims=True)

        sh = square(small[8:16, :]) * (1.0 / 8.0)
        sh = sh + (square(s1_ref[...]) + square(s2_ref[...]) + square(so_ref[...]))
        fold_z(3)()
        for j in range(3):
            sh = sh + square(sa_ref[j])
        sq[...] = jnp.broadcast_to(sh, sq.shape)

        def norm_core():
            return remote(sq, sqt, ns.at[15], nr_.at[15], sib)

        def norm_chip(i):
            return remote(sqd.at[16], sqd.at[d * 2 + x], ns.at[i - 1], nr_.at[i - 1], ((d + i // 2) % 8, (x + i % 2) % 2 * 2 + c))

        go(norm_core)
        norm_core().wait_recv()
        pair = sq[...] + sqt[...]
        sqd[16] = pair
        for i in range(1, 16):
            go(norm_chip, i)
        sqd[d * 2 + x] = pair
        for i in range(1, 16):
            norm_chip(i).wait_recv()
        tot = sqd[0]
        for i in range(1, 16):
            tot = tot + sqd[i]
        tot = tot[0:1, 0:1]
        norm_ref[...] = jnp.broadcast_to(jnp.sqrt(tot + square(small[0:8, :])), norm_ref.shape)

        for b in range(6):
            i = b % 3

            @pl.when(c == b // 3)
            def _():
                xc(i).wait_send()
                ucl(b).wait()
                ucr(b).wait_send()

            @pl.when(c != b // 3)
            def _():
                tc(i).wait_send()
                ucr(b).wait_recv()
        s_out(n - 2).wait()
        s_out(n - 1).wait()
        out_local().wait()
        out_send().wait_recv()
        for make, args in sent:
            make(*args).wait_send()


    cols = wa_ref.shape[-1]
    pl.run_scoped(
        attention_back, V((3, plen, plen), F32), V((2, plen, plen), BF16), V((width, rows), BF16), V((3, cols, plen), F32),
        V((3, width, cols), F32), V((3, 1, cols), F32), V((3, blk, width), F32), V((3, blk, width), BF16), V((3, blk, width), BF16),
        V((3, blk, width), F32))


def layer(tok, seg, prev, og, rp, bias, fbo, wam, w1m, w2m, wom):
    packs, heads, plen, _ = prev.shape
    rows, width = tok.shape
    _, part, cols = wam.shape
    ff = w1m.shape[-1]
    v = pl.BlockSpec(memory_space=pltpu.VMEM)
    h = pl.BlockSpec(memory_space=pl.ANY)
    sds = jax.ShapeDtypeStruct
    V = pltpu.VMEM
    dma = pltpu.SemaphoreType.DMA
    half = rows // 2
    return pl.pallas_call(
        layer_kernel,
        out_shape=(sds((part, ff), F32), sds((part, ff), F32), sds((part, cols), F32), sds((3, part, cols), F32),
                   sds((16, width), F32), sds((8, 128), F32), sds((rows, width), F32), sds((rows, width), BF16),
                   sds(prev.shape, BF16), sds(prev.shape, F32)),
        in_specs=[v] * 9 + [h] * 2, out_specs=(v,) * 6 + (h,) * 4,
        scratch_shapes=[
            V((width, ff), BF16), V((width, ff), BF16), V((4, part, ff), BF16), V((4, part, ff), BF16),
            V((rows, cols), BF16), V((rows, cols), BF16), V((rows, cols), BF16), V((3, width, cols), BF16),
            V((4, 1, ff), F32), V((4, width, cols), BF16), V((4, width, ff), BF16), V((4, width, ff), BF16),
            V((4, half, cols), BF16), V((rows, cols), BF16), V((8, plen), F32), V((plen, 8), F32),
            V((half, width), BF16), V((half, width), F32), V((half, cols), BF16), V((2, width, ff), BF16), V((2, width, ff), BF16),
            V((2, width, cols), BF16), V((8, width), F32), V((2, 1, ff), F32),
            V((width, cols), BF16), V((8, width), F32), V((1, ff), F32), V((3, width, cols), BF16),
            V((4, part, cols), BF16), V((4, 3, part, cols), BF16), V((3, part, cols), BF16), V((3, 3, part, cols), BF16),
            V((16, width), F32), V((8, 16, width), F32), V((8, 128), F32), V((8, 128), F32), V((17, 8, 128), F32), dma((3,)), dma((2,)),
            dma((6, 3)), dma((6, 3)), dma((6, 4)), dma((6, 4)), dma((2,)), dma((2,)),
            dma((4, 2)), dma((4, 2)), dma((2, 2)), dma((2, 2)), dma((3,)), dma((3,)), dma((3,)), dma((3,)),
            dma((6,)), dma((6,)), dma((3,)), dma((3,)),
            pltpu.SemaphoreType.REGULAR, pltpu.SemaphoreType.REGULAR, dma((4, 4)), dma((4, 4)), dma((4, 3)), dma((4, 3)), dma((7,)), dma((7,)),
            dma((3,)), dma((3,)), dma((3,)), dma((3,)), dma((3,)), dma((3,)), dma((3,)), dma((7,)), dma((7,)), dma((16,)), dma((16,)),
            dma((3,)), dma((2,))],
        compiler_params=pltpu.CompilerParams(vmem_limit_bytes=63 << 20, collective_id=1, has_side_effects=True),
        name="layer",
    )(tok, seg, bias, fbo, rp, wam, w1m, w2m, wom, prev, og)


def final_kernel(norm_ref, sa, s1, s2, so, small, wa, wo, w1, w2, wq, wf, wr, ma, mo, m1, m2, mq, mf, mr, va, vo, v1, v2, vq, vf, vr,
                 sg_hbm, tg_hbm, ot_hbm, *rest):
    outs, (sgo_hbm, tgo_hbm, oto_hbm, norm_out), (inb, outb, tbuf, obuf, insem, outsem, tis, tos, ois, oos) = rest[:25], rest[25:29], rest[29:]
    packs, heads = sg_hbm.shape[:2]
    n = packs * heads

    def s_in(i):
        return pltpu.make_async_copy(sg_hbm.at[i // heads, i % heads], inb.at[i % 3], insem.at[i % 3])

    def s_out(i):
        return pltpu.make_async_copy(outb.at[i % 3], sgo_hbm.at[i // heads, i % heads], outsem.at[i % 3])

    for i in range(3):
        s_in(i).start()
    half = ot_hbm.shape[0] // 2
    nt, trows = tis.shape[0], tbuf.shape[0] // tis.shape[0]
    tin = [pltpu.make_async_copy(tg_hbm.at[pl.ds(i * trows, trows), :], tbuf.at[pl.ds(i * trows, trows), :], tis.at[i]) for i in range(nt)]
    tout = [pltpu.make_async_copy(tbuf.at[pl.ds(i * trows, trows), :], tgo_hbm.at[pl.ds(i * trows, trows), :], tos.at[i]) for i in range(nt)]
    oin = [pltpu.make_async_copy(ot_hbm.at[pl.ds(i * half, half), :], obuf.at[i], ois.at[i]) for i in range(2)]
    oout = [pltpu.make_async_copy(obuf.at[i], oto_hbm.at[pl.ds(i * half, half), :], oos.at[i]) for i in range(2)]
    moves = list(zip(oin + tin, oout + tout))
    for first, _ in moves:
        first.start()
    norm = norm_ref[0:1, 0:1]
    norm_out[...] = norm
    factor = 1.0 / jnp.maximum(norm, 1.0)
    big_rate = wr.shape[-1] ** -0.5
    cols = wq.shape[-1]

    def update(g, w, m, v, rate, decay, o):
        g = g * factor
        mn = beta_one * m + (1.0 - beta_one) * g
        vn = beta_two * v + (1.0 - beta_two) * g * g
        corr = mn / (1.0 - beta_one ** STEP) / (jnp.sqrt(vn / (1.0 - beta_two ** STEP)) + adam_eps)
        new = w - rate * (corr + decay * w)
        o[0][...], o[1][...], o[2][...] = new, mn, vn
        if len(o) > 3:
            o[3][...] = new.astype(BF16)

    oa, oo, o1, o2 = (outs[i:i + 4] for i in range(0, 16, 4))
    oq, of, orr = (outs[i:i + 3] for i in (16, 19, 22))

    def attn_in(j):
        return lambda: update(sa[j], wa[j], ma[j], va[j], big_rate, weight_decay, [o.at[j] for o in oa])

    def smalls():
        update(small[9:11, 0:cols], wq[...], mq[...], vq[...], small_rate, 0.0, oq)
        row = small[8:9, :] * factor
        mn = beta_one * mf[...].reshape(row.shape) + (1.0 - beta_one) * row
        vn = beta_two * vf[...].reshape(row.shape) + (1.0 - beta_two) * row * row
        corr = mn / (1.0 - beta_one ** STEP) / (jnp.sqrt(vn / (1.0 - beta_two ** STEP)) + adam_eps)
        new = wf[...].reshape(row.shape) - small_rate * corr
        for o, val in zip(of, (new, mn, vn)):
            o[...] = val.reshape(o.shape)
        update(small[0:6, :], wr[...], mr[...], vr[...], small_rate, 0.0, orr)

    work = [
        lambda: update(s1[...], w1[...], m1[...], v1[...], big_rate, weight_decay, o1),
        lambda: update(s2[...], w2[...], m2[...], v2[...], big_rate, weight_decay, o2),
        attn_in(0), attn_in(1), attn_in(2),
        lambda: update(so[...].T, wo[...], mo[...], vo[...], big_rate, weight_decay, oo),
        smalls]
    for i in range(n):
        s_in(i).wait()
        if i >= 3:
            s_out(i - 3).wait()
        outb[i % 3] = inb[i % 3].astype(F32)
        s_out(i).start()
        if i + 3 < n:
            s_in(i + 3).start()
        if i < len(work):
            work[i]()
        if i < len(moves):
            moves[i][0].wait()
            moves[i][1].start()
    for i in range(n - 3, n):
        s_out(i).wait()
    for _, last in moves:
        last.wait()


def finish(norm, sa, s1, s2, so, small, ws, ms, vs, sg, tg, ot):
    vm = pl.BlockSpec(memory_space=pltpu.VMEM)
    h = pl.BlockSpec(memory_space=pl.ANY)
    sds = jax.ShapeDtypeStruct
    shapes = []
    for i, w in enumerate(ws):
        shapes += [sds(w.shape, F32)] * 3 + ([sds(w.shape, BF16)] if i < 4 else [])
    shapes += [sds(sg.shape, F32), sds(tg.shape, F32), sds(tg.shape, BF16), sds((1, 1), F32)]
    plen = sg.shape[-1]
    dma = pltpu.SemaphoreType.DMA
    return pl.pallas_call(
        final_kernel, out_shape=tuple(shapes), in_specs=[vm] * 27 + [h] * 3, out_specs=(vm,) * 25 + (h,) * 3 + (vm,),
        scratch_shapes=[pltpu.VMEM((3, plen, plen), BF16), pltpu.VMEM((3, plen, plen), F32),
                        pltpu.VMEM(tg.shape, F32), pltpu.VMEM((2, ot.shape[0] // 2, ot.shape[1]), BF16),
                        dma((3,)), dma((3,)), dma((6,)), dma((6,)), dma((2,)), dma((2,))],
        compiler_params=pltpu.CompilerParams(vmem_limit_bytes=60 << 20), name="optimizer",
    )(norm, sa, s1, s2, so, small, *ws, *ms, *vs, sg, tg, ot)


def fast_layer(
    tokens, segment_ids, prev_scores, out_grad,
    attn_in_master, attn_out_master, ffn_in_master, ffn_out_master,
    attn_in_first, attn_out_first, ffn_in_first, ffn_out_first,
    attn_in_second, attn_out_second, ffn_in_second, ffn_out_second,
    qv_bias, ffn_bias, row_params,
    qv_bias_first, ffn_bias_first, row_params_first,
    qv_bias_second, ffn_bias_second, row_params_second,
):
    s1, s2, so, sa, small, norm, tokens_grad, out_tokens, scores_grad, _ = layer(
        tokens, segment_ids, prev_scores, out_grad, row_params, qv_bias, ffn_bias,
        attn_in_master, ffn_in_master, ffn_out_master.T, attn_out_master)
    new = finish(
        norm, sa, s1, s2, so, small,
        (attn_in_master, attn_out_master, ffn_in_master, ffn_out_master.T, qv_bias, ffn_bias, row_params),
        (attn_in_first, attn_out_first, ffn_in_first, ffn_out_first.T, qv_bias_first, ffn_bias_first, row_params_first),
        (attn_in_second, attn_out_second, ffn_in_second, ffn_out_second.T, qv_bias_second, ffn_bias_second, row_params_second),
        scores_grad, tokens_grad, out_tokens)
    big = [list(new[i:i + 4]) for i in range(0, 16, 4)]
    big[3] = [a.T for a in big[3]]
    small_new = [new[i:i + 3] for i in range(16, 25, 3)]
    return (
        new[27], new[26], new[25], new[28].reshape(()),
        *[b[0] for b in big], *[b[1] for b in big], *[b[2] for b in big], *[b[3] for b in big],
        *[s[0] for s in small_new], *[s[1] for s in small_new], *[s[2] for s in small_new],
    )


def solution(mesh):
    in_specs = (
        P("dp", None),
        P("dp", None),
        P("dp", "tensor", None, None),
        P("dp", None),
        P(None, "dp", "tensor"),
        P("tensor", "dp"),
        P("dp", "tensor"),
        P("tensor", "dp"),
        P(None, "dp", "tensor"),
        P("tensor", "dp"),
        P("dp", "tensor"),
        P("tensor", "dp"),
        P(None, "dp", "tensor"),
        P("tensor", "dp"),
        P("dp", "tensor"),
        P("tensor", "dp"),
        P(None, "tensor"),
        P("tensor"),
        P(),
        P(None, "tensor"),
        P("tensor"),
        P(),
        P(None, "tensor"),
        P("tensor"),
        P(),
    )
    out_specs = (
        P("dp", None),
        P("dp", None),
        P("dp", "tensor", None, None),
        P(),
        P(None, "dp", "tensor"),
        P("tensor", "dp"),
        P("dp", "tensor"),
        P("tensor", "dp"),
        P(None, "dp", "tensor"),
        P("tensor", "dp"),
        P("dp", "tensor"),
        P("tensor", "dp"),
        P(None, "dp", "tensor"),
        P("tensor", "dp"),
        P("dp", "tensor"),
        P("tensor", "dp"),
        P(None, "dp", "tensor"),
        P("tensor", "dp"),
        P("dp", "tensor"),
        P("tensor", "dp"),
        P(None, "tensor"),
        P("tensor"),
        P(),
        P(None, "tensor"),
        P("tensor"),
        P(),
        P(None, "tensor"),
        P("tensor"),
        P(),
    )
    layer = fast_layer if dict(mesh.shape) == {"dp": 8, "tensor": 4} else plain_layer
    return jax.shard_map(
        layer, mesh=mesh, in_specs=in_specs, out_specs=out_specs, check_vma=False
    )
```
